128 devices in a mesh: gx: 8 (over x_hi, z), gy: 16 (over y, x_lo, core).
Axes of the slice: x: 4 (x_hi: 2, x_lo: 2; x = x_hi * 2 + x_lo), y: 4, z: 4, core: 2. Of those that a mesh axis runs over, the one named last changes fastest.
Arguments:
- neutral_wind: float32 [2, 128, 512, 128], P(None, 'gx', 'gy'), may hold values from -6 to 6
- forcing: float32 [2, 128, 512, 128], P(None, 'gx', 'gy'), may hold values from -3 to 3
- ion_density: float32 [2, 16384, 512], P(None, ('gx', 'gy')), may hold values from 0.5 to 2
- inverse: bfloat16 [8, 2, 512, 512], P('gx'), may hold values from -0.25 to 0.25
- drift_fraction: float32 [16384], P(('gx', 'gy')), may hold values from 0.1 to 0.4
- viscosity: float32 [128], replicated, may hold values from 0.02 to 0.15
- coupling: float32 [2, 2], replicated, may hold values from 0.2 to 0.8
- drag_rate: float32 [2], replicated, may hold values from 0.5 to 1.5
- outgoing_column: int32 [128, 128, 256], P(('gx', 'gy')), may hold values from 0 to 511
- send_level: int32 [128, 128, 256], P(('gx', 'gy')), may hold values from 0 to 127
- recv_tube: int32 [128, 128, 256], P(('gx', 'gy')), may hold values from 0 to 127
- recv_point: int32 [128, 128, 256], P(('gx', 'gy')), may hold values from 0 to 511
- recv_weight: float32 [128, 128, 256], P(('gx', 'gy')), may hold values from 0.2 to 1
- pair_count: int32 [128, 128], replicated, may hold values from 64 to 256, as said below
Outputs:
- wind_out: float32 [2, 128, 512, 128], P(None, 'gx', 'gy')
- ion_out: float32 [2, 16384, 512], P(None, ('gx', 'gy'))
The draws below stay inside these ranges and needn't reach their ends.
Inputs may be any that keep to these rules, and one draw needn't show every extreme that they name: `pair_count`: every entry is at most 256; in every draw some destination device receives exactly 256 live crossings from every source device, and a few destinations receive far more than the mean.
All inputs are finite; a program needn't handle non-finite values.
Results may differ from the reference program's by a relative error of at most 0.0003.
The reference program's roundings to bfloat16 on the way count: a program that leaves them out, or rounds other values in their place, can miss the bound.
Values sent between devices are 32-bit elements; how exact they have to be, the bound alone decides.
No kernel may reach another device: no remote copies, remote signals or barrier semaphores. Data moves between devices by JAX's collectives and lax.ppermute only.
A program may use at most 128 MiB of HBM per device.

```python
import math
import jax
import jax.numpy as jnp
from jax import lax

CX = 16
CY = 32
LEV = 128
TUB_DEV = 128
CAP = 256
TP = 512
RANKS = 128
BUNDLES = 8
NX = 128
NY = 512
TUBES = 16384
N_GX = 8
N_GY = 16


def draw_pair_count(key, part):
    key_base = jax.random.fold_in(key, 11)
    key_busy = jax.random.fold_in(key, 12)
    key_order = jax.random.fold_in(key, 13)
    base = jax.random.randint(key_base, (RANKS, RANKS), CAP // 4, 5 * CAP // 8 + 1)
    busy = jax.random.randint(key_busy, (RANKS, RANKS), CAP // 2, CAP + 1)
    order = jax.random.permutation(key_order, RANKS)
    hot_column = order < max(RANKS // 8, 1)
    counts = jnp.where(hot_column[None, :], busy, base)
    counts = jnp.where((order == 0)[None, :], CAP, counts)
    return counts.astype(jnp.int32)


def touch_ends(values, stream_key, smallest, largest):
    dims = values.shape
    spot = [jax.random.randint(jax.random.fold_in(stream_key, axis), (), 0, dims[axis]) for axis in range(len(dims))]
    values = values.at[tuple(spot)].set(smallest)
    longest = dims.index(max(dims))
    spot[longest] = (spot[longest] + 1) % dims[longest]
    return values.at[tuple(spot)].set(largest)


def level_of(rng, shape, cuts, least, largest):
    def one(dim, blocks):
        steps = jax.random.uniform(jax.random.fold_in(jax.random.fold_in(rng, 6), dim), (blocks,), jnp.float32, least / len(cuts), largest / len(cuts))
        return jnp.repeat(jnp.exp(steps), shape[dim] // blocks).reshape((-1,) + (1,) * (len(shape) - dim - 1))

    level = one(*cuts[0])
    for cut in cuts[1:]:
        level = level * one(*cut)
    return level


def centred(own_key, dims, width, limit, pieces=(), held_as=jnp.bfloat16):
    entries = jax.random.normal(own_key, dims, jnp.float32) * width
    if len(pieces) > 0:
        entries = level_of(own_key, dims, pieces, -0.22, 0.18) * entries
    return jnp.clip(entries, min=-limit, max=limit).astype(held_as)


def setup_inputs(seed: int = 0) -> dict:
    key_list = jax.random.split(jax.random.key(seed), 15)
    return {
        "neutral_wind": centred(key_list[0], (2, NX, NY, LEV), 1.0, 6.0, ((1, 8), (2, 16)), jnp.float32),
        "forcing": centred(key_list[1], (2, NX, NY, LEV), 0.5, 3.0, ((1, 8), (2, 16)), jnp.float32),
        "ion_density": jnp.clip(jnp.exp(math.log(2.0) - 1.3862944 * jax.random.uniform(key_list[2], (2, TUBES, TP), jnp.float32) ** level_of(key_list[2], (2, TUBES, TP), ((1, 128),), -0.2, 0.2)), 0.5, 2.0),
        "inverse": centred(key_list[3], (BUNDLES, 2, TP, TP), TP ** -0.5, 0.25, ((0, 8),)),
        "drift_fraction": jnp.clip(0.1 + 0.3 * jax.random.uniform(key_list[4], (TUBES,), jnp.float32) ** level_of(key_list[4], (TUBES,), ((0, 128),), -0.2, 0.2), 0.1, 0.4),
        "viscosity": jnp.clip(jnp.exp(jax.random.uniform(key_list[5], (LEV,), jnp.float32, math.log(0.02), math.log(0.15))), 0.02, 0.15),
        "coupling": jnp.clip(jax.random.uniform(key_list[6], (2, 2), jnp.float32, 0.2, 0.8), 0.2, 0.8),
        "drag_rate": jnp.clip(jax.random.uniform(key_list[7], (2,), jnp.float32, 0.5, 1.5), 0.5, 1.5),
        "outgoing_column": touch_ends(jax.random.randint(key_list[8], (RANKS, RANKS, CAP), 0, CX * CY), jax.random.fold_in(key_list[8], 1), 0, (CX * CY) - 1).astype(jnp.int32),
        "send_level": touch_ends(jax.random.randint(key_list[9], (RANKS, RANKS, CAP), 0, LEV), jax.random.fold_in(key_list[9], 1), 0, LEV - 1).astype(jnp.int32),
        "recv_tube": touch_ends(jax.random.randint(key_list[10], (RANKS, RANKS, CAP), 0, TUB_DEV), jax.random.fold_in(key_list[10], 1), 0, TUB_DEV - 1).astype(jnp.int32),
        "recv_point": touch_ends(jax.random.randint(key_list[11], (RANKS, RANKS, CAP), 0, TP), jax.random.fold_in(key_list[11], 1), 0, TP - 1).astype(jnp.int32),
        "recv_weight": jnp.clip(0.2 + 0.8 * jax.random.uniform(key_list[12], (RANKS, RANKS, CAP), jnp.float32) ** level_of(key_list[12], (RANKS, RANKS, CAP), ((0, 128),), -0.2, 0.2), 0.2, 1.0),
        "pair_count": draw_pair_count(jax.random.fold_in(key_list[14], 71), 0),
    }


neutral_step = 0.4
ion_factor = 0.5


def to_tiles(neutral):
    return neutral.reshape(2, N_GX, CX, N_GY, CY, LEV).transpose(1, 3, 0, 2, 4, 5).reshape(RANKS, 2, CX * CY * LEV)


def from_tiles(tiles):
    return tiles.reshape(N_GX, N_GY, 2, CX, CY, LEV).transpose(2, 0, 3, 1, 4, 5).reshape(2, N_GX * CX, N_GY * CY, LEV)


def interp(neutral, send_cell, recv_slot, pair_gain):
    tiles = to_tiles(neutral)
    selected_entries = jax.vmap(lambda tile, index: tile[:, index])(tiles, send_cell)
    arriving = selected_entries.transpose(2, 1, 0, 3) * pair_gain[:, None]

    def place(values, index):
        return jnp.zeros((2, TUB_DEV * TP), jnp.float32).at[:, index.reshape(-1)].add(values.reshape(2, -1))

    placed = jax.vmap(place)(arriving, recv_slot)
    return placed.reshape(RANKS, 2, TUB_DEV, TP).transpose(1, 0, 2, 3).reshape(2, RANKS * TUB_DEV, TP)


def give_back(drag_points, send_cell, recv_slot, pair_gain):
    per_device = drag_points.reshape(2, RANKS, TUB_DEV * TP).transpose(1, 0, 2)
    taken = jax.vmap(lambda points, index: points[:, index])(per_device, recv_slot) * pair_gain[:, None]
    leaving = taken.transpose(2, 1, 0, 3)

    def place(values, index):
        return jnp.zeros((2, CX * CY * LEV), jnp.float32).at[:, index.reshape(-1)].add(values.reshape(2, -1))

    return from_tiles(jax.vmap(place)(leaving, send_cell))


def ion_step(ion_state, tube_winds, inverse, coupling, drift_fraction):
    growth = coupling[:, 0, None, None] * tube_winds[0] + coupling[:, 1, None, None] * tube_winds[1]
    right_side = ion_state + ion_factor * ion_state * growth
    half_step_forcing = right_side.astype(jnp.bfloat16)
    grouped_by_bundle = half_step_forcing.astype(jnp.float32).reshape(2, BUNDLES, N_GY * TUB_DEV, TP)
    mixing = jnp.einsum("kbtp,bkpq->kbtq", grouped_by_bundle, inverse.astype(jnp.float32), precision=lax.Precision.HIGHEST)
    smoothed_field = right_side + mixing.reshape(2, -1, TP)
    outflow = drift_fraction[None, :, None] * smoothed_field
    bundled = outflow.reshape(2, BUNDLES, N_GY * TUB_DEV, TP)
    inflow = jnp.pad(bundled, ((0, 0), (0, 0), (1, 0), (0, 0)))[:, :, :-1].reshape(2, -1, TP)
    return smoothed_field - outflow + inflow


def tendency(wind_field, viscosity, drag_cells, forcing):
    padded = jnp.pad(wind_field, ((0, 0), (1, 1), (1, 1), (1, 1)))
    beside = padded[:, 2:, 1:-1, 1:-1] + padded[:, :-2, 1:-1, 1:-1]
    beside = beside + padded[:, 1:-1, 2:, 1:-1] + padded[:, 1:-1, :-2, 1:-1]
    beside = beside + padded[:, 1:-1, 1:-1, 2:] + padded[:, 1:-1, 1:-1, :-2]
    return viscosity * (beside - 6.0 * wind_field) + drag_cells + forcing


def reference(neutral_wind, forcing, ion_density, inverse, drift_fraction, viscosity, coupling, drag_rate, outgoing_column, send_level, recv_tube, recv_point, recv_weight, pair_count):
    send_cell = (outgoing_column * LEV + send_level).astype(jnp.int32)
    recv_slot = (recv_tube * TP + recv_point).astype(jnp.int32)
    position = lax.broadcasted_iota(jnp.int32, (RANKS, RANKS, CAP), 2)
    pair_gain = recv_weight * (position < pair_count.T[:, :, None]).astype(jnp.float32)

    def section(wind_field, ion_state):
        tube_winds = interp(wind_field, send_cell, recv_slot, pair_gain)
        updated = ion_step(ion_state, tube_winds, inverse, coupling, drift_fraction)
        drag_points = -(drag_rate[0] * updated[0] + drag_rate[1] * updated[1])[None] * tube_winds
        drag_cells = give_back(drag_points, send_cell, recv_slot, pair_gain)
        return updated, tendency(wind_field, viscosity, drag_cells, forcing)

    first_ions, first_tend = section(neutral_wind, ion_density)
    midpoint = neutral_wind + neutral_step * first_tend
    second_ions, second_tend = section(midpoint, first_ions)
    wind_out = neutral_wind + 0.5 * neutral_step * (first_tend + second_tend)
    ion_out = 0.5 * (ion_density + second_ions)
    return wind_out, ion_out
```

```python
import jax
import jax.numpy as jnp
from jax import lax
from jax.experimental import pallas as pl
from jax.experimental.pallas import tpu as pltpu
from jax.sharding import PartitionSpec as P

i32, f32, bf16 = jnp.int32, jnp.float32, jnp.bfloat16
VM = pl.BlockSpec(memory_space=pltpu.VMEM)
SM = pl.BlockSpec(memory_space=pltpu.SMEM)
W = 128
neutral_step = 0.4
ion_factor = 0.5


def bitonic(x):
    n, L = x.shape
    x = x.reshape(n//8, 8, L)
    sub = lax.broadcasted_iota(i32, (1, 8, L), 1)
    k = 2
    while k <= n:
        d = k//2
        while d >= 1:
            if d >= 8:
                dv = d//8
                y = x.reshape(n//(16*dv), 2, dv, 8, L)
                a, b = y[:, 0], y[:, 1]
                lo, hi = jnp.minimum(a, b), jnp.maximum(a, b)
                parts = []
                for g in range(n//(16*dv)):
                    up = ((g*2*d) & k) == 0
                    parts += [lo[g], hi[g]] if up else [hi[g], lo[g]]
                x = jnp.concatenate(parts, axis=0)
            else:
                up_r = pltpu.roll(x, 8-d, 1)
                dn_r = pltpu.roll(x, d, 1)
                first = (sub & d) == 0
                p = jnp.where(first, up_r, dn_r)
                mn, mx = jnp.minimum(x, p), jnp.maximum(x, p)
                if k >= 8:
                    if k == 8:
                        vi = lax.broadcasted_iota(i32, (n//8, 1, 1), 0)
                    parts = []
                    xs = []
                    take_min_up = first
                    kv = k//8
                    for g in range(0, n//8, kv):
                        up = (g*8 & k) == 0
                        sel = first if up else jnp.logical_not(first)
                        xs.append(jnp.where(sel, mn[g:g+kv], mx[g:g+kv]))
                    x = jnp.concatenate(xs, axis=0) if len(xs) > 1 else xs[0]
                else:
                    up = (sub & k) == 0
                    sel = first == up
                    x = jnp.where(sel, mn, mx)
            d //= 2
        k *= 2
    return x.reshape(n, L)

def sort_side(key16, cell_ref, pos_ref, inv_ref, bnd_ref):
    P, C = key16.shape
    c = lax.broadcasted_iota(i32, (P, C), 1)
    k = (key16 * 256 + c).T
    s = bitonic(k)
    cell = s >> 8
    pos = s & 255
    cell_ref[...] = cell
    pos_ref[...] = pos.T
    r = lax.broadcasted_iota(i32, (C, P), 0)
    inv = bitonic(pos*256 + r) & 255
    inv_ref[...] = inv.T
    row = (cell >> 7).reshape(C//8, 8, P)
    lo = jnp.min(jnp.min(row, axis=1), axis=1, keepdims=True)
    hi = jnp.max(jnp.max(row, axis=1), axis=1, keepdims=True)
    lane = lax.broadcasted_iota(i32, (C//8, 128), 1)
    bnd_ref[...] = jnp.where(lane == 0, lo, hi)

def sort_kernel(col, lev, tub, pnt, cellA, posA, invA, bndA, cellB, posB, invB, bndB):
    sort_side(col[0]*128 + lev[0], cellA, posA, invA, bndA)
    p = pnt[0]
    sort_side(((p >> 7) << 14) + (tub[0] << 7) + (p & 127), cellB, posB, invB, bndB)

def sort_call(col, lev, tub, pnt):
    P, C = col.shape[1:]
    side = [jax.ShapeDtypeStruct((C, P), i32), jax.ShapeDtypeStruct((P, C), i32), jax.ShapeDtypeStruct((P, C), i32), jax.ShapeDtypeStruct((C//8, 128), i32)]
    return pl.pallas_call(sort_kernel, out_shape=side*2, in_specs=[VM]*4, out_specs=[VM]*8, name="sort")(col, lev, tub, pnt)

def permute_lanes(x, idx):
    outs = []
    for h in range(2):
        ix = idx[:, h*128:(h+1)*128]
        low = ix & 127
        a = jnp.take_along_axis(x[:, :128], low, axis=1)
        b = jnp.take_along_axis(x[:, 128:], low, axis=1)
        outs.append(jnp.where(ix < 128, a, b))
    return outs

def lookup(bnd, cell_ref, t_ref, s_ref):
    def block(v, _):
        cell = cell_ref[pl.ds(pl.multiple_of(v*8, 8), 8), :]
        row, lev = cell >> 7, cell & 127
        lo, hi = bnd[v, 0], bnd[v, 1]
        g0 = lo // 8
        def rows(g, acc):
            a0, a1 = acc
            base = pl.multiple_of(g*8, 8)
            rel = row - base
            b0 = t_ref[0, pl.ds(base, 8), :]
            b1 = t_ref[1, pl.ds(base, 8), :]
            for j in range(8):
                m = rel == j
                x0 = jnp.take_along_axis(jnp.broadcast_to(b0[j:j+1], (8, 128)), lev, axis=1)
                x1 = jnp.take_along_axis(jnp.broadcast_to(b1[j:j+1], (8, 128)), lev, axis=1)
                a0 = jnp.where(m, x0, a0)
                a1 = jnp.where(m, x1, a1)
            return a0, a1
        z = jnp.zeros((8, 128), f32)
        a0, a1 = lax.fori_loop(g0, hi//8 + 1, rows, (z, z))
        s_ref[0, pl.ds(pl.multiple_of(v*8, 8), 8), :] = a0
        s_ref[1, pl.ds(pl.multiple_of(v*8, 8), 8), :] = a1
        return 0
    lax.fori_loop(0, 32, block, 0)

def scatter_add(bnd, cell_ref, val_ref, acc_ref):
    acc_ref[...] = jnp.zeros_like(acc_ref)
    iota = lax.broadcasted_iota(i32, (128, 128), 0).astype(f32).astype(bf16)
    one = jnp.ones((128, 128), bf16); zero = jnp.zeros((128, 128), bf16)
    def block(v, _):
        sl = pl.ds(pl.multiple_of(v*8, 8), 8)
        cell = cell_ref[sl, :]
        row, lev = cell >> 7, (cell & 127).astype(f32)
        lo, hi = bnd[v, 0], bnd[v, 1]
        base = (lo // 8) * 8
        vals = []
        for k in range(2):
            x = val_ref[k, sl, :]
            h = x.astype(bf16).astype(f32)
            vals.append((h, x - h))
        def spread(x):
            return jnp.broadcast_to(x, (128, 128)).astype(bf16)
        V = [[], []]
        for r in range(8):
            m = iota == spread(lev[r:r+1])
            for p in range(2):
                V[p].append(jnp.concatenate([jnp.where(m, spread(vals[k][p][r:r+1]), zero) for k in range(2)], axis=0))
        V = [jnp.concatenate(v_, axis=1) for v_ in V]
        def win(it, _):
            rb = pl.multiple_of(base + it*W, 8)
            rel = (row - rb).astype(f32)
            oh = jnp.concatenate([jnp.where(iota == spread(rel[r:r+1]), one, zero) for r in range(8)], axis=1)
            dn = (((1,), (1,)), ((), ()))
            o = lax.dot_general(oh, V[0], dn, preferred_element_type=f32) + lax.dot_general(oh, V[1], dn, preferred_element_type=f32)
            acc_ref[pl.ds(rb, W), :] += o
            return 0
        lax.fori_loop(0, (hi - base)//W + 1, win, 0)
        return 0
    lax.fori_loop(0, 32, block, 0)


def to_wire(inv, s, out, gain=None):
    for k in range(2):
        o = permute_lanes(s[k].T, inv[...])
        for h in range(2):
            x = o[h]
            if gain is not None:
                x = x * gain[:, h*128:(h+1)*128]
            out[:, 2*k+h, :] = x


def from_wire(pos, wire, val, gain=None):
    for k in range(2):
        x = [wire[:, 2*k+h, :] for h in range(2)]
        if gain is not None:
            x = [x[h] * gain[:, h*128:(h+1)*128] for h in range(2)]
        o = permute_lanes(jnp.concatenate(x, axis=1), pos[...])
        val[k, :128, :] = o[0].T
        val[k, 128:, :] = o[1].T


def gather_kernel(bnd, cell, inv, t, out, s):
    lookup(bnd, cell, t, s)
    to_wire(inv, s, out)


def tube_kernel(bnd, coupling, cell, pos, gain, drift, wire, ions, inverse, w_out, smooth_out, last_out, val, acc):
    from_wire(pos, wire, val, gain)
    scatter_add(bnd, cell, val, acc)
    w = []
    for k in range(2):
        for j in range(4):
            w_out[k, :, j*128:(j+1)*128] = acc[j*128:(j+1)*128, k*128:(k+1)*128]
    for k in range(2):
        n = ions[k]
        growth = coupling[k, 0] * w_out[0] + coupling[k, 1] * w_out[1]
        rhs = n + ion_factor * n * growth
        mix = lax.dot_general(rhs.astype(bf16), inverse[0, k], (((1,), (0,)), ((), ())), preferred_element_type=f32)
        sm = rhs + mix
        smooth_out[k] = sm
        last_out[k] = drift[127:128, :1] * sm[127:128, :]


def drag_kernel(last, bnd, drag, cell, inv, gain, drift, w, smooth, up, ions, n_out, wire, t, s):
    first = lax.broadcasted_iota(i32, (128, 128), 0) == 0
    d = drift[...]
    n = [[], []]
    for k in range(2):
        for j in range(4):
            sl = slice(j*128, (j+1)*128)
            sm = smooth[k, :, sl]
            out = d * sm
            inflow = jnp.where(first, jnp.broadcast_to(up[k, :, sl], (128, 128)), pltpu.roll(out, 1, 0))
            x = sm - out + inflow
            n[k].append(x)
            n_out[k, :, sl] = 0.5 * (ions[k, :, sl] + x) if last else x
    for j in range(4):
        f = -(drag[0] * n[0][j] + drag[1] * n[1][j])
        for k in range(2):
            t[k, j*128:(j+1)*128, :] = f * w[k, :, j*128:(j+1)*128]
    lookup(bnd, cell, t, s)
    to_wire(inv, s, wire, gain)


def tend_all(wind, forcing, visc, xlo, xhi, ylo, yhi, acc, emit):
    CX, CY = wind.shape[1], wind.shape[2]
    sub = lax.broadcasted_iota(i32, (CY, 128), 0)
    lane = lax.broadcasted_iota(i32, (CY, 128), 1)
    v = jnp.broadcast_to(visc[...], (CY, 128))
    for k in range(2):
        for i in range(CX):
            u = wind[k, i]
            b = (wind[k, i+1] if i < CX-1 else xhi[k, 0]) + (wind[k, i-1] if i > 0 else xlo[k, 0])
            nxt = jnp.where(sub == CY-1, jnp.broadcast_to(yhi[k, i], (CY, 128)), pltpu.roll(u, CY-1, 0))
            prv = jnp.where(sub == 0, jnp.broadcast_to(ylo[k, i], (CY, 128)), pltpu.roll(u, 1, 0))
            b = b + nxt + prv
            b = b + jnp.where(lane == 127, 0.0, pltpu.roll(u, 127, 1)) + jnp.where(lane == 0, 0.0, pltpu.roll(u, 1, 1))
            emit(k, i, u, v * (b - 6.0 * u) + acc[i*CY:(i+1)*CY, k*128:(k+1)*128] + forcing[k, i])


def mid_kernel(bnd, cell, pos, inv, wire, wind, forcing, visc, xlo, xhi, ylo, yhi, mid, wire_out, val, acc, s):
    from_wire(pos, wire, val)
    scatter_add(bnd, cell, val, acc)
    CY = wind.shape[2]

    def emit(k, i, u, f):
        mid[k, i*CY:(i+1)*CY, :] = u + neutral_step * f

    tend_all(wind, forcing, visc, xlo, xhi, ylo, yhi, acc, emit)
    lookup(bnd, cell, mid, s)
    to_wire(inv, s, wire_out)


def end_kernel(bnd, cell, pos, wire, start, wind, forcing, visc, xlo, xhi, ylo, yhi, out, val, acc):
    from_wire(pos, wire, val)
    scatter_add(bnd, cell, val, acc)

    def emit(k, i, u, f):
        out[k, i] = 0.5 * (start[k, i] + u) + (0.5 * neutral_step) * f

    tend_all(wind, forcing, visc, xlo, xhi, ylo, yhi, acc, emit)


def call(kernel, outs, scratch, *args, smem=1, name=None):
    return pl.pallas_call(
        kernel,
        out_shape=outs,
        in_specs=[SM] * smem + [VM] * (len(args) - smem),
        out_specs=jax.tree.map(lambda _: VM, outs),
        scratch_shapes=scratch,
        name=name,
    )(*args)


def edges(wind):
    out = []
    for axis, dim in (("gx", 1), ("gy", 2)):
        peers, length = lax.axis_size(axis), wind.shape[dim]
        up = [(i, i + 1) for i in range(peers - 1)]
        out.append(lax.ppermute(lax.slice_in_dim(wind, length - 1, length, axis=dim), axis, up))
        out.append(lax.ppermute(lax.slice_in_dim(wind, 0, 1, axis=dim), axis, [(b, a) for a, b in up]))
    return out


def exchange(x):
    return lax.all_to_all(x, ("gx", "gy"), split_axis=0, concat_axis=0, tiled=True)


def per_device(
    neutral_wind,
    forcing,
    ion_density,
    inverse,
    drift_fraction,
    viscosity,
    coupling,
    drag_rate,
    outgoing_column,
    send_level,
    recv_tube,
    recv_point,
    recv_weight,
    pair_count,
):
    own = lax.axis_index(("gx", "gy"))
    cap = recv_weight.shape[2]
    incoming = lax.dynamic_slice_in_dim(pair_count, own, 1, 1)
    position = lax.broadcasted_iota(i32, (128, cap), 1)
    gain = recv_weight[0] * (position < incoming).astype(f32)
    drift = jnp.broadcast_to(drift_fraction[:, None], (128, 128))
    visc = viscosity[None, :]
    sd = jax.ShapeDtypeStruct
    wire_t = sd((128, 4, 128), f32)
    tube_t = sd(ion_density.shape, f32)
    vals = pltpu.VMEM((2, 256, 128), f32)
    accs = pltpu.VMEM((512 + W, 256), f32)
    tabs = pltpu.VMEM((2, 512, 128), f32)
    cA, pA, iA, bA, cB, pB, iB, bB = sort_call(outgoing_column, send_level, recv_tube, recv_point)
    flat = (2, 512, 128)
    up_route = [(i, i + 1) for i in range(lax.axis_size("gy") - 1)]

    def tubes(wire, ions, last):
        w, smooth, out_last = call(
            tube_kernel, (tube_t, tube_t, sd((2, 1, 512), f32)), [vals, accs],
            bB, coupling, cB, pB, gain, drift, wire, ions, inverse, smem=2, name="tube")
        up = lax.ppermute(out_last, "gy", up_route)
        return call(
            lambda *a: drag_kernel(last, *a), (tube_t, wire_t), [tabs, vals],
            bB, drag_rate, cB, iB, gain, drift, w, smooth, up, ion_density, smem=2, name="drag")

    halo = edges(neutral_wind)
    wire = call(gather_kernel, wire_t, [vals], bA, cA, iA, neutral_wind.reshape(flat), name="first")
    n1, wire = tubes(exchange(wire), ion_density, False)
    mid, wire = call(
        mid_kernel, (sd(flat, f32), wire_t), [vals, accs, vals],
        bA, cA, pA, iA, exchange(wire), neutral_wind, forcing, visc, *halo, name="mid")
    mid = mid.reshape(neutral_wind.shape)
    halo = edges(mid)
    ion_out, wire = tubes(exchange(wire), n1, True)
    wind_out = call(
        end_kernel, sd(neutral_wind.shape, f32), [vals, accs],
        bA, cA, pA, exchange(wire), neutral_wind, mid, forcing, visc, *halo, name="end")
    return (wind_out, ion_out)


def solution(mesh):
    placed = (
        P(None, "gx", "gy", None),
        P(None, "gx", "gy", None),
        P(None, ("gx", "gy"), None),
        P("gx", None, None, None),
        P(("gx", "gy")),
        P(),
        P(),
        P(),
        P(("gx", "gy"), None, None),
        P(("gx", "gy"), None, None),
        P(("gx", "gy"), None, None),
        P(("gx", "gy"), None, None),
        P(("gx", "gy"), None, None),
        P(),
    )
    return jax.shard_map(
        per_device,
        mesh=mesh,
        in_specs=placed,
        out_specs=(P(None, "gx", "gy", None), P(None, ("gx", "gy"), None)),
        check_vma=False,
    )
```

```python
import jax
import jax.numpy as jnp
from jax import lax
from jax.experimental import pallas as pl
from jax.experimental.pallas import tpu as pltpu
from jax.sharding import PartitionSpec as P

i32, f32, bf16 = jnp.int32, jnp.float32, jnp.bfloat16
VM = pl.BlockSpec(memory_space=pltpu.VMEM)
SM = pl.BlockSpec(memory_space=pltpu.SMEM)
W, NB, LB, LR = 64, 16, 8, 16
neutral_step = 0.4
ion_factor = 0.5


def bitonic(x):
    n, L = x.shape
    x = x.reshape(n//8, 8, L)
    sub = lax.broadcasted_iota(i32, (1, 8, L), 1)
    k = 2
    while k <= n:
        d = k//2
        while d >= 1:
            if d >= 8:
                dv = d//8
                y = x.reshape(n//(16*dv), 2, dv, 8, L)
                a, b = y[:, 0], y[:, 1]
                lo, hi = jnp.minimum(a, b), jnp.maximum(a, b)
                parts = []
                for g in range(n//(16*dv)):
                    up = ((g*2*d) & k) == 0
                    parts += [lo[g], hi[g]] if up else [hi[g], lo[g]]
                x = jnp.concatenate(parts, axis=0)
            else:
                up_r = pltpu.roll(x, 8-d, 1)
                dn_r = pltpu.roll(x, d, 1)
                first = (sub & d) == 0
                p = jnp.where(first, up_r, dn_r)
                mn, mx = jnp.minimum(x, p), jnp.maximum(x, p)
                if k >= 8:
                    if k == 8:
                        vi = lax.broadcasted_iota(i32, (n//8, 1, 1), 0)
                    parts = []
                    xs = []
                    take_min_up = first
                    kv = k//8
                    for g in range(0, n//8, kv):
                        up = (g*8 & k) == 0
                        sel = first if up else jnp.logical_not(first)
                        xs.append(jnp.where(sel, mn[g:g+kv], mx[g:g+kv]))
                    x = jnp.concatenate(xs, axis=0) if len(xs) > 1 else xs[0]
                else:
                    up = (sub & k) == 0
                    sel = first == up
                    x = jnp.where(sel, mn, mx)
            d //= 2
        k *= 2
    return x.reshape(n, L)

def sort_side(key16, cell_ref, pos_ref, inv_ref, bnd_ref):
    P, C = key16.shape
    c = lax.broadcasted_iota(i32, (P, C), 1)
    k = (key16 * 256 + c).T
    s = bitonic(k)
    cell = s >> 8
    pos = s & 255
    cell_ref[...] = cell
    pos_ref[...] = pos.T
    r = lax.broadcasted_iota(i32, (C, P), 0)
    inv = bitonic(pos*256 + r) & 255
    inv_ref[...] = inv.T
    row = (cell >> 7).reshape(C//8, 8, P)
    lo = jnp.min(jnp.min(row, axis=1), axis=1, keepdims=True)
    hi = jnp.max(jnp.max(row, axis=1), axis=1, keepdims=True)
    lane = lax.broadcasted_iota(i32, (C//8, 128), 1)
    bnd_ref[...] = jnp.where(lane == 0, lo, hi)

def sort_kernel(col, lev, tub, pnt, cellA, posA, invA, bndA, cellB, posB, invB, bndB):
    def key(row, lane):
        return ((row & 255) << 8) + ((row >> 8) << 7) + lane

    sort_side(key(col[0], lev[0]), cellA, posA, invA, bndA)
    p = pnt[0]
    sort_side(key((p >> 7)*128 + tub[0], p & 127), cellB, posB, invB, bndB)

def sort_call(col, lev, tub, pnt):
    P, C = col.shape[1:]
    side = [jax.ShapeDtypeStruct((C, P), i32), jax.ShapeDtypeStruct((P, C), i32), jax.ShapeDtypeStruct((P, C), i32), jax.ShapeDtypeStruct((C//8, 128), i32)]
    return pl.pallas_call(sort_kernel, out_shape=side*2, in_specs=[VM]*4, out_specs=[VM]*8, name="sort")(col, lev, tub, pnt)

def permute_lanes(x, idx):
    outs = []
    for h in range(2):
        ix = idx[:, h*128:(h+1)*128]
        low = ix & 127
        a = jnp.take_along_axis(x[:, :128], low, axis=1)
        b = jnp.take_along_axis(x[:, 128:], low, axis=1)
        outs.append(jnp.where(ix < 128, a, b))
    return outs

def lookup(bnd, cell_ref, t_ref, s_ref):
    half = t_ref.shape[1] // 2

    def blocks(u, _):
        row, lev, start, count = [], [], [], None
        for i in range(LB):
            v = u*LB + i
            key = cell_ref[pl.ds(pl.multiple_of(v*8, 8), 8), :]
            row.append(key >> 7)
            lev.append(key & 127)
            lo = bnd[v, 0] >> 1
            start.append(lo)
            need = (bnd[v, 1] - 2*lo) // LR + 1
            count = need if count is None else jnp.maximum(count, need)

        def rows(g, acc):
            acc = list(acc)
            for i in range(LB):
                base = jnp.minimum(start[i] + g*(LR//2), half - LR//2)
                rel = row[i] - 2*base
                for j in range(LR):
                    m = rel == j
                    for k in range(2):
                        x = t_ref[k, pl.ds(base + (j//2) + (j % 2)*half, 1), :]
                        x = jnp.take_along_axis(jnp.broadcast_to(x, (8, 128)), lev[i], axis=1, mode="promise_in_bounds")
                        acc[2*i+k] = jnp.where(m, x, acc[2*i+k])
            return tuple(acc)

        acc = lax.fori_loop(0, count, rows, (jnp.zeros((8, 128), f32),)*(2*LB))
        for i in range(LB):
            for k in range(2):
                s_ref[k, pl.ds(pl.multiple_of((u*LB + i)*8, 8), 8), :] = acc[2*i+k]
        return 0

    lax.fori_loop(0, 32//LB, blocks, 0)


def scatter_add(bnd, cell_ref, val_ref, acc_ref):
    acc_ref[...] = jnp.zeros_like(acc_ref)
    iota = lax.broadcasted_iota(i32, (256, 128), 0).astype(f32).astype(bf16)
    one, zero = jnp.ones((256, 128), bf16), jnp.zeros((256, 128), bf16)

    def spread(x, n):
        return jnp.broadcast_to(x, (n, 128)).astype(bf16)

    def block(v, _):
        sl = pl.ds(pl.multiple_of(v*NB, 8), NB)
        key = cell_ref[sl, :]
        q, lane = key >> 8, (key & 255).astype(f32)
        lo, hi = bnd[v*(NB//8), 0] >> 1, bnd[(v+1)*(NB//8) - 1, 1] >> 1
        base = (lo // 8) * 8
        vals = []
        for k in range(2):
            x = val_ref[k, sl, :]
            h = x.astype(bf16).astype(f32)
            vals += [h, x - h]
        lanes = jnp.concatenate([jnp.where(iota == spread(lane[r:r+1], 256), one, zero) for r in range(NB)], axis=1)

        def window(it, _):
            rb = pl.multiple_of(base + it*W, 8)
            rel = (q - rb).astype(f32)
            rows = []
            for r in range(NB):
                m = iota[:W] == spread(rel[r:r+1], W)
                rows.append(jnp.concatenate([jnp.where(m, spread(x[r:r+1], W), zero[:W]) for x in vals], axis=0))
            z = lax.dot_general(jnp.concatenate(rows, axis=1), lanes, (((1,), (1,)), ((), ())), preferred_element_type=f32)
            for k in range(2):
                acc_ref[k, pl.ds(rb, W), :] += z[2*k*W:(2*k+1)*W] + z[(2*k+1)*W:(2*k+2)*W]
            return 0

        lax.fori_loop(0, (hi - base)//W + 1, window, 0)
        return 0

    lax.fori_loop(0, 256//NB, block, 0)


def to_wire(inv, s, out, gain=None):
    for k in range(2):
        o = permute_lanes(s[k].T, inv[...])
        for h in range(2):
            x = o[h]
            if gain is not None:
                x = x * gain[:, h*128:(h+1)*128]
            out[:, 2*k+h, :] = x


def from_wire(pos, wire, val, gain=None):
    for k in range(2):
        x = [wire[:, 2*k+h, :] for h in range(2)]
        if gain is not None:
            x = [x[h] * gain[:, h*128:(h+1)*128] for h in range(2)]
        o = permute_lanes(jnp.concatenate(x, axis=1), pos[...])
        val[k, :128, :] = o[0].T
        val[k, 128:, :] = o[1].T


def gather_kernel(bnd, cell, inv, t, out, s):
    lookup(bnd, cell, t, s)
    to_wire(inv, s, out)


def tube_kernel(bnd, coupling, cell, pos, gain, drift, wire, ions, inverse, w_out, smooth_out, last_out, val, acc):
    from_wire(pos, wire, val, gain)
    scatter_add(bnd, cell, val, acc)
    w = []
    for k in range(2):
        for j in range(4):
            w_out[k, :, j*128:(j+1)*128] = acc[k, (j%2)*128:(j%2+1)*128, (j//2)*128:(j//2+1)*128]
    for k in range(2):
        n = ions[k]
        growth = coupling[k, 0] * w_out[0] + coupling[k, 1] * w_out[1]
        rhs = n + ion_factor * n * growth
        mix = lax.dot_general(rhs.astype(bf16), inverse[0, k], (((1,), (0,)), ((), ())), preferred_element_type=f32)
        sm = rhs + mix
        smooth_out[k] = sm
        last_out[k] = drift[127:128, :1] * sm[127:128, :]


def drag_kernel(last, bnd, drag, cell, inv, gain, drift, w, smooth, up, ions, n_out, wire, t, s):
    first = lax.broadcasted_iota(i32, (128, 128), 0) == 0
    d = drift[...]
    n = [[], []]
    for k in range(2):
        for j in range(4):
            sl = slice(j*128, (j+1)*128)
            sm = smooth[k, :, sl]
            out = d * sm
            inflow = jnp.where(first, jnp.broadcast_to(up[k, :, sl], (128, 128)), pltpu.roll(out, 1, 0))
            x = sm - out + inflow
            n[k].append(x)
            n_out[k, :, sl] = 0.5 * (ions[k, :, sl] + x) if last else x
    for j in range(4):
        f = -(drag[0] * n[0][j] + drag[1] * n[1][j])
        for k in range(2):
            t[k, j*128:(j+1)*128, :] = f * w[k, :, j*128:(j+1)*128]
    lookup(bnd, cell, t, s)
    to_wire(inv, s, wire, gain)


def tend_all(wind, forcing, visc, xlo, xhi, ylo, yhi, acc, emit):
    CX, CY = wind.shape[1], wind.shape[2]
    sub = lax.broadcasted_iota(i32, (CY, 128), 0)
    lane = lax.broadcasted_iota(i32, (CY, 128), 1)
    v = jnp.broadcast_to(visc[...], (CY, 128))
    for k in range(2):
        for i in range(CX):
            u = wind[k, i]
            b = (wind[k, i+1] if i < CX-1 else xhi[k, 0]) + (wind[k, i-1] if i > 0 else xlo[k, 0])
            nxt = jnp.where(sub == CY-1, jnp.broadcast_to(yhi[k, i], (CY, 128)), pltpu.roll(u, CY-1, 0))
            prv = jnp.where(sub == 0, jnp.broadcast_to(ylo[k, i], (CY, 128)), pltpu.roll(u, 1, 0))
            b = b + nxt + prv
            b = b + jnp.where(lane == 127, 0.0, pltpu.roll(u, 127, 1)) + jnp.where(lane == 0, 0.0, pltpu.roll(u, 1, 1))
            emit(k, i, u, v * (b - 6.0 * u) + acc[k, (i*CY) % 256:(i*CY) % 256 + CY, (i*CY)//256*128:(i*CY)//256*128 + 128] + forcing[k, i])


def mid_kernel(bnd, cell, pos, inv, wire, wind, forcing, visc, xlo, xhi, ylo, yhi, mid, wire_out, val, acc, s):
    from_wire(pos, wire, val)
    scatter_add(bnd, cell, val, acc)
    CY = wind.shape[2]

    def emit(k, i, u, f):
        mid[k, i*CY:(i+1)*CY, :] = u + neutral_step * f

    tend_all(wind, forcing, visc, xlo, xhi, ylo, yhi, acc, emit)
    lookup(bnd, cell, mid, s)
    to_wire(inv, s, wire_out)


def end_kernel(bnd, cell, pos, wire, start, wind, forcing, visc, xlo, xhi, ylo, yhi, out, val, acc):
    from_wire(pos, wire, val)
    scatter_add(bnd, cell, val, acc)

    def emit(k, i, u, f):
        out[k, i] = 0.5 * (start[k, i] + u) + (0.5 * neutral_step) * f

    tend_all(wind, forcing, visc, xlo, xhi, ylo, yhi, acc, emit)


def call(kernel, outs, scratch, *args, smem=1, name=None):
    return pl.pallas_call(
        kernel,
        out_shape=outs,
        in_specs=[SM] * smem + [VM] * (len(args) - smem),
        out_specs=jax.tree.map(lambda _: VM, outs),
        scratch_shapes=scratch,
        name=name,
    )(*args)


def edges(wind):
    out = []
    for axis, dim in (("gx", 1), ("gy", 2)):
        peers, length = lax.axis_size(axis), wind.shape[dim]
        up = [(i, i + 1) for i in range(peers - 1)]
        out.append(lax.ppermute(lax.slice_in_dim(wind, length - 1, length, axis=dim), axis, up))
        out.append(lax.ppermute(lax.slice_in_dim(wind, 0, 1, axis=dim), axis, [(b, a) for a, b in up]))
    return out


def exchange(x):
    return lax.all_to_all(x, ("gx", "gy"), split_axis=0, concat_axis=0, tiled=True)


def per_device(
    neutral_wind,
    forcing,
    ion_density,
    inverse,
    drift_fraction,
    viscosity,
    coupling,
    drag_rate,
    outgoing_column,
    send_level,
    recv_tube,
    recv_point,
    recv_weight,
    pair_count,
):
    own = lax.axis_index(("gx", "gy"))
    cap = recv_weight.shape[2]
    incoming = lax.dynamic_slice_in_dim(pair_count, own, 1, 1)
    position = lax.broadcasted_iota(i32, (128, cap), 1)
    gain = recv_weight[0] * (position < incoming).astype(f32)
    drift = jnp.broadcast_to(drift_fraction[:, None], (128, 128))
    visc = viscosity[None, :]
    sd = jax.ShapeDtypeStruct
    wire_t = sd((128, 4, 128), f32)
    tube_t = sd(ion_density.shape, f32)
    vals = pltpu.VMEM((2, 256, 128), f32)
    accs = pltpu.VMEM((2, 256 + W, 256), f32)
    tabs = pltpu.VMEM((2, 512, 128), f32)
    cA, pA, iA, bA, cB, pB, iB, bB = sort_call(outgoing_column, send_level, recv_tube, recv_point)
    flat = (2, 512, 128)
    up_route = [(i, i + 1) for i in range(lax.axis_size("gy") - 1)]

    def tubes(wire, ions, last):
        w, smooth, out_last = call(
            tube_kernel, (tube_t, tube_t, sd((2, 1, 512), f32)), [vals, accs],
            bB, coupling, cB, pB, gain, drift, wire, ions, inverse, smem=2, name="tube")
        up = lax.ppermute(out_last, "gy", up_route)
        return call(
            lambda *a: drag_kernel(last, *a), (tube_t, wire_t), [tabs, vals],
            bB, drag_rate, cB, iB, gain, drift, w, smooth, up, ion_density, smem=2, name="drag")

    halo = edges(neutral_wind)
    wire = call(gather_kernel, wire_t, [vals], bA, cA, iA, neutral_wind.reshape(flat), name="first")
    n1, wire = tubes(exchange(wire), ion_density, False)
    mid, wire = call(
        mid_kernel, (sd(flat, f32), wire_t), [vals, accs, vals],
        bA, cA, pA, iA, exchange(wire), neutral_wind, forcing, visc, *halo, name="mid")
    mid = mid.reshape(neutral_wind.shape)
    halo = edges(mid)
    ion_out, wire = tubes(exchange(wire), n1, True)
    wind_out = call(
        end_kernel, sd(neutral_wind.shape, f32), [vals, accs],
        bA, cA, pA, exchange(wire), neutral_wind, mid, forcing, visc, *halo, name="end")
    return (wind_out, ion_out)


def solution(mesh):
    placed = (
        P(None, "gx", "gy", None),
        P(None, "gx", "gy", None),
        P(None, ("gx", "gy"), None),
        P("gx", None, None, None),
        P(("gx", "gy")),
        P(),
        P(),
        P(),
        P(("gx", "gy"), None, None),
        P(("gx", "gy"), None, None),
        P(("gx", "gy"), None, None),
        P(("gx", "gy"), None, None),
        P(("gx", "gy"), None, None),
        P(),
    )
    return jax.shard_map(
        per_device,
        mesh=mesh,
        in_specs=placed,
        out_specs=(P(None, "gx", "gy", None), P(None, ("gx", "gy"), None)),
        check_vma=False,
    )
```

```python
import jax
import jax.numpy as jnp
from jax import lax
from jax.experimental import pallas as pl
from jax.experimental.pallas import tpu as pltpu
from jax.sharding import PartitionSpec as P

i32, f32, bf16 = jnp.int32, jnp.float32, jnp.bfloat16
VM = pl.BlockSpec(memory_space=pltpu.VMEM)
SM = pl.BlockSpec(memory_space=pltpu.SMEM)
W, NB, LB, LR = 64, 16, 8, 16
neutral_step = 0.4
ion_factor = 0.5


def bitonic(x):
    n, L = x.shape
    x = x.reshape(n//8, 8, L)
    sub = lax.broadcasted_iota(i32, (1, 8, L), 1)
    k = 2
    while k <= n:
        d = k//2
        while d >= 1:
            if d >= 8:
                dv = d//8
                y = x.reshape(n//(16*dv), 2, dv, 8, L)
                a, b = y[:, 0], y[:, 1]
                lo, hi = jnp.minimum(a, b), jnp.maximum(a, b)
                parts = []
                for g in range(n//(16*dv)):
                    up = ((g*2*d) & k) == 0
                    parts += [lo[g], hi[g]] if up else [hi[g], lo[g]]
                x = jnp.concatenate(parts, axis=0)
            else:
                up_r = pltpu.roll(x, 8-d, 1)
                dn_r = pltpu.roll(x, d, 1)
                first = (sub & d) == 0
                p = jnp.where(first, up_r, dn_r)
                mn, mx = jnp.minimum(x, p), jnp.maximum(x, p)
                if k >= 8:
                    if k == 8:
                        vi = lax.broadcasted_iota(i32, (n//8, 1, 1), 0)
                    parts = []
                    xs = []
                    take_min_up = first
                    kv = k//8
                    for g in range(0, n//8, kv):
                        up = (g*8 & k) == 0
                        sel = first if up else jnp.logical_not(first)
                        xs.append(jnp.where(sel, mn[g:g+kv], mx[g:g+kv]))
                    x = jnp.concatenate(xs, axis=0) if len(xs) > 1 else xs[0]
                else:
                    up = (sub & k) == 0
                    sel = first == up
                    x = jnp.where(sel, mn, mx)
            d //= 2
        k *= 2
    return x.reshape(n, L)

def sort_side(key16, cell_ref, pos_ref, inv_ref, bnd_ref):
    P, C = key16.shape
    c = lax.broadcasted_iota(i32, (P, C), 1)
    k = (key16 * 256 + c).T
    s = bitonic(k)
    cell = s >> 8
    pos = s & 255
    cell_ref[...] = cell
    pos_ref[...] = pos.T
    r = lax.broadcasted_iota(i32, (C, P), 0)
    inv = bitonic(pos*256 + r) & 255
    inv_ref[...] = inv.T
    row = (cell >> 7).reshape(C//8, 8, P)
    lo = jnp.min(jnp.min(row, axis=1), axis=1, keepdims=True)
    hi = jnp.max(jnp.max(row, axis=1), axis=1, keepdims=True)
    lane = lax.broadcasted_iota(i32, (C//8, 128), 1)
    bnd_ref[...] = jnp.where(lane == 0, lo, hi)

def cell_key(row, lane):
    return ((row & 255) << 8) + ((row >> 8) << 7) + lane


def put_edges(get, xa, xb, ya, yb):
    for k in range(2):
        xa[k, 0] = get(k, 0)
        n = ya.shape[1]
        xb[k, 0] = get(k, n-1)
        for i in range(n):
            u = get(k, i)
            ya[k, i] = u[:1]
            yb[k, i] = u[-1:]


def tile_sort_kernel(col, lev, wind, cell, pos, inv, bnd, *edge):
    sort_side(cell_key(col[0], lev[0]), cell, pos, inv, bnd)
    put_edges(lambda k, i: wind[k, i], *edge)


def tube_sort_kernel(tub, pnt, weight, count, drift, cell, pos, inv, bnd, gain, drift_out):
    p = pnt[0]
    sort_side(cell_key((p >> 7)*128 + tub[0], p & 127), cell, pos, inv, bnd)
    own = lax.axis_index("gx") * lax.axis_size("gy") + lax.axis_index("gy")
    lane = lax.broadcasted_iota(i32, (128, 128), 1)
    live = jnp.sum(jnp.where(lane == own, count[...], 0).astype(f32), axis=1, keepdims=True)
    c = lax.broadcasted_iota(i32, (128, 256), 1).astype(f32)
    gain[...] = jnp.where(c < live, weight[0], 0.0)
    drift_out[...] = jnp.broadcast_to(drift[...], (128, 128)).T


def permute_lanes(x, idx):
    outs = []
    for h in range(2):
        ix = idx[:, h*128:(h+1)*128]
        low = ix & 127
        a = jnp.take_along_axis(x[:, :128], low, axis=1)
        b = jnp.take_along_axis(x[:, 128:], low, axis=1)
        outs.append(jnp.where(ix < 128, a, b))
    return outs

def lookup(bnd, cell_ref, t_ref, s_ref):
    half = t_ref.shape[1] // 2

    def blocks(u, _):
        row, lev, start, count = [], [], [], None
        for i in range(LB):
            v = u*LB + i
            key = cell_ref[pl.ds(pl.multiple_of(v*8, 8), 8), :]
            row.append(key >> 7)
            lev.append(key & 127)
            lo = bnd[v, 0] >> 1
            start.append(lo)
            need = (bnd[v, 1] - 2*lo) // LR + 1
            count = need if count is None else jnp.maximum(count, need)

        def rows(g, acc):
            acc = list(acc)
            for i in range(LB):
                base = jnp.minimum(start[i] + g*(LR//2), half - LR//2)
                rel = row[i] - 2*base
                for j in range(LR):
                    m = rel == j
                    for k in range(2):
                        x = t_ref[k, pl.ds(base + (j//2) + (j % 2)*half, 1), :]
                        x = jnp.take_along_axis(jnp.broadcast_to(x, (8, 128)), lev[i], axis=1, mode="promise_in_bounds")
                        acc[2*i+k] = jnp.where(m, x, acc[2*i+k])
            return tuple(acc)

        acc = lax.fori_loop(0, count, rows, (jnp.zeros((8, 128), f32),)*(2*LB))
        for i in range(LB):
            for k in range(2):
                s_ref[k, pl.ds(pl.multiple_of((u*LB + i)*8, 8), 8), :] = acc[2*i+k]
        return 0

    lax.fori_loop(0, 32//LB, blocks, 0)


def scatter_add(bnd, cell_ref, val_ref, acc_ref):
    acc_ref[...] = jnp.zeros_like(acc_ref)
    iota = lax.broadcasted_iota(i32, (256, 128), 0).astype(f32).astype(bf16)
    one, zero = jnp.ones((256, 128), bf16), jnp.zeros((256, 128), bf16)

    def spread(x, n):
        return jnp.broadcast_to(x, (n, 128)).astype(bf16)

    def block(v, _):
        sl = pl.ds(pl.multiple_of(v*NB, 8), NB)
        key = cell_ref[sl, :]
        q, lane = key >> 8, (key & 255).astype(f32)
        lo, hi = bnd[v*(NB//8), 0] >> 1, bnd[(v+1)*(NB//8) - 1, 1] >> 1
        base = (lo // 8) * 8
        vals = []
        for k in range(2):
            x = val_ref[k, sl, :]
            h = x.astype(bf16).astype(f32)
            vals += [h, x - h]
        lanes = jnp.concatenate([jnp.where(iota == spread(lane[r:r+1], 256), one, zero) for r in range(NB)], axis=1)

        def window(it, _):
            rb = pl.multiple_of(base + it*W, 8)
            rel = (q - rb).astype(f32)
            rows = []
            for r in range(NB):
                m = iota[:W] == spread(rel[r:r+1], W)
                rows.append(jnp.concatenate([jnp.where(m, spread(x[r:r+1], W), zero[:W]) for x in vals], axis=0))
            z = lax.dot_general(jnp.concatenate(rows, axis=1), lanes, (((1,), (1,)), ((), ())), preferred_element_type=f32)
            for k in range(2):
                acc_ref[k, pl.ds(rb, W), :] += z[2*k*W:(2*k+1)*W] + z[(2*k+1)*W:(2*k+2)*W]
            return 0

        lax.fori_loop(0, (hi - base)//W + 1, window, 0)
        return 0

    lax.fori_loop(0, 256//NB, block, 0)


def to_wire(inv, s, out, gain=None):
    for k in range(2):
        o = permute_lanes(s[k].T, inv[...])
        for h in range(2):
            x = o[h]
            if gain is not None:
                x = x * gain[:, h*128:(h+1)*128]
            out[:, 2*k+h, :] = x


def from_wire(pos, wire, val, gain=None):
    for k in range(2):
        x = [wire[:, 2*k+h, :] for h in range(2)]
        if gain is not None:
            x = [x[h] * gain[:, h*128:(h+1)*128] for h in range(2)]
        o = permute_lanes(jnp.concatenate(x, axis=1), pos[...])
        val[k, :128, :] = o[0].T
        val[k, 128:, :] = o[1].T


def gather_kernel(bnd, cell, inv, t, out, s):
    lookup(bnd, cell, t, s)
    to_wire(inv, s, out)


def tube_kernel(bnd, coupling, cell, pos, gain, drift, wire, ions, inverse, w_out, smooth_out, last_out, val, acc):
    from_wire(pos, wire, val, gain)
    scatter_add(bnd, cell, val, acc)
    w = []
    for k in range(2):
        for j in range(4):
            w_out[k, :, j*128:(j+1)*128] = acc[k, (j%2)*128:(j%2+1)*128, (j//2)*128:(j//2+1)*128]
    for k in range(2):
        n = ions[k]
        growth = coupling[k, 0] * w_out[0] + coupling[k, 1] * w_out[1]
        rhs = n + ion_factor * n * growth
        mix = lax.dot_general(rhs.astype(bf16), inverse[0, k], (((1,), (0,)), ((), ())), preferred_element_type=f32)
        sm = rhs + mix
        smooth_out[k] = sm
        last_out[k] = drift[127:128, :1] * sm[127:128, :]


def drag_kernel(last, bnd, drag, cell, inv, gain, drift, w, smooth, up, ions, n_out, wire, t, s):
    first = lax.broadcasted_iota(i32, (128, 128), 0) == 0
    d = drift[...]
    n = [[], []]
    for k in range(2):
        for j in range(4):
            sl = slice(j*128, (j+1)*128)
            sm = smooth[k, :, sl]
            out = d * sm
            inflow = jnp.where(first, jnp.broadcast_to(up[k, :, sl], (128, 128)), pltpu.roll(out, 1, 0))
            x = sm - out + inflow
            n[k].append(x)
            n_out[k, :, sl] = 0.5 * (ions[k, :, sl] + x) if last else x
    for j in range(4):
        f = -(drag[0] * n[0][j] + drag[1] * n[1][j])
        for k in range(2):
            t[k, j*128:(j+1)*128, :] = f * w[k, :, j*128:(j+1)*128]
    lookup(bnd, cell, t, s)
    to_wire(inv, s, wire, gain)


def tend_all(wind, forcing, visc, xlo, xhi, ylo, yhi, acc, emit):
    CX, CY = wind.shape[1], wind.shape[2]
    sub = lax.broadcasted_iota(i32, (CY, 128), 0)
    lane = lax.broadcasted_iota(i32, (CY, 128), 1)
    v = jnp.broadcast_to(visc[...], (CY, 128))
    for k in range(2):
        for i in range(CX):
            u = wind[k, i]
            b = (wind[k, i+1] if i < CX-1 else xhi[k, 0]) + (wind[k, i-1] if i > 0 else xlo[k, 0])
            nxt = jnp.where(sub == CY-1, jnp.broadcast_to(yhi[k, i], (CY, 128)), pltpu.roll(u, CY-1, 0))
            prv = jnp.where(sub == 0, jnp.broadcast_to(ylo[k, i], (CY, 128)), pltpu.roll(u, 1, 0))
            b = b + nxt + prv
            b = b + jnp.where(lane == 127, 0.0, pltpu.roll(u, 127, 1)) + jnp.where(lane == 0, 0.0, pltpu.roll(u, 1, 1))
            emit(k, i, u, v * (b - 6.0 * u) + acc[k, (i*CY) % 256:(i*CY) % 256 + CY, (i*CY)//256*128:(i*CY)//256*128 + 128] + forcing[k, i])


def mid_kernel(bnd, cell, pos, inv, wire, wind, forcing, visc, xlo, xhi, ylo, yhi, mid, wire_out, xa, xb, ya, yb, val, acc, s):
    from_wire(pos, wire, val)
    scatter_add(bnd, cell, val, acc)
    CY = wind.shape[2]

    def emit(k, i, u, f):
        mid[k, i*CY:(i+1)*CY, :] = u + neutral_step * f

    tend_all(wind, forcing, visc, xlo, xhi, ylo, yhi, acc, emit)
    put_edges(lambda k, i: mid[k, i*CY:(i+1)*CY, :], xa, xb, ya, yb)
    lookup(bnd, cell, mid, s)
    to_wire(inv, s, wire_out)


def end_kernel(bnd, cell, pos, wire, start, wind, forcing, visc, xlo, xhi, ylo, yhi, out, val, acc):
    from_wire(pos, wire, val)
    scatter_add(bnd, cell, val, acc)

    def emit(k, i, u, f):
        out[k, i] = 0.5 * (start[k, i] + u) + (0.5 * neutral_step) * f

    tend_all(wind, forcing, visc, xlo, xhi, ylo, yhi, acc, emit)


def call(kernel, outs, scratch, *args, smem=1, name=None):
    return pl.pallas_call(
        kernel,
        out_shape=outs,
        in_specs=[SM] * smem + [VM] * (len(args) - smem),
        out_specs=jax.tree.map(lambda _: VM, outs),
        scratch_shapes=scratch,
        name=name,
    )(*args)


def beside(axis, first, last):
    peers = lax.axis_size(axis)
    up = [(i, i + 1) for i in range(peers - 1)]
    return [lax.ppermute(last, axis, up), lax.ppermute(first, axis, [(b, a) for a, b in up])]


def tied(*arrays):
    return lax.optimization_barrier(arrays)


def exchange(x):
    return lax.all_to_all(x, ("gx", "gy"), split_axis=0, concat_axis=0, tiled=True)


def per_device(
    neutral_wind,
    forcing,
    ion_density,
    inverse,
    drift_fraction,
    viscosity,
    coupling,
    drag_rate,
    outgoing_column,
    send_level,
    recv_tube,
    recv_point,
    recv_weight,
    pair_count,
):
    visc = viscosity[None, :]
    sd = jax.ShapeDtypeStruct
    wire_t = sd((128, 4, 128), f32)
    tube_t = sd(ion_density.shape, f32)
    vals = pltpu.VMEM((2, 256, 128), f32)
    accs = pltpu.VMEM((2, 256 + W, 256), f32)
    tabs = pltpu.VMEM((2, 512, 128), f32)
    flat = (2, 512, 128)
    up_route = [(i, i + 1) for i in range(lax.axis_size("gy") - 1)]
    CX, CY = neutral_wind.shape[1:3]
    edge_t = (sd((2, 1, CY, 128), f32),)*2 + (sd((2, CX, 1, 128), f32),)*2
    side_t = (sd((256, 128), i32), sd((128, 256), i32), sd((128, 256), i32), sd((32, 128), i32))

    cA, pA, iA, bA, xa, xb, ya, yb = call(
        tile_sort_kernel, side_t + edge_t, [], outgoing_column, send_level, neutral_wind, smem=0, name="tilesort")
    wire = call(gather_kernel, wire_t, [vals], bA, cA, iA, neutral_wind.reshape(flat), name="first")
    came = exchange(wire)
    wire, tub, xa, xb = tied(wire, recv_tube, xa, xb)
    cB, pB, iB, bB, gain, drift = call(
        tube_sort_kernel, side_t + (sd((128, 256), f32), sd((128, 128), f32)), [],
        tub, recv_point, recv_weight, pair_count, drift_fraction[None, :], smem=0, name="tubesort")
    halo = beside("gx", xa, xb)
    came, *halo = tied(came, *halo)

    def tubes(came, ions, last):
        w, smooth, out_last = call(
            tube_kernel, (tube_t, tube_t, sd((2, 1, 512), f32)), [vals, accs],
            bB, coupling, cB, pB, gain, drift, came, ions, inverse, smem=2, name="tube")
        up = lax.ppermute(out_last, "gy", up_route)
        return call(
            lambda *a: drag_kernel(last, *a), (tube_t, wire_t), [tabs, vals],
            bB, drag_rate, cB, iB, gain, drift, w, smooth, up, ion_density, smem=2, name="drag")

    n1, wire = tubes(came, ion_density, False)
    came = exchange(wire)
    wire, ya, yb = tied(wire, ya, yb)
    halo += beside("gy", ya, yb)
    mid, wire, xa, xb, ya, yb = call(
        mid_kernel, (sd(flat, f32), wire_t) + edge_t, [vals, accs, vals],
        bA, cA, pA, iA, came, neutral_wind, forcing, visc, *halo, name="mid")
    mid = mid.reshape(neutral_wind.shape)
    came = exchange(wire)
    halo = beside("gx", xa, xb)
    came, *halo = tied(came, *halo)
    ion_out, wire = tubes(came, n1, True)
    came = exchange(wire)
    wire, ya, yb = tied(wire, ya, yb)
    halo += beside("gy", ya, yb)
    wind_out = call(
        end_kernel, sd(neutral_wind.shape, f32), [vals, accs],
        bA, cA, pA, came, neutral_wind, mid, forcing, visc, *halo, name="end")
    return (wind_out, ion_out)


def solution(mesh):
    placed = (
        P(None, "gx", "gy", None),
        P(None, "gx", "gy", None),
        P(None, ("gx", "gy"), None),
        P("gx", None, None, None),
        P(("gx", "gy")),
        P(),
        P(),
        P(),
        P(("gx", "gy"), None, None),
        P(("gx", "gy"), None, None),
        P(("gx", "gy"), None, None),
        P(("gx", "gy"), None, None),
        P(("gx", "gy"), None, None),
        P(),
    )
    return jax.shard_map(
        per_device,
        mesh=mesh,
        in_specs=placed,
        out_specs=(P(None, "gx", "gy", None), P(None, ("gx", "gy"), None)),
        check_vma=False,
    )
```

```python
import jax
import jax.numpy as jnp
from jax import lax
from jax.experimental import pallas as pl
from jax.experimental.pallas import tpu as pltpu
from jax.sharding import PartitionSpec as P

i32, f32, bf16 = jnp.int32, jnp.float32, jnp.bfloat16
VM = pl.BlockSpec(memory_space=pltpu.VMEM)
SM = pl.BlockSpec(memory_space=pltpu.SMEM)
W, NB = 64, 16
neutral_step = 0.4
ion_factor = 0.5


def bitonic(x):
    n, L = x.shape
    x = x.reshape(n//8, 8, L)
    sub = lax.broadcasted_iota(i32, (1, 8, L), 1)
    k = 2
    while k <= n:
        d = k//2
        while d >= 1:
            if d >= 8:
                dv = d//8
                y = x.reshape(n//(16*dv), 2, dv, 8, L)
                a, b = y[:, 0], y[:, 1]
                lo, hi = jnp.minimum(a, b), jnp.maximum(a, b)
                parts = []
                for g in range(n//(16*dv)):
                    up = ((g*2*d) & k) == 0
                    parts += [lo[g], hi[g]] if up else [hi[g], lo[g]]
                x = jnp.concatenate(parts, axis=0)
            else:
                up_r = pltpu.roll(x, 8-d, 1)
                dn_r = pltpu.roll(x, d, 1)
                first = (sub & d) == 0
                p = jnp.where(first, up_r, dn_r)
                mn, mx = jnp.minimum(x, p), jnp.maximum(x, p)
                if k >= 8:
                    if k == 8:
                        vi = lax.broadcasted_iota(i32, (n//8, 1, 1), 0)
                    parts = []
                    xs = []
                    take_min_up = first
                    kv = k//8
                    for g in range(0, n//8, kv):
                        up = (g*8 & k) == 0
                        sel = first if up else jnp.logical_not(first)
                        xs.append(jnp.where(sel, mn[g:g+kv], mx[g:g+kv]))
                    x = jnp.concatenate(xs, axis=0) if len(xs) > 1 else xs[0]
                else:
                    up = (sub & k) == 0
                    sel = first == up
                    x = jnp.where(sel, mn, mx)
            d //= 2
        k *= 2
    return x.reshape(n, L)

def take(x, idx):
    return jnp.take_along_axis(x, idx, axis=1, mode="promise_in_bounds")


def take2(x, idx):
    low = idx & 127
    return jnp.where(idx < 128, take(x[:, :128], low), take(x[:, 128:], low))


def slot_keys(order, first, turn, slots):
    lane = lax.broadcasted_iota(i32, (128, 128), 1)
    for j in range(8):
        idx = take(first[...], 8*j + (lane >> 4)) + 16*turn + (lane & 15)
        slots[j*128:(j+1)*128, :] = (take2(order, jnp.minimum(idx, 255)) & 1023).T


def sort_side(key16, cell_ref, pos_ref, bnd_ref, slot_ref, order_ref, first_ref, place_ref, ctl_ref):
    P, C = key16.shape
    c = lax.broadcasted_iota(i32, (P, C), 1)
    s = bitonic((key16 * 256 + c).T)
    cell = s >> 8
    cell_ref[...] = cell
    pos = (s & 255).T
    pos_ref[...] = pos
    row = (cell >> 7).reshape(C//8, 8, P)
    lo = jnp.min(jnp.min(row, axis=1), axis=1, keepdims=True)
    hi = jnp.max(jnp.max(row, axis=1), axis=1, keepdims=True)
    lane = lax.broadcasted_iota(i32, (C//8, 128), 1)
    bnd_ref[...] = jnp.where(lane == 0, lo, hi)
    tall = cell.reshape(C//8, 8, P)
    below = []
    for b in range(64):
        n = jnp.sum(jnp.where(tall < b*1024, 1.0, 0.0), axis=0)
        below.append(jnp.sum(n, axis=0, keepdims=True))
    full = jnp.full((64, P), float(C), f32)
    below = jnp.concatenate(below + [full], axis=0)
    most = jnp.max(pltpu.roll(below, 127, 0)[:64] - below[:64], axis=1, keepdims=True)
    most = jnp.max(jnp.broadcast_to(most, (64, 128)).reshape(8, 8, 128), axis=1)
    top = jnp.max(most, axis=0, keepdims=True)
    ctl_ref[...] = jnp.where(lane[:8] == 0, most, jnp.broadcast_to(top, (8, 128))).astype(i32)
    first = below.T.astype(i32)
    first_ref[...] = first
    order = cell.T
    order_ref[...] = order
    slot_keys(order, first_ref, 0, slot_ref)
    b = order >> 10
    w = c - jnp.concatenate([take(first, b[:, :128]), take(first, b[:, 128:])], axis=1)
    place = (pos << 14) + ((w >> 4) << 10) + (b << 4) + (w & 15)
    place_ref[...] = (bitonic(place.T) & 16383).T


def cell_key(row, lane):
    return ((row & 255) << 8) + ((row >> 8) << 7) + lane


def put_edges(get, xa, xb, ya, yb):
    for k in range(2):
        xa[k, 0] = get(k, 0)
        n = ya.shape[1]
        xb[k, 0] = get(k, n-1)
        for i in range(n):
            u = get(k, i)
            ya[k, i] = u[:1]
            yb[k, i] = u[-1:]


def tile_sort_kernel(col, lev, wind, *outs):
    side, edge = outs[:8], outs[8:]
    sort_side(cell_key(col[0], lev[0]), *side)
    put_edges(lambda k, i: wind[k, i], *edge)


def tube_sort_kernel(tub, pnt, weight, count, drift, *outs):
    side, gain, drift_out = outs[:8], outs[8], outs[9]
    p = pnt[0]
    sort_side(cell_key((p >> 7)*128 + tub[0], p & 127), *side)
    own = lax.axis_index("gx") * lax.axis_size("gy") + lax.axis_index("gy")
    lane = lax.broadcasted_iota(i32, (128, 128), 1)
    live = jnp.sum(jnp.where(lane == own, count[...], 0).astype(f32), axis=1, keepdims=True)
    c = lax.broadcasted_iota(i32, (128, 256), 1).astype(f32)
    gain[...] = jnp.where(c < live, weight[0], 0.0)
    drift_out[...] = jnp.broadcast_to(drift[...], (128, 128)).T


def permute_lanes(x, idx):
    return [take2(x, idx[:, :128]), take2(x, idx[:, 128:])]


def lookup(ctl, slot, order, first, place, t_ref, wire, s_ref, key_ref, gain=None):
    half = t_ref.shape[1] // 2
    key_ref[...] = slot[...]

    def turn(t, _):
        @pl.when(t > 0)
        def _():
            slot_keys(order[...], first, t, key_ref)

        def group(g, _):
            @pl.when(ctl[g, 0] > 16*t)
            def _():
                for b in range(8):
                    rows = []
                    for j in range(8):
                        at = g*32 + 4*b + j//2 + (j % 2)*half
                        rows.append([jnp.broadcast_to(t_ref[k, pl.ds(at, 1), :], (8, 128)) for k in range(2)])
                    for i in range(2):
                        sl = pl.ds(pl.multiple_of(g*128 + b*16 + i*8, 8), 8)
                        key = key_ref[sl, :]
                        sub, lev = key >> 7, key & 127
                        acc = [take(rows[0][k], lev) for k in range(2)]
                        for j in range(1, 8):
                            m = sub == j
                            for k in range(2):
                                acc[k] = jnp.where(m, take(rows[j][k], lev), acc[k])
                        for k in range(2):
                            s_ref[k, sl, :] = acc[k]
            return 0

        lax.fori_loop(0, 8, group, 0)
        parts = [[s_ref[k, j*128:(j+1)*128, :].T for j in range(8)] for k in range(2)]
        for h in range(2):
            at = place[:, h*128:(h+1)*128]
            low, tile, mine = at & 127, (at >> 7) & 7, (at >> 10) == t
            for k in range(2):
                x = take(parts[k][0], low)
                for j in range(1, 8):
                    x = jnp.where(tile == j, take(parts[k][j], low), x)
                if gain is not None:
                    x = x * gain[:, h*128:(h+1)*128]
                wire[:, 2*k+h, :] = jnp.where(mine, x, wire[:, 2*k+h, :])
        return 0

    lax.fori_loop(0, (ctl[0, 1] + 15) // 16, turn, 0)


def scatter_add(bnd, cell_ref, val_ref, acc_ref):
    acc_ref[...] = jnp.zeros_like(acc_ref)
    iota = lax.broadcasted_iota(i32, (256, 128), 0).astype(f32).astype(bf16)
    one, zero = jnp.ones((256, 128), bf16), jnp.zeros((256, 128), bf16)

    def spread(x, n):
        return jnp.broadcast_to(x, (n, 128)).astype(bf16)

    def block(v, _):
        sl = pl.ds(pl.multiple_of(v*NB, 8), NB)
        key = cell_ref[sl, :]
        q, lane = key >> 8, (key & 255).astype(f32)
        lo, hi = bnd[v*(NB//8), 0] >> 1, bnd[(v+1)*(NB//8) - 1, 1] >> 1
        base = (lo // 8) * 8
        vals = []
        for k in range(2):
            x = val_ref[k, sl, :]
            h = x.astype(bf16).astype(f32)
            vals += [h, x - h]
        lanes = jnp.concatenate([jnp.where(iota == spread(lane[r:r+1], 256), one, zero) for r in range(NB)], axis=1)

        def window(it, _):
            rb = pl.multiple_of(base + it*W, 8)
            rel = (q - rb).astype(f32)
            rows = []
            for r in range(NB):
                m = iota[:W] == spread(rel[r:r+1], W)
                rows.append(jnp.concatenate([jnp.where(m, spread(x[r:r+1], W), zero[:W]) for x in vals], axis=0))
            z = lax.dot_general(jnp.concatenate(rows, axis=1), lanes, (((1,), (1,)), ((), ())), preferred_element_type=f32)
            for k in range(2):
                acc_ref[k, pl.ds(rb, W), :] += z[2*k*W:(2*k+1)*W] + z[(2*k+1)*W:(2*k+2)*W]
            return 0

        lax.fori_loop(0, (hi - base)//W + 1, window, 0)
        return 0

    lax.fori_loop(0, 256//NB, block, 0)


def from_wire(pos, wire, val, gain=None):
    for k in range(2):
        x = [wire[:, 2*k+h, :] for h in range(2)]
        if gain is not None:
            x = [x[h] * gain[:, h*128:(h+1)*128] for h in range(2)]
        o = permute_lanes(jnp.concatenate(x, axis=1), pos[...])
        val[k, :128, :] = o[0].T
        val[k, 128:, :] = o[1].T


def gather_kernel(ctl, slot, order, first, place, t, wire, s, keys):
    lookup(ctl, slot, order, first, place, t, wire, s, keys)


def tube_kernel(bnd, coupling, cell, pos, gain, drift, wire, ions, inverse, w_out, smooth_out, last_out, val, acc):
    from_wire(pos, wire, val, gain)
    scatter_add(bnd, cell, val, acc)
    w = []
    for k in range(2):
        for j in range(4):
            w_out[k, :, j*128:(j+1)*128] = acc[k, (j%2)*128:(j%2+1)*128, (j//2)*128:(j//2+1)*128]
    for k in range(2):
        n = ions[k]
        growth = coupling[k, 0] * w_out[0] + coupling[k, 1] * w_out[1]
        rhs = n + ion_factor * n * growth
        mix = lax.dot_general(rhs.astype(bf16), inverse[0, k], (((1,), (0,)), ((), ())), preferred_element_type=f32)
        sm = rhs + mix
        smooth_out[k] = sm
        last_out[k] = drift[127:128, :1] * sm[127:128, :]


def drag_kernel(last, ctl, drag, slot, order, first_at, place, gain, drift, w, smooth, up, ions, n_out, wire, t, s, keys):
    first = lax.broadcasted_iota(i32, (128, 128), 0) == 0
    d = drift[...]
    n = [[], []]
    for k in range(2):
        for j in range(4):
            sl = slice(j*128, (j+1)*128)
            sm = smooth[k, :, sl]
            out = d * sm
            inflow = jnp.where(first, jnp.broadcast_to(up[k, :, sl], (128, 128)), pltpu.roll(out, 1, 0))
            x = sm - out + inflow
            n[k].append(x)
            n_out[k, :, sl] = 0.5 * (ions[k, :, sl] + x) if last else x
    for j in range(4):
        f = -(drag[0] * n[0][j] + drag[1] * n[1][j])
        for k in range(2):
            t[k, j*128:(j+1)*128, :] = f * w[k, :, j*128:(j+1)*128]
    lookup(ctl, slot, order, first_at, place, t, wire, s, keys, gain)


def tend_all(wind, forcing, visc, xlo, xhi, ylo, yhi, acc, emit):
    CX, CY = wind.shape[1], wind.shape[2]
    sub = lax.broadcasted_iota(i32, (CY, 128), 0)
    lane = lax.broadcasted_iota(i32, (CY, 128), 1)
    v = jnp.broadcast_to(visc[...], (CY, 128))
    for k in range(2):
        for i in range(CX):
            u = wind[k, i]
            b = (wind[k, i+1] if i < CX-1 else xhi[k, 0]) + (wind[k, i-1] if i > 0 else xlo[k, 0])
            nxt = jnp.where(sub == CY-1, jnp.broadcast_to(yhi[k, i], (CY, 128)), pltpu.roll(u, CY-1, 0))
            prv = jnp.where(sub == 0, jnp.broadcast_to(ylo[k, i], (CY, 128)), pltpu.roll(u, 1, 0))
            b = b + nxt + prv
            b = b + jnp.where(lane == 127, 0.0, pltpu.roll(u, 127, 1)) + jnp.where(lane == 0, 0.0, pltpu.roll(u, 1, 1))
            emit(k, i, u, v * (b - 6.0 * u) + acc[k, (i*CY) % 256:(i*CY) % 256 + CY, (i*CY)//256*128:(i*CY)//256*128 + 128] + forcing[k, i])


def mid_kernel(bnd, ctl, cell, pos, slot, order, first, place, wire, wind, forcing, visc, xlo, xhi, ylo, yhi, mid, wire_out, xa, xb, ya, yb, val, acc, s, keys):
    from_wire(pos, wire, val)
    scatter_add(bnd, cell, val, acc)
    CY = wind.shape[2]

    def emit(k, i, u, f):
        mid[k, i*CY:(i+1)*CY, :] = u + neutral_step * f

    tend_all(wind, forcing, visc, xlo, xhi, ylo, yhi, acc, emit)
    put_edges(lambda k, i: mid[k, i*CY:(i+1)*CY, :], xa, xb, ya, yb)
    lookup(ctl, slot, order, first, place, mid, wire_out, s, keys)


def end_kernel(bnd, cell, pos, wire, start, wind, forcing, visc, xlo, xhi, ylo, yhi, out, val, acc):
    from_wire(pos, wire, val)
    scatter_add(bnd, cell, val, acc)

    def emit(k, i, u, f):
        out[k, i] = 0.5 * (start[k, i] + u) + (0.5 * neutral_step) * f

    tend_all(wind, forcing, visc, xlo, xhi, ylo, yhi, acc, emit)


def call(kernel, outs, scratch, *args, smem=1, name=None):
    return pl.pallas_call(
        kernel,
        out_shape=outs,
        in_specs=[SM] * smem + [VM] * (len(args) - smem),
        out_specs=jax.tree.map(lambda _: VM, outs),
        scratch_shapes=scratch,
        name=name,
    )(*args)


def beside(axis, first, last):
    peers = lax.axis_size(axis)
    up = [(i, i + 1) for i in range(peers - 1)]
    return [lax.ppermute(last, axis, up), lax.ppermute(first, axis, [(b, a) for a, b in up])]


def tied(*arrays):
    return lax.optimization_barrier(arrays)


def exchange(x):
    return lax.all_to_all(x, ("gx", "gy"), split_axis=0, concat_axis=0, tiled=True)


def per_device(
    neutral_wind,
    forcing,
    ion_density,
    inverse,
    drift_fraction,
    viscosity,
    coupling,
    drag_rate,
    outgoing_column,
    send_level,
    recv_tube,
    recv_point,
    recv_weight,
    pair_count,
):
    visc = viscosity[None, :]
    sd = jax.ShapeDtypeStruct
    wire_t = sd((128, 4, 128), f32)
    tube_t = sd(ion_density.shape, f32)
    vals = pltpu.VMEM((2, 256, 128), f32)
    accs = pltpu.VMEM((2, 256 + W, 256), f32)
    tabs = pltpu.VMEM((2, 512, 128), f32)
    flat = (2, 512, 128)
    up_route = [(i, i + 1) for i in range(lax.axis_size("gy") - 1)]
    CX, CY = neutral_wind.shape[1:3]
    edge_t = (sd((2, 1, CY, 128), f32),)*2 + (sd((2, CX, 1, 128), f32),)*2
    side_t = (sd((256, 128), i32), sd((128, 256), i32), sd((32, 128), i32), sd((1024, 128), i32))
    side_t += (sd((128, 256), i32), sd((128, 128), i32), sd((128, 256), i32), sd((8, 128), i32))
    seek = [pltpu.VMEM((2, 1024, 128), f32), pltpu.VMEM((1024, 128), i32)]

    cA, pA, bA, *gA, ctA, xa, xb, ya, yb = call(
        tile_sort_kernel, side_t + edge_t, [], outgoing_column, send_level, neutral_wind, smem=0, name="tilesort")
    wire = call(gather_kernel, wire_t, seek, ctA, *gA, neutral_wind.reshape(flat), name="first")
    came = exchange(wire)
    wire, tub, xa, xb = tied(wire, recv_tube, xa, xb)
    cB, pB, bB, *gB, ctB, gain, drift = call(
        tube_sort_kernel, side_t + (sd((128, 256), f32), sd((128, 128), f32)), [],
        tub, recv_point, recv_weight, pair_count, drift_fraction[None, :], smem=0, name="tubesort")
    halo = beside("gx", xa, xb)
    came, *halo = tied(came, *halo)

    def tubes(came, ions, last):
        w, smooth, out_last = call(
            tube_kernel, (tube_t, tube_t, sd((2, 1, 512), f32)), [vals, accs],
            bB, coupling, cB, pB, gain, drift, came, ions, inverse, smem=2, name="tube")
        up = lax.ppermute(out_last, "gy", up_route)
        return call(
            lambda *a: drag_kernel(last, *a), (tube_t, wire_t), [tabs] + seek,
            ctB, drag_rate, *gB, gain, drift, w, smooth, up, ion_density, smem=2, name="drag")

    n1, wire = tubes(came, ion_density, False)
    came = exchange(wire)
    wire, ya, yb = tied(wire, ya, yb)
    halo += beside("gy", ya, yb)
    mid, wire, xa, xb, ya, yb = call(
        mid_kernel, (sd(flat, f32), wire_t) + edge_t, [vals, accs] + seek,
        bA, ctA, cA, pA, *gA, came, neutral_wind, forcing, visc, *halo, smem=2, name="mid")
    mid = mid.reshape(neutral_wind.shape)
    came = exchange(wire)
    halo = beside("gx", xa, xb)
    came, *halo = tied(came, *halo)
    ion_out, wire = tubes(came, n1, True)
    came = exchange(wire)
    wire, ya, yb = tied(wire, ya, yb)
    halo += beside("gy", ya, yb)
    wind_out = call(
        end_kernel, sd(neutral_wind.shape, f32), [vals, accs],
        bA, cA, pA, came, neutral_wind, mid, forcing, visc, *halo, name="end")
    return (wind_out, ion_out)


def solution(mesh):
    placed = (
        P(None, "gx", "gy", None),
        P(None, "gx", "gy", None),
        P(None, ("gx", "gy"), None),
        P("gx", None, None, None),
        P(("gx", "gy")),
        P(),
        P(),
        P(),
        P(("gx", "gy"), None, None),
        P(("gx", "gy"), None, None),
        P(("gx", "gy"), None, None),
        P(("gx", "gy"), None, None),
        P(("gx", "gy"), None, None),
        P(),
    )
    return jax.shard_map(
        per_device,
        mesh=mesh,
        in_specs=placed,
        out_specs=(P(None, "gx", "gy", None), P(None, ("gx", "gy"), None)),
        check_vma=False,
    )
```

```python
import jax
import jax.numpy as jnp
from jax import lax
from jax.experimental import pallas as pl
from jax.experimental.pallas import tpu as pltpu
from jax.sharding import PartitionSpec as P

i32, f32, bf16 = jnp.int32, jnp.float32, jnp.bfloat16
VM = pl.BlockSpec(memory_space=pltpu.VMEM)
SM = pl.BlockSpec(memory_space=pltpu.SMEM)
W, NB, UN = 80, 16, 2
neutral_step = 0.4
ion_factor = 0.5


def bitonic(x):
    n, L = x.shape
    x = x.reshape(n//8, 8, L)
    sub = lax.broadcasted_iota(i32, (1, 8, L), 1)
    k = 2
    while k <= n:
        d = k//2
        while d >= 1:
            if d >= 8:
                dv = d//8
                y = x.reshape(n//(16*dv), 2, dv, 8, L)
                a, b = y[:, 0], y[:, 1]
                lo, hi = jnp.minimum(a, b), jnp.maximum(a, b)
                parts = []
                for g in range(n//(16*dv)):
                    up = ((g*2*d) & k) == 0
                    parts += [lo[g], hi[g]] if up else [hi[g], lo[g]]
                x = jnp.concatenate(parts, axis=0)
            else:
                up_r = pltpu.roll(x, 8-d, 1)
                dn_r = pltpu.roll(x, d, 1)
                first = (sub & d) == 0
                p = jnp.where(first, up_r, dn_r)
                mn, mx = jnp.minimum(x, p), jnp.maximum(x, p)
                if k >= 8:
                    if k == 8:
                        vi = lax.broadcasted_iota(i32, (n//8, 1, 1), 0)
                    parts = []
                    xs = []
                    take_min_up = first
                    kv = k//8
                    for g in range(0, n//8, kv):
                        up = (g*8 & k) == 0
                        sel = first if up else jnp.logical_not(first)
                        xs.append(jnp.where(sel, mn[g:g+kv], mx[g:g+kv]))
                    x = jnp.concatenate(xs, axis=0) if len(xs) > 1 else xs[0]
                else:
                    up = (sub & k) == 0
                    sel = first == up
                    x = jnp.where(sel, mn, mx)
            d //= 2
        k *= 2
    return x.reshape(n, L)

def take(x, idx):
    return jnp.take_along_axis(x, idx, axis=1, mode="promise_in_bounds")


def take2(x, idx):
    low = idx & 127
    return jnp.where(idx < 128, take(x[:, :128], low), take(x[:, 128:], low))


def slot_tile(order, first, turn, j, slots):
    lane = lax.broadcasted_iota(i32, (128, 128), 1)
    idx = take(first[...], 8*j + (lane >> 4)) + 16*turn + (lane & 15)
    slots[pl.ds(pl.multiple_of(j*128, 128), 128), :] = (take2(order, jnp.minimum(idx, 255)) & 1023).T


def sort_side(key16, cell_ref, pos_ref, bnd_ref, slot_ref, order_ref, first_ref, place_ref, ctl_ref):
    P, C = key16.shape
    c = lax.broadcasted_iota(i32, (P, C), 1)
    s = bitonic((key16 * 256 + c).T)
    cell = s >> 8
    cell_ref[...] = cell
    pos = (s & 255).T
    pos_ref[...] = pos
    row = (cell >> 7).reshape(C//8, 8, P)
    lo = jnp.min(jnp.min(row, axis=1), axis=1, keepdims=True)
    hi = jnp.max(jnp.max(row, axis=1), axis=1, keepdims=True)
    lane = lax.broadcasted_iota(i32, (C//8, 128), 1)
    bnd_ref[...] = jnp.where(lane == 0, lo, hi)
    tall = cell.reshape(C//8, 8, P)
    below = []
    for b in range(64):
        n = jnp.sum(jnp.where(tall < b*1024, 1.0, 0.0), axis=0)
        below.append(jnp.sum(n, axis=0, keepdims=True))
    full = jnp.full((64, P), float(C), f32)
    below = jnp.concatenate(below + [full], axis=0)
    most = jnp.max(pltpu.roll(below, 127, 0)[:64] - below[:64], axis=1, keepdims=True)
    most = jnp.max(jnp.broadcast_to(most, (64, 128)).reshape(8, 8, 128), axis=1)
    top = jnp.max(most, axis=0, keepdims=True)
    ctl_ref[...] = jnp.where(lane[:8] == 0, most, jnp.broadcast_to(top, (8, 128))).astype(i32)
    first = below.T.astype(i32)
    first_ref[...] = first
    order = cell.T
    order_ref[...] = order
    for j in range(8):
        slot_tile(order, first_ref, 0, j, slot_ref)
    b = order >> 10
    w = c - jnp.concatenate([take(first, b[:, :128]), take(first, b[:, 128:])], axis=1)
    place = (pos << 14) + ((w >> 4) << 10) + (b << 4) + (w & 15)
    place_ref[...] = (bitonic(place.T) & 16383).T


def cell_key(row, lane):
    return ((row & 255) << 8) + ((row >> 8) << 7) + lane


def put_edges(get, xa, xb, ya, yb):
    for k in range(2):
        xa[k, 0] = get(k, 0)
        n = ya.shape[1]
        xb[k, 0] = get(k, n-1)
        for i in range(n):
            u = get(k, i)
            ya[k, i] = u[:1]
            yb[k, i] = u[-1:]


def tile_sort_kernel(col, lev, wind, *outs):
    side, edge = outs[:8], outs[8:]
    sort_side(cell_key(col[0], lev[0]), *side)
    put_edges(lambda k, i: wind[k, i], *edge)


def tube_sort_kernel(tub, pnt, weight, count, drift, *outs):
    side, gain, drift_out = outs[:8], outs[8], outs[9]
    p = pnt[0]
    sort_side(cell_key((p >> 7)*128 + tub[0], p & 127), *side)
    own = lax.axis_index("gx") * lax.axis_size("gy") + lax.axis_index("gy")
    lane = lax.broadcasted_iota(i32, (128, 128), 1)
    live = jnp.sum(jnp.where(lane == own, count[...], 0).astype(f32), axis=1, keepdims=True)
    c = lax.broadcasted_iota(i32, (128, 256), 1).astype(f32)
    gain[...] = jnp.where(c < live, weight[0], 0.0)
    drift_out[...] = jnp.broadcast_to(drift[...], (128, 128)).T


def permute_lanes(x, idx):
    return [take2(x, idx[:, :128]), take2(x, idx[:, 128:])]


def lookup(ctl, slot, order, first, place, t_ref, wire, s_ref, key_ref, gain=None):
    half = t_ref.shape[1] // 2

    def group(g, keys):
        for b in range(8):
            rows = []
            for j in range(8):
                at = g*32 + 4*b + j//2 + (j % 2)*half
                rows.append([jnp.broadcast_to(t_ref[k, pl.ds(at, 1), :], (8, 128)) for k in range(2)])
            for i in range(2):
                sl = pl.ds(pl.multiple_of(g*128 + b*16 + i*8, 8), 8)
                key = keys[sl, :]
                sub, lev = key >> 7, key & 127
                acc = [take(rows[0][k], lev) for k in range(2)]
                for j in range(1, 8):
                    m = sub == j
                    for k in range(2):
                        acc[k] = jnp.where(m, take(rows[j][k], lev), acc[k])
                for k in range(2):
                    s_ref[k, sl, :] = acc[k]

    def each(g, _):
        group(g, slot)
        return 0

    def scaled(x, h):
        return x if gain is None else x * gain[:, h*128:(h+1)*128]

    lax.fori_loop(0, 8, each, 0)
    parts = [[s_ref[k, j*128:(j+1)*128, :].T for j in range(8)] for k in range(2)]
    for h in range(2):
        at = place[:, h*128:(h+1)*128]
        low, tile = at & 127, (at >> 7) & 7
        for k in range(2):
            x = take(parts[k][0], low)
            for j in range(1, 8):
                x = jnp.where(tile == j, take(parts[k][j], low), x)
            wire[:, 2*k+h, :] = scaled(x, h)

    def turn(t, _):
        def late(g, _):
            @pl.when(ctl[g, 0] > 16*t)
            def _():
                slot_tile(order[...], first, t, g, key_ref)
                group(g, key_ref)
                tile = pl.ds(pl.multiple_of(g*128, 128), 128)
                for h in range(2):
                    at = place[:, h*128:(h+1)*128]
                    mine = (at >> 7) == 8*t + g
                    for k in range(2):
                        x = take(s_ref[k, tile, :].T, at & 127)
                        wire[:, 2*k+h, :] = jnp.where(mine, scaled(x, h), wire[:, 2*k+h, :])
            return 0

        lax.fori_loop(0, 8, late, 0)
        return 0

    lax.fori_loop(1, (ctl[0, 1] + 15) // 16, turn, 0)


def scatter_add(bnd, cell_ref, val_ref, acc_ref):
    acc_ref[...] = jnp.zeros_like(acc_ref)
    iota = lax.broadcasted_iota(i32, (256, 128), 0).astype(f32).astype(bf16)
    one, zero = jnp.ones((256, 128), bf16), jnp.zeros((256, 128), bf16)

    def spread(x, n):
        return jnp.broadcast_to(x, (n, 128)).astype(bf16)

    def begin(v):
        return ((bnd[v*(NB//8), 0] >> 1) // 8) * 8

    def window(v, rb):
        rb = pl.multiple_of(rb, 8)
        sl = pl.ds(pl.multiple_of(v*NB, 8), NB)
        key = cell_ref[sl, :]
        rel, lane = ((key >> 8) - rb).astype(f32), (key & 255).astype(f32)
        vals = []
        for k in range(2):
            x = val_ref[k, sl, :]
            h = x.astype(bf16).astype(f32)
            vals += [h, x - h]
        rows, lanes = [], []
        for r in range(NB):
            lanes.append(jnp.where(iota == spread(lane[r:r+1], 256), one, zero))
            m = iota[:W] == spread(rel[r:r+1], W)
            rows.append(jnp.concatenate([jnp.where(m, spread(x[r:r+1], W), zero[:W]) for x in vals], axis=0))
        z = lax.dot_general(
            jnp.concatenate(rows, axis=1), jnp.concatenate(lanes, axis=1),
            (((1,), (1,)), ((), ())), preferred_element_type=f32)
        for k in range(2):
            acc_ref[k, pl.ds(rb, W), :] += z[2*k*W:(2*k+1)*W] + z[(2*k+1)*W:(2*k+2)*W]

    def block(v, _):
        window(v, begin(v))
        return 0

    def rest(v, _):
        base = begin(v)

        def more(it, _):
            window(v, base + it*W)
            return 0

        return lax.fori_loop(1, ((bnd[(v+1)*(NB//8) - 1, 1] >> 1) - base)//W + 1, more, 0)

    lax.fori_loop(0, 256//NB, block, 0, unroll=UN)
    lax.fori_loop(0, 256//NB, rest, 0)


def from_wire(pos, wire, val, gain=None):
    for k in range(2):
        x = [wire[:, 2*k+h, :] for h in range(2)]
        if gain is not None:
            x = [x[h] * gain[:, h*128:(h+1)*128] for h in range(2)]
        o = permute_lanes(jnp.concatenate(x, axis=1), pos[...])
        val[k, :128, :] = o[0].T
        val[k, 128:, :] = o[1].T


def gather_kernel(ctl, slot, order, first, place, t, wire, s, keys):
    lookup(ctl, slot, order, first, place, t, wire, s, keys)


def tube_kernel(bnd, coupling, cell, pos, gain, drift, wire, ions, inverse, w_out, smooth_out, last_out, val, acc):
    from_wire(pos, wire, val, gain)
    scatter_add(bnd, cell, val, acc)
    w = []
    for k in range(2):
        for j in range(4):
            w_out[k, :, j*128:(j+1)*128] = acc[k, (j%2)*128:(j%2+1)*128, (j//2)*128:(j//2+1)*128]
    for k in range(2):
        n = ions[k]
        growth = coupling[k, 0] * w_out[0] + coupling[k, 1] * w_out[1]
        rhs = n + ion_factor * n * growth
        mix = lax.dot_general(rhs.astype(bf16), inverse[0, k], (((1,), (0,)), ((), ())), preferred_element_type=f32)
        sm = rhs + mix
        smooth_out[k] = sm
        last_out[k] = drift[127:128, :1] * sm[127:128, :]


def drag_kernel(last, ctl, drag, slot, order, first_at, place, gain, drift, w, smooth, up, ions, n_out, wire, t, s, keys):
    first = lax.broadcasted_iota(i32, (128, 128), 0) == 0
    d = drift[...]
    n = [[], []]
    for k in range(2):
        for j in range(4):
            sl = slice(j*128, (j+1)*128)
            sm = smooth[k, :, sl]
            out = d * sm
            inflow = jnp.where(first, jnp.broadcast_to(up[k, :, sl], (128, 128)), pltpu.roll(out, 1, 0))
            x = sm - out + inflow
            n[k].append(x)
            n_out[k, :, sl] = 0.5 * (ions[k, :, sl] + x) if last else x
    for j in range(4):
        f = -(drag[0] * n[0][j] + drag[1] * n[1][j])
        for k in range(2):
            t[k, j*128:(j+1)*128, :] = f * w[k, :, j*128:(j+1)*128]
    lookup(ctl, slot, order, first_at, place, t, wire, s, keys, gain)


def tend_all(wind, forcing, visc, xlo, xhi, ylo, yhi, acc, emit):
    CX, CY = wind.shape[1], wind.shape[2]
    sub = lax.broadcasted_iota(i32, (CY, 128), 0)
    lane = lax.broadcasted_iota(i32, (CY, 128), 1)
    v = jnp.broadcast_to(visc[...], (CY, 128))
    for k in range(2):
        for i in range(CX):
            u = wind[k, i]
            b = (wind[k, i+1] if i < CX-1 else xhi[k, 0]) + (wind[k, i-1] if i > 0 else xlo[k, 0])
            nxt = jnp.where(sub == CY-1, jnp.broadcast_to(yhi[k, i], (CY, 128)), pltpu.roll(u, CY-1, 0))
            prv = jnp.where(sub == 0, jnp.broadcast_to(ylo[k, i], (CY, 128)), pltpu.roll(u, 1, 0))
            b = b + nxt + prv
            b = b + jnp.where(lane == 127, 0.0, pltpu.roll(u, 127, 1)) + jnp.where(lane == 0, 0.0, pltpu.roll(u, 1, 1))
            emit(k, i, u, v * (b - 6.0 * u) + acc[k, (i*CY) % 256:(i*CY) % 256 + CY, (i*CY)//256*128:(i*CY)//256*128 + 128] + forcing[k, i])


def mid_kernel(bnd, ctl, cell, pos, slot, order, first, place, wire, wind, forcing, visc, xlo, xhi, ylo, yhi, mid, wire_out, xa, xb, ya, yb, val, acc, s, keys):
    from_wire(pos, wire, val)
    scatter_add(bnd, cell, val, acc)
    CY = wind.shape[2]

    def emit(k, i, u, f):
        mid[k, i*CY:(i+1)*CY, :] = u + neutral_step * f

    tend_all(wind, forcing, visc, xlo, xhi, ylo, yhi, acc, emit)
    put_edges(lambda k, i: mid[k, i*CY:(i+1)*CY, :], xa, xb, ya, yb)
    lookup(ctl, slot, order, first, place, mid, wire_out, s, keys)


def end_kernel(bnd, cell, pos, wire, start, wind, forcing, visc, xlo, xhi, ylo, yhi, out, val, acc):
    from_wire(pos, wire, val)
    scatter_add(bnd, cell, val, acc)

    def emit(k, i, u, f):
        out[k, i] = 0.5 * (start[k, i] + u) + (0.5 * neutral_step) * f

    tend_all(wind, forcing, visc, xlo, xhi, ylo, yhi, acc, emit)


def call(kernel, outs, scratch, *args, smem=1, name=None):
    return pl.pallas_call(
        kernel,
        out_shape=outs,
        in_specs=[SM] * smem + [VM] * (len(args) - smem),
        out_specs=jax.tree.map(lambda _: VM, outs),
        scratch_shapes=scratch,
        name=name,
    )(*args)


def beside(axis, first, last):
    peers = lax.axis_size(axis)
    up = [(i, i + 1) for i in range(peers - 1)]
    return [lax.ppermute(last, axis, up), lax.ppermute(first, axis, [(b, a) for a, b in up])]


def tied(*arrays):
    return lax.optimization_barrier(arrays)


def exchange(x):
    return lax.all_to_all(x, ("gx", "gy"), split_axis=0, concat_axis=0, tiled=True)


def per_device(
    neutral_wind,
    forcing,
    ion_density,
    inverse,
    drift_fraction,
    viscosity,
    coupling,
    drag_rate,
    outgoing_column,
    send_level,
    recv_tube,
    recv_point,
    recv_weight,
    pair_count,
):
    visc = viscosity[None, :]
    sd = jax.ShapeDtypeStruct
    wire_t = sd((128, 4, 128), f32)
    tube_t = sd(ion_density.shape, f32)
    vals = pltpu.VMEM((2, 256, 128), f32)
    accs = pltpu.VMEM((2, 256 + W, 256), f32)
    tabs = pltpu.VMEM((2, 512, 128), f32)
    flat = (2, 512, 128)
    up_route = [(i, i + 1) for i in range(lax.axis_size("gy") - 1)]
    CX, CY = neutral_wind.shape[1:3]
    edge_t = (sd((2, 1, CY, 128), f32),)*2 + (sd((2, CX, 1, 128), f32),)*2
    side_t = (sd((256, 128), i32), sd((128, 256), i32), sd((32, 128), i32), sd((1024, 128), i32))
    side_t += (sd((128, 256), i32), sd((128, 128), i32), sd((128, 256), i32), sd((8, 128), i32))
    seek = [pltpu.VMEM((2, 1024, 128), f32), pltpu.VMEM((1024, 128), i32)]

    cA, pA, bA, *gA, ctA, xa, xb, ya, yb = call(
        tile_sort_kernel, side_t + edge_t, [], outgoing_column, send_level, neutral_wind, smem=0, name="tilesort")
    wire = call(gather_kernel, wire_t, seek, ctA, *gA, neutral_wind.reshape(flat), name="first")
    came = exchange(wire)
    wire, tub, xa, xb = tied(wire, recv_tube, xa, xb)
    cB, pB, bB, *gB, ctB, gain, drift = call(
        tube_sort_kernel, side_t + (sd((128, 256), f32), sd((128, 128), f32)), [],
        tub, recv_point, recv_weight, pair_count, drift_fraction[None, :], smem=0, name="tubesort")
    halo = beside("gx", xa, xb)
    came, *halo = tied(came, *halo)

    def tubes(came, ions, last):
        w, smooth, out_last = call(
            tube_kernel, (tube_t, tube_t, sd((2, 1, 512), f32)), [vals, accs],
            bB, coupling, cB, pB, gain, drift, came, ions, inverse, smem=2, name="tube")
        up = lax.ppermute(out_last, "gy", up_route)
        return call(
            lambda *a: drag_kernel(last, *a), (tube_t, wire_t), [tabs] + seek,
            ctB, drag_rate, *gB, gain, drift, w, smooth, up, ion_density, smem=2, name="drag")

    n1, wire = tubes(came, ion_density, False)
    came = exchange(wire)
    wire, ya, yb = tied(wire, ya, yb)
    halo += beside("gy", ya, yb)
    mid, wire, xa, xb, ya, yb = call(
        mid_kernel, (sd(flat, f32), wire_t) + edge_t, [vals, accs] + seek,
        bA, ctA, cA, pA, *gA, came, neutral_wind, forcing, visc, *halo, smem=2, name="mid")
    mid = mid.reshape(neutral_wind.shape)
    came = exchange(wire)
    halo = beside("gx", xa, xb)
    came, *halo = tied(came, *halo)
    ion_out, wire = tubes(came, n1, True)
    came = exchange(wire)
    wire, ya, yb = tied(wire, ya, yb)
    halo += beside("gy", ya, yb)
    wind_out = call(
        end_kernel, sd(neutral_wind.shape, f32), [vals, accs],
        bA, cA, pA, came, neutral_wind, mid, forcing, visc, *halo, name="end")
    return (wind_out, ion_out)


def solution(mesh):
    placed = (
        P(None, "gx", "gy", None),
        P(None, "gx", "gy", None),
        P(None, ("gx", "gy"), None),
        P("gx", None, None, None),
        P(("gx", "gy")),
        P(),
        P(),
        P(),
        P(("gx", "gy"), None, None),
        P(("gx", "gy"), None, None),
        P(("gx", "gy"), None, None),
        P(("gx", "gy"), None, None),
        P(("gx", "gy"), None, None),
        P(),
    )
    return jax.shard_map(
        per_device,
        mesh=mesh,
        in_specs=placed,
        out_specs=(P(None, "gx", "gy", None), P(None, ("gx", "gy"), None)),
        check_vma=False,
    )
```

```python
import jax
import jax.numpy as jnp
from jax import lax
from jax.experimental import pallas as pl
from jax.experimental.pallas import tpu as pltpu
from jax.sharding import PartitionSpec as P

i32, f32, bf16 = jnp.int32, jnp.float32, jnp.bfloat16
VM = pl.BlockSpec(memory_space=pltpu.VMEM)
SM = pl.BlockSpec(memory_space=pltpu.SMEM)
W, NB, UN = 80, 16, 2
neutral_step = 0.4
ion_factor = 0.5


def bitonic(x):
    n, L = x.shape
    x = x.reshape(n//8, 8, L)
    sub = lax.broadcasted_iota(i32, (1, 8, L), 1)
    k = 2
    while k <= n:
        d = k//2
        while d >= 1:
            if d >= 8:
                dv = d//8
                y = x.reshape(n//(16*dv), 2, dv, 8, L)
                a, b = y[:, 0], y[:, 1]
                lo, hi = jnp.minimum(a, b), jnp.maximum(a, b)
                parts = []
                for g in range(n//(16*dv)):
                    up = ((g*2*d) & k) == 0
                    parts += [lo[g], hi[g]] if up else [hi[g], lo[g]]
                x = jnp.concatenate(parts, axis=0)
            else:
                up_r = pltpu.roll(x, 8-d, 1)
                dn_r = pltpu.roll(x, d, 1)
                first = (sub & d) == 0
                p = jnp.where(first, up_r, dn_r)
                mn, mx = jnp.minimum(x, p), jnp.maximum(x, p)
                if k >= 8:
                    if k == 8:
                        vi = lax.broadcasted_iota(i32, (n//8, 1, 1), 0)
                    parts = []
                    xs = []
                    take_min_up = first
                    kv = k//8
                    for g in range(0, n//8, kv):
                        up = (g*8 & k) == 0
                        sel = first if up else jnp.logical_not(first)
                        xs.append(jnp.where(sel, mn[g:g+kv], mx[g:g+kv]))
                    x = jnp.concatenate(xs, axis=0) if len(xs) > 1 else xs[0]
                else:
                    up = (sub & k) == 0
                    sel = first == up
                    x = jnp.where(sel, mn, mx)
            d //= 2
        k *= 2
    return x.reshape(n, L)

def take(x, idx):
    return jnp.take_along_axis(x, idx, axis=1, mode="promise_in_bounds")


def take2(x, idx):
    low = idx & 127
    return jnp.where(idx < 128, take(x[:, :128], low), take(x[:, 128:], low))


def slot_tile(order, first, turn, j, slots):
    lane = lax.broadcasted_iota(i32, (128, 128), 1)
    idx = take(first[...], 8*j + (lane >> 4)) + 16*turn + (lane & 15)
    slots[pl.ds(pl.multiple_of(j*128, 128), 128), :] = (take2(order, jnp.minimum(idx, 255)) & 1023).T


def sort_side(key16, cell_ref, pos_ref, bnd_ref, slot_ref, order_ref, first_ref, place_ref, ctl_ref):
    P, C = key16.shape
    c = lax.broadcasted_iota(i32, (P, C), 1)
    s = bitonic((key16 * 256 + c).T)
    cell = s >> 8
    cell_ref[...] = cell
    pos = (s & 255).T
    pos_ref[...] = pos
    row = (cell >> 7).reshape(C//8, 8, P)
    lo = jnp.min(jnp.min(row, axis=1), axis=1, keepdims=True)
    hi = jnp.max(jnp.max(row, axis=1), axis=1, keepdims=True)
    lane = lax.broadcasted_iota(i32, (C//8, 128), 1)
    bnd_ref[...] = jnp.where(lane == 0, lo, hi)
    tall = cell.reshape(C//8, 8, P)
    below = []
    for b in range(64):
        n = jnp.sum(jnp.where(tall < b*1024, 1.0, 0.0), axis=0)
        below.append(jnp.sum(n, axis=0, keepdims=True))
    full = jnp.full((64, P), float(C), f32)
    below = jnp.concatenate(below + [full], axis=0)
    most = jnp.max(pltpu.roll(below, 127, 0)[:64] - below[:64], axis=1, keepdims=True)
    most = jnp.max(jnp.broadcast_to(most, (64, 128)).reshape(8, 8, 128), axis=1)
    top = jnp.max(most, axis=0, keepdims=True)
    ctl_ref[...] = jnp.where(lane[:8] == 0, most, jnp.broadcast_to(top, (8, 128))).astype(i32)
    first = below.T.astype(i32)
    first_ref[...] = first
    order = cell.T
    order_ref[...] = order
    for j in range(8):
        slot_tile(order, first_ref, 0, j, slot_ref)
    b = order >> 10
    w = c - jnp.concatenate([take(first, b[:, :128]), take(first, b[:, 128:])], axis=1)
    place = (pos << 14) + ((w >> 4) << 10) + (b << 4) + (w & 15)
    place_ref[...] = (bitonic(place.T) & 16383).T


def cell_key(row, lane):
    return ((row & 255) << 8) + ((row >> 8) << 7) + lane


def put_edges(t, wire):
    CX, CY = 16, t.shape[1] // 16
    for k in range(2):
        wire[k*CY:(k+1)*CY, 2, 0, :] = t[k, (CX-1)*CY:CX*CY, :]
        wire[(2+k)*CY:(3+k)*CY, 2, 0, :] = t[k, :CY, :]
        for i in range(CX):
            wire[k*CX+i:k*CX+i+1, 2, 1, :] = t[k, (i+1)*CY-1:(i+1)*CY, :]
            wire[(2+k)*CX+i:(2+k)*CX+i+1, 2, 1, :] = t[k, i*CY:i*CY+1, :]
    wire[4*CX:, 2, 1, :] = jnp.zeros((128 - 4*CX, 128), f32)


def place_of():
    x, y = lax.axis_index("gx"), lax.axis_index("gy")
    return x, y, x * lax.axis_size("gy") + y


def pass_edges(wire, out):
    q = place_of()[2]
    step = lax.axis_size("gy")
    for r, (cut, d) in enumerate(((64, step), (32, 1))):
        x = wire[:, 2, r, :]
        out[r] = jnp.where(q < cut, pltpu.roll(x, d, 0), pltpu.roll(x, 128-d, 0))


def beside_tile(wire):
    x, y = place_of()[:2]
    a, b = wire[:, 2, 0, :], wire[:64, 2, 1, :]
    return (
        jnp.where(x > 0, a[:64], 0.0),
        jnp.where(x < lax.axis_size("gx") - 1, a[64:], 0.0),
        jnp.where(y > 0, b[:32], 0.0),
        jnp.where(y < lax.axis_size("gy") - 1, b[32:], 0.0),
    )


def tile_sort_kernel(col, lev, *side):
    sort_side(cell_key(col[0], lev[0]), *side)


def tube_sort_kernel(tub, pnt, weight, count, drift, *outs):
    side, gain, drift_out = outs[:8], outs[8], outs[9]
    p = pnt[0]
    sort_side(cell_key((p >> 7)*128 + tub[0], p & 127), *side)
    own = place_of()[2]
    lane = lax.broadcasted_iota(i32, (128, 128), 1)
    live = jnp.sum(jnp.where(lane == own, count[...], 0).astype(f32), axis=1, keepdims=True)
    c = lax.broadcasted_iota(i32, (128, 256), 1).astype(f32)
    gain[...] = jnp.where(c < live, weight[0], 0.0)
    drift_out[...] = jnp.broadcast_to(drift[...], (128, 128)).T


def permute_lanes(x, idx):
    return [take2(x, idx[:, :128]), take2(x, idx[:, 128:])]


def lookup(ctl, slot, order, first, place, t_ref, wire, s_ref, key_ref, gain=None):
    half = t_ref.shape[1] // 2

    def group(g, keys):
        for b in range(8):
            rows = []
            for j in range(8):
                at = g*32 + 4*b + j//2 + (j % 2)*half
                rows.append([jnp.broadcast_to(t_ref[k, pl.ds(at, 1), :], (8, 128)) for k in range(2)])
            for i in range(2):
                sl = pl.ds(pl.multiple_of(g*128 + b*16 + i*8, 8), 8)
                key = keys[sl, :]
                sub, lev = key >> 7, key & 127
                acc = [take(rows[0][k], lev) for k in range(2)]
                for j in range(1, 8):
                    m = sub == j
                    for k in range(2):
                        acc[k] = jnp.where(m, take(rows[j][k], lev), acc[k])
                for k in range(2):
                    s_ref[k, sl, :] = acc[k]

    def each(g, _):
        group(g, slot)
        return 0

    def scaled(x, h):
        return x if gain is None else x * gain[:, h*128:(h+1)*128]

    lax.fori_loop(0, 8, each, 0)
    parts = [[s_ref[k, j*128:(j+1)*128, :].T for j in range(8)] for k in range(2)]
    for h in range(2):
        at = place[:, h*128:(h+1)*128]
        low, tile = at & 127, (at >> 7) & 7
        for k in range(2):
            x = take(parts[k][0], low)
            for j in range(1, 8):
                x = jnp.where(tile == j, take(parts[k][j], low), x)
            wire[:, k, h, :] = scaled(x, h)

    def turn(t, _):
        def late(g, _):
            @pl.when(ctl[g, 0] > 16*t)
            def _():
                slot_tile(order[...], first, t, g, key_ref)
                group(g, key_ref)
                tile = pl.ds(pl.multiple_of(g*128, 128), 128)
                for h in range(2):
                    at = place[:, h*128:(h+1)*128]
                    mine = (at >> 7) == 8*t + g
                    for k in range(2):
                        x = take(s_ref[k, tile, :].T, at & 127)
                        wire[:, k, h, :] = jnp.where(mine, scaled(x, h), wire[:, k, h, :])
            return 0

        lax.fori_loop(0, 8, late, 0)
        return 0

    lax.fori_loop(1, (ctl[0, 1] + 15) // 16, turn, 0)


def scatter_add(bnd, cell_ref, val_ref, acc_ref):
    acc_ref[...] = jnp.zeros_like(acc_ref)
    iota = lax.broadcasted_iota(i32, (256, 128), 0).astype(f32).astype(bf16)
    one, zero = jnp.ones((256, 128), bf16), jnp.zeros((256, 128), bf16)

    def spread(x, n):
        return jnp.broadcast_to(x, (n, 128)).astype(bf16)

    def begin(v):
        return ((bnd[v*(NB//8), 0] >> 1) // 8) * 8

    def window(v, rb):
        rb = pl.multiple_of(rb, 8)
        sl = pl.ds(pl.multiple_of(v*NB, 8), NB)
        key = cell_ref[sl, :]
        rel, lane = ((key >> 8) - rb).astype(f32), (key & 255).astype(f32)
        vals = []
        for k in range(2):
            x = val_ref[k, sl, :]
            h = x.astype(bf16).astype(f32)
            vals += [h, x - h]
        rows, lanes = [], []
        for r in range(NB):
            lanes.append(jnp.where(iota == spread(lane[r:r+1], 256), one, zero))
            m = iota[:W] == spread(rel[r:r+1], W)
            rows.append(jnp.concatenate([jnp.where(m, spread(x[r:r+1], W), zero[:W]) for x in vals], axis=0))
        z = lax.dot_general(
            jnp.concatenate(rows, axis=1), jnp.concatenate(lanes, axis=1),
            (((1,), (1,)), ((), ())), preferred_element_type=f32)
        for k in range(2):
            acc_ref[k, pl.ds(rb, W), :] += z[2*k*W:(2*k+1)*W] + z[(2*k+1)*W:(2*k+2)*W]

    def block(v, _):
        window(v, begin(v))
        return 0

    def rest(v, _):
        base = begin(v)

        def more(it, _):
            window(v, base + it*W)
            return 0

        return lax.fori_loop(1, ((bnd[(v+1)*(NB//8) - 1, 1] >> 1) - base)//W + 1, more, 0)

    lax.fori_loop(0, 256//NB, block, 0, unroll=UN)
    lax.fori_loop(0, 256//NB, rest, 0)


def from_wire(pos, wire, val, gain=None):
    for k in range(2):
        x = [wire[:, k, h, :] for h in range(2)]
        if gain is not None:
            x = [x[h] * gain[:, h*128:(h+1)*128] for h in range(2)]
        o = permute_lanes(jnp.concatenate(x, axis=1), pos[...])
        val[k, :128, :] = o[0].T
        val[k, 128:, :] = o[1].T


def gather_kernel(ctl, slot, order, first, place, t, wire, s, keys):
    put_edges(t, wire)
    lookup(ctl, slot, order, first, place, t, wire, s, keys)


def tube_kernel(bnd, coupling, cell, pos, gain, drift, wire, ions, inverse, w_out, smooth_out, last_out, edge_out, val, acc):
    pass_edges(wire, edge_out)
    from_wire(pos, wire, val, gain)
    scatter_add(bnd, cell, val, acc)
    w = []
    for k in range(2):
        for j in range(4):
            w_out[k, :, j*128:(j+1)*128] = acc[k, (j%2)*128:(j%2+1)*128, (j//2)*128:(j//2+1)*128]
    for k in range(2):
        n = ions[k]
        growth = coupling[k, 0] * w_out[0] + coupling[k, 1] * w_out[1]
        rhs = n + ion_factor * n * growth
        mix = lax.dot_general(rhs.astype(bf16), inverse[0, k], (((1,), (0,)), ((), ())), preferred_element_type=f32)
        sm = rhs + mix
        smooth_out[k] = sm
        last_out[k] = drift[127:128, :1] * sm[127:128, :]


def drag_kernel(last, ctl, drag, slot, order, first_at, place, gain, drift, w, smooth, up, ions, edge, n_out, wire, t, s, keys):
    for r in range(2):
        wire[:, 2, r, :] = edge[r]
    first = lax.broadcasted_iota(i32, (128, 128), 0) == 0
    d = drift[...]
    n = [[], []]
    for k in range(2):
        for j in range(4):
            sl = slice(j*128, (j+1)*128)
            sm = smooth[k, :, sl]
            out = d * sm
            inflow = jnp.where(first, jnp.broadcast_to(up[k, :, sl], (128, 128)), pltpu.roll(out, 1, 0))
            x = sm - out + inflow
            n[k].append(x)
            n_out[k, :, sl] = 0.5 * (ions[k, :, sl] + x) if last else x
    for j in range(4):
        f = -(drag[0] * n[0][j] + drag[1] * n[1][j])
        for k in range(2):
            t[k, j*128:(j+1)*128, :] = f * w[k, :, j*128:(j+1)*128]
    lookup(ctl, slot, order, first_at, place, t, wire, s, keys, gain)


def tend_all(wind, forcing, visc, wire, acc, emit):
    CX, CY = wind.shape[1], wind.shape[2]
    xlo, xhi, ylo, yhi = beside_tile(wire)
    sub = lax.broadcasted_iota(i32, (CY, 128), 0)
    lane = lax.broadcasted_iota(i32, (CY, 128), 1)
    v = jnp.broadcast_to(visc[...], (CY, 128))
    for k in range(2):
        for i in range(CX):
            u = wind[k, i]
            b = (wind[k, i+1] if i < CX-1 else xhi[k*CY:(k+1)*CY]) + (wind[k, i-1] if i > 0 else xlo[k*CY:(k+1)*CY])
            nxt = jnp.where(sub == CY-1, jnp.broadcast_to(yhi[k*CX+i:k*CX+i+1], (CY, 128)), pltpu.roll(u, CY-1, 0))
            prv = jnp.where(sub == 0, jnp.broadcast_to(ylo[k*CX+i:k*CX+i+1], (CY, 128)), pltpu.roll(u, 1, 0))
            b = b + nxt + prv
            b = b + jnp.where(lane == 127, 0.0, pltpu.roll(u, 127, 1)) + jnp.where(lane == 0, 0.0, pltpu.roll(u, 1, 1))
            emit(k, i, u, v * (b - 6.0 * u) + acc[k, (i*CY) % 256:(i*CY) % 256 + CY, (i*CY)//256*128:(i*CY)//256*128 + 128] + forcing[k, i])


def mid_kernel(bnd, ctl, cell, pos, slot, order, first, place, wire, wind, forcing, visc, mid, wire_out, val, acc, s, keys):
    from_wire(pos, wire, val)
    scatter_add(bnd, cell, val, acc)
    CY = wind.shape[2]

    def emit(k, i, u, f):
        mid[k, i*CY:(i+1)*CY, :] = u + neutral_step * f

    tend_all(wind, forcing, visc, wire, acc, emit)
    put_edges(mid, wire_out)
    lookup(ctl, slot, order, first, place, mid, wire_out, s, keys)


def end_kernel(bnd, cell, pos, wire, start, wind, forcing, visc, out, val, acc):
    from_wire(pos, wire, val)
    scatter_add(bnd, cell, val, acc)

    def emit(k, i, u, f):
        out[k, i] = 0.5 * (start[k, i] + u) + (0.5 * neutral_step) * f

    tend_all(wind, forcing, visc, wire, acc, emit)


def call(kernel, outs, scratch, *args, smem=1, name=None):
    return pl.pallas_call(
        kernel,
        out_shape=outs,
        in_specs=[SM] * smem + [VM] * (len(args) - smem),
        out_specs=jax.tree.map(lambda _: VM, outs),
        scratch_shapes=scratch,
        name=name,
    )(*args)


def tied(*arrays):
    return lax.optimization_barrier(arrays)


def exchange(x):
    return lax.all_to_all(x, ("gx", "gy"), split_axis=0, concat_axis=0, tiled=True)


def per_device(
    neutral_wind,
    forcing,
    ion_density,
    inverse,
    drift_fraction,
    viscosity,
    coupling,
    drag_rate,
    outgoing_column,
    send_level,
    recv_tube,
    recv_point,
    recv_weight,
    pair_count,
):
    visc = viscosity[None, :]
    sd = jax.ShapeDtypeStruct
    wire_t = sd((128, 3, 2, 128), f32)
    tube_t = sd(ion_density.shape, f32)
    vals = pltpu.VMEM((2, 256, 128), f32)
    accs = pltpu.VMEM((2, 256 + W, 256), f32)
    tabs = pltpu.VMEM((2, 512, 128), f32)
    flat = (2, 512, 128)
    up_route = [(i, i + 1) for i in range(lax.axis_size("gy") - 1)]
    side_t = (sd((256, 128), i32), sd((128, 256), i32), sd((32, 128), i32), sd((1024, 128), i32))
    side_t += (sd((128, 256), i32), sd((128, 128), i32), sd((128, 256), i32), sd((8, 128), i32))
    seek = [pltpu.VMEM((2, 1024, 128), f32), pltpu.VMEM((1024, 128), i32)]

    cA, pA, bA, *gA, ctA = call(
        tile_sort_kernel, side_t, [], outgoing_column, send_level, smem=0, name="tilesort")
    wire = call(gather_kernel, wire_t, seek, ctA, *gA, neutral_wind.reshape(flat), name="first")
    came = exchange(wire)
    wire, tub = tied(wire, recv_tube)
    cB, pB, bB, *gB, ctB, gain, drift = call(
        tube_sort_kernel, side_t + (sd((128, 256), f32), sd((128, 128), f32)), [],
        tub, recv_point, recv_weight, pair_count, drift_fraction[None, :], smem=0, name="tubesort")

    def tubes(came, ions, last):
        w, smooth, out_last, edge = call(
            tube_kernel, (tube_t, tube_t, sd((2, 1, 512), f32), sd((2, 128, 128), f32)), [vals, accs],
            bB, coupling, cB, pB, gain, drift, came, ions, inverse, smem=2, name="tube")
        up = lax.ppermute(out_last, "gy", up_route)
        return call(
            lambda *a: drag_kernel(last, *a), (tube_t, wire_t), [tabs] + seek,
            ctB, drag_rate, *gB, gain, drift, w, smooth, up, ion_density, edge, smem=2, name="drag")

    n1, wire = tubes(came, ion_density, False)
    mid, wire = call(
        mid_kernel, (sd(flat, f32), wire_t), [vals, accs] + seek,
        bA, ctA, cA, pA, *gA, exchange(wire), neutral_wind, forcing, visc, smem=2, name="mid")
    ion_out, wire = tubes(exchange(wire), n1, True)
    wind_out = call(
        end_kernel, sd(neutral_wind.shape, f32), [vals, accs],
        bA, cA, pA, exchange(wire), neutral_wind, mid.reshape(neutral_wind.shape), forcing, visc, name="end")
    return (wind_out, ion_out)


def solution(mesh):
    placed = (
        P(None, "gx", "gy", None),
        P(None, "gx", "gy", None),
        P(None, ("gx", "gy"), None),
        P("gx", None, None, None),
        P(("gx", "gy")),
        P(),
        P(),
        P(),
        P(("gx", "gy"), None, None),
        P(("gx", "gy"), None, None),
        P(("gx", "gy"), None, None),
        P(("gx", "gy"), None, None),
        P(("gx", "gy"), None, None),
        P(),
    )
    return jax.shard_map(
        per_device,
        mesh=mesh,
        in_specs=placed,
        out_specs=(P(None, "gx", "gy", None), P(None, ("gx", "gy"), None)),
        check_vma=False,
    )
```

```python
import jax
import jax.numpy as jnp
from jax import lax
from jax.experimental import pallas as pl
from jax.experimental.pallas import tpu as pltpu
from jax.sharding import PartitionSpec as P

i32, f32, bf16 = jnp.int32, jnp.float32, jnp.bfloat16
VM = pl.BlockSpec(memory_space=pltpu.VMEM)
SM = pl.BlockSpec(memory_space=pltpu.SMEM)
W, NB, UN = 80, 16, 2
neutral_step = 0.4
ion_factor = 0.5


def bitonic(x):
    n, L = x.shape
    x = x.reshape(n//8, 8, L)
    sub = lax.broadcasted_iota(i32, (1, 8, L), 1)
    k = 2
    while k <= n:
        d = k//2
        while d >= 1:
            if d >= 8:
                dv = d//8
                y = x.reshape(n//(16*dv), 2, dv, 8, L)
                a, b = y[:, 0], y[:, 1]
                lo, hi = jnp.minimum(a, b), jnp.maximum(a, b)
                parts = []
                for g in range(n//(16*dv)):
                    up = ((g*2*d) & k) == 0
                    parts += [lo[g], hi[g]] if up else [hi[g], lo[g]]
                x = jnp.concatenate(parts, axis=0)
            else:
                up_r = pltpu.roll(x, 8-d, 1)
                dn_r = pltpu.roll(x, d, 1)
                first = (sub & d) == 0
                p = jnp.where(first, up_r, dn_r)
                mn, mx = jnp.minimum(x, p), jnp.maximum(x, p)
                if k >= 8:
                    if k == 8:
                        vi = lax.broadcasted_iota(i32, (n//8, 1, 1), 0)
                    parts = []
                    xs = []
                    take_min_up = first
                    kv = k//8
                    for g in range(0, n//8, kv):
                        up = (g*8 & k) == 0
                        sel = first if up else jnp.logical_not(first)
                        xs.append(jnp.where(sel, mn[g:g+kv], mx[g:g+kv]))
                    x = jnp.concatenate(xs, axis=0) if len(xs) > 1 else xs[0]
                else:
                    up = (sub & k) == 0
                    sel = first == up
                    x = jnp.where(sel, mn, mx)
            d //= 2
        k *= 2
    return x.reshape(n, L)

def row_of(r, start=0, count=128):
    return pl.ds(6*start + r, count, stride=6)


def take(x, idx):
    return jnp.take_along_axis(x, idx, axis=1, mode="promise_in_bounds")


def take2(x, idx):
    low = idx & 127
    return jnp.where(idx < 128, take(x[:, :128], low), take(x[:, 128:], low))


def slot_tile(order, first, turn, j, slots):
    lane = lax.broadcasted_iota(i32, (128, 128), 1)
    idx = take(first[...], 8*j + (lane >> 4)) + 16*turn + (lane & 15)
    slots[pl.ds(pl.multiple_of(j*128, 128), 128), :] = (take2(order, jnp.minimum(idx, 255)) & 1023).T


def sort_side(key16, cell_ref, pos_ref, bnd_ref, slot_ref, order_ref, first_ref, place_ref, ctl_ref):
    P, C = key16.shape
    c = lax.broadcasted_iota(i32, (P, C), 1)
    s = bitonic((key16 * 256 + c).astype(f32).T).astype(i32)
    cell = s >> 8
    cell_ref[...] = cell
    pos = (s & 255).T
    pos_ref[...] = pos
    row = (cell >> 7).reshape(C//8, 8, P)
    lo = jnp.min(jnp.min(row, axis=1), axis=1, keepdims=True)
    hi = jnp.max(jnp.max(row, axis=1), axis=1, keepdims=True)
    lane = lax.broadcasted_iota(i32, (C//8, 128), 1)
    bnd_ref[...] = jnp.where(lane == 0, lo, hi)
    order = cell.T
    order_ref[...] = order
    lane = lax.broadcasted_iota(i32, (P, 128), 1)
    first = jnp.zeros((P, 128), i32)
    for step in (128, 64, 32, 16, 8, 4, 2, 1, 1):
        probe = first + step
        first = jnp.where(take2(order, probe - 1) < lane*1024, probe, first)
    first_ref[...] = first
    most = jnp.max((pltpu.roll(first, 127, 1) - first).astype(f32), axis=0, keepdims=True)
    most = jnp.where(lane[:1] < 64, most, 0.0)
    top = jnp.broadcast_to(jnp.max(most, axis=1, keepdims=True), (1, 128))
    ctl_ref[...] = jnp.broadcast_to(jnp.where(lane[:1] < 64, most, top), (8, 128)).astype(i32)
    for j in range(8):
        slot_tile(order, first_ref, 0, j, slot_ref)
    b = order >> 10
    w = c - jnp.concatenate([take(first, b[:, :128]), take(first, b[:, 128:])], axis=1)
    place = (pos << 14) + ((w >> 4) << 10) + (b << 4) + (w & 15)
    place_ref[...] = (bitonic(place.astype(f32).T).astype(i32) & 16383).T


def cell_key(row, lane):
    return ((row & 255) << 8) + ((row >> 8) << 7) + lane


def put_edges(t, wire):
    CX, CY = 16, t.shape[1] // 16
    for k in range(2):
        wire[row_of(4, k*CY, CY), :] = t[k, (CX-1)*CY:CX*CY, :]
        wire[row_of(4, (2+k)*CY, CY), :] = t[k, :CY, :]
        for i in range(CX):
            for q, at in ((k*CX+i, (i+1)*CY-1), ((2+k)*CX+i, i*CY)):
                wire[6*q+5:6*q+6, :] = t[k, at:at+1, :]
    wire[row_of(5, 4*CX, 128 - 4*CX), :] = jnp.zeros((128 - 4*CX, 128), f32)


def place_of():
    x, y = lax.axis_index("gx"), lax.axis_index("gy")
    return x, y, x * lax.axis_size("gy") + y


def pass_edges(wire, out):
    q = place_of()[2]
    step = lax.axis_size("gy")
    for r, (cut, d) in enumerate(((64, step), (32, 1))):
        x = wire[row_of(4+r), :]
        out[r] = jnp.where(q < cut, pltpu.roll(x, d, 0), pltpu.roll(x, 128-d, 0))


def beside_tile(wire):
    x, y = place_of()[:2]
    a, b = wire[row_of(4), :], wire[row_of(5, 0, 64), :]
    return (
        jnp.where(x > 0, a[:64], 0.0),
        jnp.where(x < lax.axis_size("gx") - 1, a[64:], 0.0),
        jnp.where(y > 0, b[:32], 0.0),
        jnp.where(y < lax.axis_size("gy") - 1, b[32:], 0.0),
    )


def tube_sort_kernel(tub, pnt, weight, count, drift, *outs):
    side, gain, drift_out = outs[:8], outs[8], outs[9]
    p = pnt[0]
    sort_side(cell_key((p >> 7)*128 + tub[0], p & 127), *side)
    own = place_of()[2]
    lane = lax.broadcasted_iota(i32, (128, 128), 1)
    live = jnp.sum(jnp.where(lane == own, count[...], 0).astype(f32), axis=1, keepdims=True)
    c = lax.broadcasted_iota(i32, (128, 256), 1).astype(f32)
    gain[...] = jnp.where(c < live, weight[0], 0.0)
    drift_out[...] = jnp.broadcast_to(drift[...], (128, 128)).T


def permute_lanes(x, idx):
    return [take2(x, idx[:, :128]), take2(x, idx[:, 128:])]


def lookup(ctl, slot, order, first, place, t_ref, wire, s_ref, key_ref, gain=None, limit_copy=None):
    half = t_ref.shape[1] // 2

    def group(g, keys):
        for b in range(8):
            rows = []
            for j in range(8):
                at = g*32 + 4*b + j//2 + (j % 2)*half
                rows.append([jnp.broadcast_to(t_ref[k, pl.ds(at, 1), :], (8, 128)) for k in range(2)])
            for i in range(2):
                sl = pl.ds(pl.multiple_of(g*128 + b*16 + i*8, 8), 8)
                key = keys[sl, :]
                sub, lev = key >> 7, key & 127
                acc = [take(rows[0][k], lev) for k in range(2)]
                for j in range(1, 8):
                    m = sub == j
                    for k in range(2):
                        acc[k] = jnp.where(m, take(rows[j][k], lev), acc[k])
                for k in range(2):
                    s_ref[k, sl, :] = acc[k]

    def each(g, _):
        group(g, slot)
        return 0

    def scaled(x, h):
        return x if gain is None else x * gain[:, h*128:(h+1)*128]

    lax.fori_loop(0, 8, each, 0)
    if limit_copy is not None:
        limit_copy.start()
    parts = [[s_ref[k, j*128:(j+1)*128, :].T for j in range(8)] for k in range(2)]
    for h in range(2):
        at = place[:, h*128:(h+1)*128]
        low, tile = at & 127, (at >> 7) & 7
        for k in range(2):
            x = take(parts[k][0], low)
            for j in range(1, 8):
                x = jnp.where(tile == j, take(parts[k][j], low), x)
            wire[row_of(2*k+h), :] = scaled(x, h)

    def turn(t, _):
        def late(g, _):
            most = ctl[0, 8*g]
            for b in range(1, 8):
                most = jnp.maximum(most, ctl[0, 8*g + b])

            @pl.when(most > 16*t)
            def _():
                slot_tile(order[...], first, t, g, key_ref)
                group(g, key_ref)
                tile = pl.ds(pl.multiple_of(g*128, 128), 128)
                for h in range(2):
                    at = place[:, h*128:(h+1)*128]
                    mine = (at >> 7) == 8*t + g
                    for k in range(2):
                        x = take(s_ref[k, tile, :].T, at & 127)
                        wire[row_of(2*k+h), :] = jnp.where(mine, scaled(x, h), wire[row_of(2*k+h), :])
            return 0

        lax.fori_loop(0, 8, late, 0)
        return 0

    if limit_copy is not None:
        limit_copy.wait()
    lax.fori_loop(1, (ctl[0, 64] + 15) // 16, turn, 0)


def scatter_add(bnd, cell_ref, val_ref, acc_ref):
    acc_ref[...] = jnp.zeros_like(acc_ref)
    iota = lax.broadcasted_iota(i32, (256, 128), 0).astype(f32).astype(bf16)
    one, zero = jnp.ones((256, 128), bf16), jnp.zeros((256, 128), bf16)

    def spread(x, n):
        return jnp.broadcast_to(x, (n, 128)).astype(bf16)

    def begin(v):
        return ((bnd[v*(NB//8), 0] >> 1) // 8) * 8

    def window(v, rb):
        rb = pl.multiple_of(rb, 8)
        sl = pl.ds(pl.multiple_of(v*NB, 8), NB)
        key = cell_ref[sl, :]
        rel, lane = ((key >> 8) - rb).astype(f32), (key & 255).astype(f32)
        vals = []
        for k in range(2):
            x = val_ref[k, sl, :]
            h = x.astype(bf16).astype(f32)
            vals += [h, x - h]
        rows, lanes = [], []
        for r in range(NB):
            lanes.append(jnp.where(iota == spread(lane[r:r+1], 256), one, zero))
            m = iota[:W] == spread(rel[r:r+1], W)
            rows.append(jnp.concatenate([jnp.where(m, spread(x[r:r+1], W), zero[:W]) for x in vals], axis=0))
        z = lax.dot_general(
            jnp.concatenate(rows, axis=1), jnp.concatenate(lanes, axis=1),
            (((1,), (1,)), ((), ())), preferred_element_type=f32)
        for k in range(2):
            acc_ref[k, pl.ds(rb, W), :] += z[2*k*W:(2*k+1)*W] + z[(2*k+1)*W:(2*k+2)*W]

    def block(v, _):
        window(v, begin(v))
        return 0

    def rest(v, _):
        base = begin(v)

        def more(it, _):
            window(v, base + it*W)
            return 0

        return lax.fori_loop(1, ((bnd[(v+1)*(NB//8) - 1, 1] >> 1) - base)//W + 1, more, 0)

    lax.fori_loop(0, 256//NB, block, 0, unroll=UN)
    lax.fori_loop(0, 256//NB, rest, 0)


def from_wire(pos, wire, val, gain=None):
    for k in range(2):
        x = [wire[row_of(2*k+h), :] for h in range(2)]
        if gain is not None:
            x = [x[h] * gain[:, h*128:(h+1)*128] for h in range(2)]
        o = permute_lanes(jnp.concatenate(x, axis=1), pos[...])
        val[k, :128, :] = o[0].T
        val[k, 128:, :] = o[1].T


def first_kernel(col, lev, t, *refs):
    side, wire, s, keys, limits, sem = refs[:8], refs[8], *refs[9:]
    sort_side(cell_key(col[0], lev[0]), *side)
    copy = pltpu.make_async_copy(side[7], limits, sem)
    put_edges(t, wire)
    lookup(limits, *side[3:7], t, wire, s, keys, limit_copy=copy)


def tube_kernel(bnd, coupling, cell, pos, gain, drift, wire, ions, inverse, w_out, smooth_out, last_out, edge_out, val, acc):
    pass_edges(wire, edge_out)
    from_wire(pos, wire, val, gain)
    scatter_add(bnd, cell, val, acc)
    w = []
    for k in range(2):
        for j in range(4):
            w_out[k, :, j*128:(j+1)*128] = acc[k, (j%2)*128:(j%2+1)*128, (j//2)*128:(j//2+1)*128]
    for k in range(2):
        n = ions[k]
        growth = coupling[k, 0] * w_out[0] + coupling[k, 1] * w_out[1]
        rhs = n + ion_factor * n * growth
        mix = lax.dot_general(rhs.astype(bf16), inverse[0, k], (((1,), (0,)), ((), ())), preferred_element_type=f32)
        sm = rhs + mix
        smooth_out[k] = sm
        last_out[k] = drift[127:128, :1] * sm[127:128, :]


def drag_kernel(last, ctl, drag, slot, order, first_at, place, gain, drift, w, smooth, up, ions, edge, n_out, wire, t, s, keys):
    for r in range(2):
        wire[row_of(4+r), :] = edge[r]
    first = lax.broadcasted_iota(i32, (128, 128), 0) == 0
    d = drift[...]
    n = [[], []]
    for k in range(2):
        for j in range(4):
            sl = slice(j*128, (j+1)*128)
            sm = smooth[k, :, sl]
            out = d * sm
            inflow = jnp.where(first, jnp.broadcast_to(up[k, :, sl], (128, 128)), pltpu.roll(out, 1, 0))
            x = sm - out + inflow
            n[k].append(x)
            n_out[k, :, sl] = 0.5 * (ions[k, :, sl] + x) if last else x
    for j in range(4):
        f = -(drag[0] * n[0][j] + drag[1] * n[1][j])
        for k in range(2):
            t[k, j*128:(j+1)*128, :] = f * w[k, :, j*128:(j+1)*128]
    lookup(ctl, slot, order, first_at, place, t, wire, s, keys, gain)


def tend_all(wind, forcing, visc, wire, acc, emit):
    CX, CY = wind.shape[1], wind.shape[2]
    xlo, xhi, ylo, yhi = beside_tile(wire)
    sub = lax.broadcasted_iota(i32, (CY, 128), 0)
    lane = lax.broadcasted_iota(i32, (CY, 128), 1)
    v = jnp.broadcast_to(visc[...], (CY, 128))
    for k in range(2):
        for i in range(CX):
            u = wind[k, i]
            b = (wind[k, i+1] if i < CX-1 else xhi[k*CY:(k+1)*CY]) + (wind[k, i-1] if i > 0 else xlo[k*CY:(k+1)*CY])
            nxt = jnp.where(sub == CY-1, jnp.broadcast_to(yhi[k*CX+i:k*CX+i+1], (CY, 128)), pltpu.roll(u, CY-1, 0))
            prv = jnp.where(sub == 0, jnp.broadcast_to(ylo[k*CX+i:k*CX+i+1], (CY, 128)), pltpu.roll(u, 1, 0))
            b = b + nxt + prv
            b = b + jnp.where(lane == 127, 0.0, pltpu.roll(u, 127, 1)) + jnp.where(lane == 0, 0.0, pltpu.roll(u, 1, 1))
            emit(k, i, u, v * (b - 6.0 * u) + acc[k, (i*CY) % 256:(i*CY) % 256 + CY, (i*CY)//256*128:(i*CY)//256*128 + 128] + forcing[k, i])


def mid_kernel(bnd, ctl, cell, pos, slot, order, first, place, wire, wind, forcing, visc, mid, wire_out, val, acc, s, keys):
    from_wire(pos, wire, val)
    scatter_add(bnd, cell, val, acc)
    CY = wind.shape[2]

    def emit(k, i, u, f):
        mid[k, i*CY:(i+1)*CY, :] = u + neutral_step * f

    tend_all(wind, forcing, visc, wire, acc, emit)
    put_edges(mid, wire_out)
    lookup(ctl, slot, order, first, place, mid, wire_out, s, keys)


def end_kernel(bnd, cell, pos, wire, start, wind, forcing, visc, out, val, acc):
    from_wire(pos, wire, val)
    scatter_add(bnd, cell, val, acc)

    def emit(k, i, u, f):
        out[k, i] = 0.5 * (start[k, i] + u) + (0.5 * neutral_step) * f

    tend_all(wind, forcing, visc, wire, acc, emit)


def call(kernel, outs, scratch, *args, smem=1, name=None):
    return pl.pallas_call(
        kernel,
        out_shape=outs,
        in_specs=[SM] * smem + [VM] * (len(args) - smem),
        out_specs=jax.tree.map(lambda _: VM, outs),
        scratch_shapes=scratch,
        name=name,
    )(*args)


def tied(*arrays):
    return lax.optimization_barrier(arrays)


def exchange(x):
    x = x.reshape(128, 3, 2, 128)
    return lax.all_to_all(x, ("gx", "gy"), split_axis=0, concat_axis=0, tiled=True).reshape(768, 128)


def per_device(
    neutral_wind,
    forcing,
    ion_density,
    inverse,
    drift_fraction,
    viscosity,
    coupling,
    drag_rate,
    outgoing_column,
    send_level,
    recv_tube,
    recv_point,
    recv_weight,
    pair_count,
):
    visc = viscosity[None, :]
    sd = jax.ShapeDtypeStruct
    wire_t = sd((768, 128), f32)
    tube_t = sd(ion_density.shape, f32)
    vals = pltpu.VMEM((2, 256, 128), f32)
    accs = pltpu.VMEM((2, 256 + W, 256), f32)
    tabs = pltpu.VMEM((2, 512, 128), f32)
    flat = (2, 512, 128)
    up_route = [(i, i + 1) for i in range(lax.axis_size("gy") - 1)]
    side_t = (sd((256, 128), i32), sd((128, 256), i32), sd((32, 128), i32), sd((1024, 128), i32))
    side_t += (sd((128, 256), i32), sd((128, 128), i32), sd((128, 256), i32), sd((8, 128), i32))
    seek = [pltpu.VMEM((2, 1024, 128), f32), pltpu.VMEM((1024, 128), i32)]

    cA, pA, bA, *gA, ctA, wire = call(
        first_kernel, side_t + (wire_t,), seek + [pltpu.SMEM((8, 128), i32), pltpu.SemaphoreType.DMA],
        outgoing_column, send_level, neutral_wind.reshape(flat), smem=0, name="first")
    came = exchange(wire)
    wire, tub = tied(wire, recv_tube)
    cB, pB, bB, *gB, ctB, gain, drift = call(
        tube_sort_kernel, side_t + (sd((128, 256), f32), sd((128, 128), f32)), [],
        tub, recv_point, recv_weight, pair_count, drift_fraction[None, :], smem=0, name="tubesort")

    def tubes(came, ions, last):
        w, smooth, out_last, edge = call(
            tube_kernel, (tube_t, tube_t, sd((2, 1, 512), f32), sd((2, 128, 128), f32)), [vals, accs],
            bB, coupling, cB, pB, gain, drift, came, ions, inverse, smem=2, name="tube")
        up = lax.ppermute(out_last, "gy", up_route)
        return call(
            lambda *a: drag_kernel(last, *a), (tube_t, wire_t), [tabs] + seek,
            ctB, drag_rate, *gB, gain, drift, w, smooth, up, ion_density, edge, smem=2, name="drag")

    n1, wire = tubes(came, ion_density, False)
    mid, wire = call(
        mid_kernel, (sd(flat, f32), wire_t), [vals, accs] + seek,
        bA, ctA, cA, pA, *gA, exchange(wire), neutral_wind, forcing, visc, smem=2, name="mid")
    ion_out, wire = tubes(exchange(wire), n1, True)
    wind_out = call(
        end_kernel, sd(neutral_wind.shape, f32), [vals, accs],
        bA, cA, pA, exchange(wire), neutral_wind, mid.reshape(neutral_wind.shape), forcing, visc, name="end")
    return (wind_out, ion_out)


def solution(mesh):
    placed = (
        P(None, "gx", "gy", None),
        P(None, "gx", "gy", None),
        P(None, ("gx", "gy"), None),
        P("gx", None, None, None),
        P(("gx", "gy")),
        P(),
        P(),
        P(),
        P(("gx", "gy"), None, None),
        P(("gx", "gy"), None, None),
        P(("gx", "gy"), None, None),
        P(("gx", "gy"), None, None),
        P(("gx", "gy"), None, None),
        P(),
    )
    return jax.shard_map(
        per_device,
        mesh=mesh,
        in_specs=placed,
        out_specs=(P(None, "gx", "gy", None), P(None, ("gx", "gy"), None)),
        check_vma=False,
    )
```

```python
import jax
import jax.numpy as jnp
from jax import lax
from jax.experimental import pallas as pl
from jax.experimental.pallas import tpu as pltpu
from jax.sharding import PartitionSpec as P

i32, f32, bf16 = jnp.int32, jnp.float32, jnp.bfloat16
VM = pl.BlockSpec(memory_space=pltpu.VMEM)
SM = pl.BlockSpec(memory_space=pltpu.SMEM)
W, NB, UN = 80, 16, 2
neutral_step = 0.4
ion_factor = 0.5


def bitonic(x):
    n, L = x.shape
    x = x.reshape(n//8, 8, L)
    sub = lax.broadcasted_iota(i32, (1, 8, L), 1)
    k = 2
    while k <= n:
        d = k//2
        while d >= 1:
            if d >= 8:
                dv = d//8
                y = x.reshape(n//(16*dv), 2, dv, 8, L)
                a, b = y[:, 0], y[:, 1]
                lo, hi = jnp.minimum(a, b), jnp.maximum(a, b)
                parts = []
                for g in range(n//(16*dv)):
                    up = ((g*2*d) & k) == 0
                    parts += [lo[g], hi[g]] if up else [hi[g], lo[g]]
                x = jnp.concatenate(parts, axis=0)
            else:
                up_r = pltpu.roll(x, 8-d, 1)
                dn_r = pltpu.roll(x, d, 1)
                first = (sub & d) == 0
                p = jnp.where(first, up_r, dn_r)
                mn, mx = jnp.minimum(x, p), jnp.maximum(x, p)
                if k >= 8:
                    if k == 8:
                        vi = lax.broadcasted_iota(i32, (n//8, 1, 1), 0)
                    parts = []
                    xs = []
                    take_min_up = first
                    kv = k//8
                    for g in range(0, n//8, kv):
                        up = (g*8 & k) == 0
                        sel = first if up else jnp.logical_not(first)
                        xs.append(jnp.where(sel, mn[g:g+kv], mx[g:g+kv]))
                    x = jnp.concatenate(xs, axis=0) if len(xs) > 1 else xs[0]
                else:
                    up = (sub & k) == 0
                    sel = first == up
                    x = jnp.where(sel, mn, mx)
            d //= 2
        k *= 2
    return x.reshape(n, L)

def row_of(r, start=0, count=128):
    return pl.ds(6*start + r, count, stride=6)


def take(x, idx):
    return jnp.take_along_axis(x, idx, axis=1, mode="promise_in_bounds")


def take2(x, idx):
    low = idx & 127
    return jnp.where(idx < 128, take(x[:, :128], low), take(x[:, 128:], low))


def slot_tile(order, first, turn, j, slots):
    lane = lax.broadcasted_iota(i32, (128, 128), 1)
    idx = take(first[...], 8*j + (lane >> 4)) + 16*turn + (lane & 15)
    slots[pl.ds(pl.multiple_of(j*128, 128), 128), :] = (take2(order, jnp.minimum(idx, 255)) & 1023).T


def sort_side(key16, cell_ref, pos_ref, bnd_ref, slot_ref, order_ref, first_ref, place_ref, ctl_ref):
    P, C = key16.shape
    c = lax.broadcasted_iota(i32, (P, C), 1)
    s = bitonic((key16 * 256 + c).astype(f32).T).astype(i32)
    cell = s >> 8
    cell_ref[...] = cell
    pos = (s & 255).T
    pos_ref[...] = pos
    row = (cell >> 7).reshape(C//8, 8, P)
    lo = jnp.min(jnp.min(row, axis=1), axis=1, keepdims=True)
    hi = jnp.max(jnp.max(row, axis=1), axis=1, keepdims=True)
    lane = lax.broadcasted_iota(i32, (C//8, 128), 1)
    bnd_ref[...] = jnp.where(lane == 0, lo, hi)
    order = cell.T
    order_ref[...] = order
    lane = lax.broadcasted_iota(i32, (P, 128), 1)
    first = jnp.zeros((P, 128), i32)
    for step in (128, 64, 32, 16, 8, 4, 2, 1, 1):
        probe = first + step
        first = jnp.where(take2(order, probe - 1) < lane*1024, probe, first)
    first_ref[...] = first
    most = jnp.max((pltpu.roll(first, 127, 1) - first).astype(f32), axis=0, keepdims=True)
    most = jnp.where(lane[:1] < 64, most, 0.0)
    top = jnp.broadcast_to(jnp.max(most, axis=1, keepdims=True), (1, 128))
    ctl_ref[...] = jnp.broadcast_to(jnp.where(lane[:1] < 64, most, top), (8, 128)).astype(i32)
    for j in range(8):
        slot_tile(order, first_ref, 0, j, slot_ref)
    b = order >> 10
    w = c - jnp.concatenate([take(first, b[:, :128]), take(first, b[:, 128:])], axis=1)
    place = (pos << 14) + ((w >> 4) << 10) + (b << 4) + (w & 15)
    place_ref[...] = (bitonic(place.astype(f32).T).astype(i32) & 16383).T


def cell_key(row, lane):
    return ((row & 255) << 8) + ((row >> 8) << 7) + lane


def put_edges(t, wire):
    CX, CY = 16, t.shape[1] // 16
    for k in range(2):
        wire[row_of(4, k*CY, CY), :] = t[k, (CX-1)*CY:CX*CY, :]
        wire[row_of(4, (2+k)*CY, CY), :] = t[k, :CY, :]
        for i in range(CX):
            for q, at in ((k*CX+i, (i+1)*CY-1), ((2+k)*CX+i, i*CY)):
                wire[6*q+5:6*q+6, :] = t[k, at:at+1, :]
    wire[row_of(5, 4*CX, 128 - 4*CX), :] = jnp.zeros((128 - 4*CX, 128), f32)


def place_of():
    x, y = lax.axis_index("gx"), lax.axis_index("gy")
    return x, y, x * lax.axis_size("gy") + y


def pass_edges(wire, out):
    q = place_of()[2]
    step = lax.axis_size("gy")
    for r, (cut, d) in enumerate(((64, step), (32, 1))):
        x = wire[row_of(4+r), :]
        out[r] = jnp.where(q < cut, pltpu.roll(x, d, 0), pltpu.roll(x, 128-d, 0))


def beside_tile(wire):
    x, y = place_of()[:2]
    a, b = wire[row_of(4), :], wire[row_of(5, 0, 64), :]
    return (
        jnp.where(x > 0, a[:64], 0.0),
        jnp.where(x < lax.axis_size("gx") - 1, a[64:], 0.0),
        jnp.where(y > 0, b[:32], 0.0),
        jnp.where(y < lax.axis_size("gy") - 1, b[32:], 0.0),
    )


def tube_sort_kernel(tub, pnt, weight, count, drift, *outs):
    side, gain, drift_out = outs[:8], outs[8], outs[9]
    p = pnt[0]
    sort_side(cell_key((p >> 7)*128 + tub[0], p & 127), *side)
    own = place_of()[2]
    lane = lax.broadcasted_iota(i32, (128, 128), 1)
    live = jnp.sum(jnp.where(lane == own, count[...], 0).astype(f32), axis=1, keepdims=True)
    c = lax.broadcasted_iota(i32, (128, 256), 1).astype(f32)
    gain[...] = jnp.where(c < live, weight[0], 0.0)
    drift_out[...] = jnp.broadcast_to(drift[...], (128, 128)).T


def permute_lanes(x, idx):
    return [take2(x, idx[:, :128]), take2(x, idx[:, 128:])]


def lookup(ctl, slot, order, first, place, t_ref, wire, s_ref, key_ref, gain=None, limit_copy=None, hook=None):
    half = t_ref.shape[1] // 2

    slot = slot() if callable(slot) else slot

    def group(g, keys):
        for b in range(8):
            rows = []
            for j in range(8):
                at = g*32 + 4*b + j//2 + (j % 2)*half
                rows.append([jnp.broadcast_to(t_ref[k, pl.ds(at, 1), :], (8, 128)) for k in range(2)])
            for i in range(2):
                sl = pl.ds(pl.multiple_of(g*128 + b*16 + i*8, 8), 8)
                key = keys[sl, :]
                sub, lev = key >> 7, key & 127
                acc = [take(rows[0][k], lev) for k in range(2)]
                for j in range(1, 8):
                    m = sub == j
                    for k in range(2):
                        acc[k] = jnp.where(m, take(rows[j][k], lev), acc[k])
                for k in range(2):
                    s_ref[k, sl, :] = acc[k]

    def each(g, _):
        group(g, slot)
        return 0

    def scaled(x, h):
        return x if gain is None else x * gain[:, h*128:(h+1)*128]

    lax.fori_loop(0, 8, each, 0)
    if limit_copy is not None:
        limit_copy.start()
    if hook is not None:
        hook()
    place, order, first = [x() if callable(x) else x for x in (place, order, first)]
    gain = gain() if callable(gain) else gain
    parts = [[s_ref[k, j*128:(j+1)*128, :].T for j in range(8)] for k in range(2)]
    for h in range(2):
        at = place[:, h*128:(h+1)*128]
        low, tile = at & 127, (at >> 7) & 7
        for k in range(2):
            x = take(parts[k][0], low)
            for j in range(1, 8):
                x = jnp.where(tile == j, take(parts[k][j], low), x)
            wire[row_of(2*k+h), :] = scaled(x, h)

    def turn(t, _):
        def late(g, _):
            most = ctl[0, 8*g]
            for b in range(1, 8):
                most = jnp.maximum(most, ctl[0, 8*g + b])

            @pl.when(most > 16*t)
            def _():
                slot_tile(order[...], first, t, g, key_ref)
                group(g, key_ref)
                tile = pl.ds(pl.multiple_of(g*128, 128), 128)
                for h in range(2):
                    at = place[:, h*128:(h+1)*128]
                    mine = (at >> 7) == 8*t + g
                    for k in range(2):
                        x = take(s_ref[k, tile, :].T, at & 127)
                        wire[row_of(2*k+h), :] = jnp.where(mine, scaled(x, h), wire[row_of(2*k+h), :])
            return 0

        lax.fori_loop(0, 8, late, 0)
        return 0

    if limit_copy is not None:
        limit_copy.wait()
    lax.fori_loop(1, (ctl[0, 64] + 15) // 16, turn, 0)


def scatter_add(bnd, cell_ref, val_ref, acc_ref):
    acc_ref[...] = jnp.zeros_like(acc_ref)
    iota = lax.broadcasted_iota(i32, (256, 128), 0).astype(f32).astype(bf16)
    one, zero = jnp.ones((256, 128), bf16), jnp.zeros((256, 128), bf16)

    def spread(x, n):
        return jnp.broadcast_to(x, (n, 128)).astype(bf16)

    def begin(v):
        return ((bnd[v*(NB//8), 0] >> 1) // 8) * 8

    def window(v, rb):
        rb = pl.multiple_of(rb, 8)
        sl = pl.ds(pl.multiple_of(v*NB, 8), NB)
        key = cell_ref[sl, :]
        rel, lane = ((key >> 8) - rb).astype(f32), (key & 255).astype(f32)
        vals = []
        for k in range(2):
            x = val_ref[k, sl, :]
            h = x.astype(bf16).astype(f32)
            vals += [h, x - h]
        rows, lanes = [], []
        for r in range(NB):
            lanes.append(jnp.where(iota == spread(lane[r:r+1], 256), one, zero))
            m = iota[:W] == spread(rel[r:r+1], W)
            rows.append(jnp.concatenate([jnp.where(m, spread(x[r:r+1], W), zero[:W]) for x in vals], axis=0))
        z = lax.dot_general(
            jnp.concatenate(rows, axis=1), jnp.concatenate(lanes, axis=1),
            (((1,), (1,)), ((), ())), preferred_element_type=f32)
        for k in range(2):
            acc_ref[k, pl.ds(rb, W), :] += z[2*k*W:(2*k+1)*W] + z[(2*k+1)*W:(2*k+2)*W]

    def block(v, _):
        window(v, begin(v))
        return 0

    def rest(v, _):
        base = begin(v)

        def more(it, _):
            window(v, base + it*W)
            return 0

        return lax.fori_loop(1, ((bnd[(v+1)*(NB//8) - 1, 1] >> 1) - base)//W + 1, more, 0)

    lax.fori_loop(0, 256//NB, block, 0, unroll=UN)
    lax.fori_loop(0, 256//NB, rest, 0)


def from_wire(pos, wire, val, gain=None):
    for k in range(2):
        x = [wire[row_of(2*k+h), :] for h in range(2)]
        if gain is not None:
            x = [x[h] * gain[:, h*128:(h+1)*128] for h in range(2)]
        o = permute_lanes(jnp.concatenate(x, axis=1), pos[...])
        val[k, :128, :] = o[0].T
        val[k, 128:, :] = o[1].T


def first_kernel(col, lev, t, *refs):
    side, wire, s, keys, limits, sem = refs[:8], refs[8], *refs[9:]
    cell, pos, bnd, slot, order, first, place, ctl = side
    view = [x.ref for x in (cell, pos)] + [bnd] + [x.ref for x in (slot, order, first, place)] + [ctl]
    sort_side(cell_key(col[0], lev[0]), *view)
    t = t()
    put_edges(t, wire)

    def hook():
        for x in (slot, cell, pos, order, place, first):
            x.send()

    lookup(limits, *view[3:7], t, wire, s, keys, limit_copy=pltpu.make_async_copy(ctl, limits, sem), hook=hook)


def tube_kernel(bnd, coupling, cell, pos, gain, drift, wire, ions, inverse, w_out, smooth_out, last_out, edge_out, val, acc):
    wire = wire()
    pass_edges(wire, edge_out.ref)
    from_wire(pos(), wire, val, gain())
    scatter_add(bnd, cell(), val, acc)
    edge_out.send()
    w = w_out.ref
    for k in range(2):
        for j in range(4):
            w[k, :, j*128:(j+1)*128] = acc[k, (j % 2)*128:(j % 2+1)*128, (j//2)*128:(j//2+1)*128]
    ions, drift, inverse = ions(), drift(), inverse()
    for k in range(2):
        n = ions[k]
        growth = coupling[k, 0] * w[0] + coupling[k, 1] * w[1]
        rhs = n + ion_factor * n * growth
        mix = lax.dot_general(rhs.astype(bf16), inverse[0, k], (((1,), (0,)), ((), ())), preferred_element_type=f32)
        sm = rhs + mix
        smooth_out[k] = sm
        last_out[k] = drift[127:128, :1] * sm[127:128, :]
        if k == 0:
            w_out.send()


def drag_kernel(last, ctl, drag, slot, order, first_at, place, gain, drift, w, smooth, up, ions, edge, n_out, wire, t, s, keys):
    w, smooth, drift = w(), smooth(), drift()
    ions = ions() if last else None
    first = lax.broadcasted_iota(i32, (128, 128), 0) == 0
    d = drift[...]
    n = [[], []]
    for k in range(2):
        for j in range(4):
            sl = slice(j*128, (j+1)*128)
            sm = smooth[k, :, sl]
            out = d * sm
            inflow = jnp.where(first, jnp.broadcast_to(up[k, :, sl], (128, 128)), pltpu.roll(out, 1, 0))
            x = sm - out + inflow
            n[k].append(x)
            n_out.ref[k, :, sl] = 0.5 * (ions[k, :, sl] + x) if last else x
    for j in range(4):
        f = -(drag[0] * n[0][j] + drag[1] * n[1][j])
        for k in range(2):
            t[k, j*128:(j+1)*128, :] = f * w[k, :, j*128:(j+1)*128]

    def hook():
        n_out.send()
        move = edge()
        for r in range(2):
            wire[row_of(4+r), :] = move[r]

    lookup(ctl, slot, order, first_at, place, t, wire, s, keys, gain, hook=hook)


def tend_all(wind, forcing, visc, wire, acc, emit):
    CX, CY = wind.shape[1], wind.shape[2]
    xlo, xhi, ylo, yhi = beside_tile(wire)
    sub = lax.broadcasted_iota(i32, (CY, 128), 0)
    lane = lax.broadcasted_iota(i32, (CY, 128), 1)
    v = jnp.broadcast_to(visc[...], (CY, 128))
    for k in range(2):
        for i in range(CX):
            u = wind[k, i]
            b = (wind[k, i+1] if i < CX-1 else xhi[k*CY:(k+1)*CY]) + (wind[k, i-1] if i > 0 else xlo[k*CY:(k+1)*CY])
            nxt = jnp.where(sub == CY-1, jnp.broadcast_to(yhi[k*CX+i:k*CX+i+1], (CY, 128)), pltpu.roll(u, CY-1, 0))
            prv = jnp.where(sub == 0, jnp.broadcast_to(ylo[k*CX+i:k*CX+i+1], (CY, 128)), pltpu.roll(u, 1, 0))
            b = b + nxt + prv
            b = b + jnp.where(lane == 127, 0.0, pltpu.roll(u, 127, 1)) + jnp.where(lane == 0, 0.0, pltpu.roll(u, 1, 1))
            emit(k, i, u, v * (b - 6.0 * u) + acc[k, (i*CY) % 256:(i*CY) % 256 + CY, (i*CY)//256*128:(i*CY)//256*128 + 128] + forcing[k, i])


def mid_kernel(bnd, ctl, cell, pos, slot, order, first, place, wire, wind, forcing, visc, mid, wire_out, val, acc, s, keys):
    wire = wire()
    from_wire(pos(), wire, val)
    scatter_add(bnd, cell(), val, acc)
    wind, forcing, out = wind(), forcing(), mid
    mid = out.ref
    CY = wind.shape[2]

    def emit(k, i, u, f):
        mid[k, i*CY:(i+1)*CY, :] = u + neutral_step * f

    tend_all(wind, forcing, visc, wire, acc, emit)
    put_edges(mid, wire_out)
    lookup(ctl, slot, order, first, place, mid, wire_out, s, keys, hook=out.send)


def end_kernel(bnd, cell, pos, wire, start, wind, forcing, visc, out, val, acc):
    wire = wire()
    from_wire(pos(), wire, val)
    scatter_add(bnd, cell(), val, acc)
    wind, forcing, start = wind(), forcing(), start()

    def emit(k, i, u, f):
        out[k, i] = 0.5 * (start[k, i] + u) + (0.5 * neutral_step) * f

    tend_all(wind, forcing, visc, wire, acc, emit)


class Incoming:
    def __init__(self, src, dst, sem):
        self.ref, self.copy, self.due = dst, pltpu.make_async_copy(src, dst, sem), True
        self.copy.start()

    def __call__(self):
        if self.due:
            self.due = False
            self.copy.wait()
        return self.ref


class Outgoing:
    def __init__(self, dst, src, sem):
        self.ref, self.copy, self.sent = src, pltpu.make_async_copy(src, dst, sem), False

    def send(self):
        self.sent = True
        self.copy.start()


def call(kernel, outs, scratch, *args, smem=1, early=(), late=(), name=None):
    single = not isinstance(outs, tuple)
    outs = (outs,) if single else outs
    early, late = list(early), list(late)
    anywhere = pl.BlockSpec(memory_space=pl.ANY)
    moved = [pltpu.VMEM(args[i].shape, args[i].dtype) for i in early]
    moved += [pltpu.VMEM(outs[i].shape, outs[i].dtype) for i in late]
    count = len(moved)

    def body(*refs):
        ins = list(refs[:len(args)])
        made = list(refs[len(args):len(args)+len(outs)])
        rest = refs[len(args)+len(outs):]
        own, bufs = rest[:len(scratch)], rest[len(scratch):]
        for n, i in enumerate(early):
            ins[i] = Incoming(ins[i], bufs[n], bufs[count].at[n])
        for n, i in enumerate(late, len(early)):
            made[i] = Outgoing(made[i], bufs[n], bufs[count].at[n])
        kernel(*ins, *made, *own)
        for i in early:
            ins[i]()
        for i in late:
            if not made[i].sent:
                made[i].send()
            made[i].copy.wait()

    result = pl.pallas_call(
        body,
        out_shape=outs,
        in_specs=[SM if i < smem else anywhere if i in early else VM for i in range(len(args))],
        out_specs=tuple(anywhere if i in late else VM for i in range(len(outs))),
        scratch_shapes=list(scratch) + moved + ([pltpu.SemaphoreType.DMA((count,))] if count else []),
        name=name,
    )(*args)
    return result[0] if single else result


def tied(*arrays):
    return lax.optimization_barrier(arrays)


def exchange(x):
    x = x.reshape(128, 3, 2, 128)
    return lax.all_to_all(x, ("gx", "gy"), split_axis=0, concat_axis=0, tiled=True).reshape(768, 128)


def per_device(
    neutral_wind,
    forcing,
    ion_density,
    inverse,
    drift_fraction,
    viscosity,
    coupling,
    drag_rate,
    outgoing_column,
    send_level,
    recv_tube,
    recv_point,
    recv_weight,
    pair_count,
):
    visc = viscosity[None, :]
    sd = jax.ShapeDtypeStruct
    wire_t = sd((768, 128), f32)
    tube_t = sd(ion_density.shape, f32)
    vals = pltpu.VMEM((2, 256, 128), f32)
    accs = pltpu.VMEM((2, 256 + W, 256), f32)
    tabs = pltpu.VMEM((2, 512, 128), f32)
    flat = (2, 512, 128)
    up_route = [(i, i + 1) for i in range(lax.axis_size("gy") - 1)]
    side_t = (sd((256, 128), i32), sd((128, 256), i32), sd((32, 128), i32), sd((1024, 128), i32))
    side_t += (sd((128, 256), i32), sd((128, 128), i32), sd((128, 256), i32), sd((8, 128), i32))
    seek = [pltpu.VMEM((2, 1024, 128), f32), pltpu.VMEM((1024, 128), i32)]

    cA, pA, bA, *gA, ctA, wire = call(
        first_kernel, side_t + (wire_t,), seek + [pltpu.SMEM((8, 128), i32), pltpu.SemaphoreType.DMA],
        outgoing_column, send_level, neutral_wind.reshape(flat), smem=0, early=(2,), late=(0, 1, 3, 4, 5, 6), name="first")
    came = exchange(wire)
    wire, tub = tied(wire, recv_tube)
    cB, pB, bB, *gB, ctB, gain, drift = call(
        tube_sort_kernel, side_t + (sd((128, 256), f32), sd((128, 128), f32)), [],
        tub, recv_point, recv_weight, pair_count, drift_fraction[None, :], smem=0, name="tubesort")

    def tubes(came, ions, last):
        w, smooth, out_last, edge = call(
            tube_kernel, (tube_t, tube_t, sd((2, 1, 512), f32), sd((2, 128, 128), f32)), [vals, accs],
            bB, coupling, cB, pB, gain, drift, came, ions, inverse, smem=2, early=(6, 3, 4, 2, 7, 8, 5), late=(0, 3), name="tube")
        up = lax.ppermute(out_last, "gy", up_route)
        return call(
            lambda *a: drag_kernel(last, *a), (tube_t, wire_t), [tabs] + seek,
            ctB, drag_rate, *gB, gain, drift, w, smooth, up, ion_density if last else up, edge, smem=2,
            early=(9, 8) + ((11,) if last else ()) + (7, 2, 12, 5, 6, 3, 4), late=(0,), name="drag")

    n1, wire = tubes(came, ion_density, False)
    mid, wire = call(
        mid_kernel, (sd(flat, f32), wire_t), [vals, accs] + seek,
        bA, ctA, cA, pA, *gA, exchange(wire), neutral_wind, forcing, visc, smem=2,
        early=(8, 3, 2, 9, 10, 4, 7, 5, 6), late=(0,), name="mid")
    ion_out, wire = tubes(exchange(wire), n1, True)
    wind_out = call(
        end_kernel, sd(neutral_wind.shape, f32), [vals, accs],
        bA, cA, pA, exchange(wire), neutral_wind, mid.reshape(neutral_wind.shape), forcing, visc, early=(3, 2, 1, 5, 6, 4), name="end")
    return (wind_out, ion_out)


def solution(mesh):
    placed = (
        P(None, "gx", "gy", None),
        P(None, "gx", "gy", None),
        P(None, ("gx", "gy"), None),
        P("gx", None, None, None),
        P(("gx", "gy")),
        P(),
        P(),
        P(),
        P(("gx", "gy"), None, None),
        P(("gx", "gy"), None, None),
        P(("gx", "gy"), None, None),
        P(("gx", "gy"), None, None),
        P(("gx", "gy"), None, None),
        P(),
    )
    return jax.shard_map(
        per_device,
        mesh=mesh,
        in_specs=placed,
        out_specs=(P(None, "gx", "gy", None), P(None, ("gx", "gy"), None)),
        check_vma=False,
    )
```

```python
import jax
import jax.numpy as jnp
from jax import lax
from jax.experimental import pallas as pl
from jax.experimental.pallas import tpu as pltpu
from jax.sharding import PartitionSpec as P

i32, f32, bf16 = jnp.int32, jnp.float32, jnp.bfloat16
VM = pl.BlockSpec(memory_space=pltpu.VMEM)
SM = pl.BlockSpec(memory_space=pltpu.SMEM)
W, NB, UN, GB, LIMIT = 80, 16, 2, 16, 24
neutral_step = 0.4
ion_factor = 0.5


def bitonic(x):
    n, L = x.shape
    x = x.reshape(n//8, 8, L)
    sub = lax.broadcasted_iota(i32, (1, 8, L), 1)
    k = 2
    while k <= n:
        d = k//2
        while d >= 1:
            if d >= 8:
                dv = d//8
                y = x.reshape(n//(16*dv), 2, dv, 8, L)
                a, b = y[:, 0], y[:, 1]
                lo, hi = jnp.minimum(a, b), jnp.maximum(a, b)
                parts = []
                for g in range(n//(16*dv)):
                    up = ((g*2*d) & k) == 0
                    parts += [lo[g], hi[g]] if up else [hi[g], lo[g]]
                x = jnp.concatenate(parts, axis=0)
            else:
                up_r = pltpu.roll(x, 8-d, 1)
                dn_r = pltpu.roll(x, d, 1)
                first = (sub & d) == 0
                p = jnp.where(first, up_r, dn_r)
                mn, mx = jnp.minimum(x, p), jnp.maximum(x, p)
                if k >= 8:
                    if k == 8:
                        vi = lax.broadcasted_iota(i32, (n//8, 1, 1), 0)
                    parts = []
                    xs = []
                    take_min_up = first
                    kv = k//8
                    for g in range(0, n//8, kv):
                        up = (g*8 & k) == 0
                        sel = first if up else jnp.logical_not(first)
                        xs.append(jnp.where(sel, mn[g:g+kv], mx[g:g+kv]))
                    x = jnp.concatenate(xs, axis=0) if len(xs) > 1 else xs[0]
                else:
                    up = (sub & k) == 0
                    sel = first == up
                    x = jnp.where(sel, mn, mx)
            d //= 2
        k *= 2
    return x.reshape(n, L)

def row_of(r, start=0, count=128):
    return pl.ds(6*start + r, count, stride=6)


def take(x, idx):
    return jnp.take_along_axis(x, idx, axis=1, mode="promise_in_bounds")


def take2(x, idx):
    low = idx & 127
    return jnp.where(idx < 128, take(x[:, :128], low), take(x[:, 128:], low))


def slot_tile(order, first, turn, j, slots):
    lane = lax.broadcasted_iota(i32, (128, 128), 1)
    idx = take(first[...], 8*j + (lane >> 4)) + 16*turn + (lane & 15)
    slots[pl.ds(pl.multiple_of(j*128, 128), 128), :] = (take2(order, jnp.minimum(idx, 255)) & 1023).T


def sort_side(key16, cell_ref, pos_ref, bnd_ref, slot_ref, order_ref, first_ref, place_ref, ctl_ref):
    P, C = key16.shape
    c = lax.broadcasted_iota(i32, (P, C), 1)
    s = bitonic((key16 * 256 + c).astype(f32).T).astype(i32)
    cell = s >> 8
    cell_ref[...] = cell
    pos = (s & 255).T
    pos_ref[...] = pos
    row = (cell >> 7).reshape(C//8, 8, P)
    lo = jnp.min(jnp.min(row, axis=1), axis=1, keepdims=True)
    hi = jnp.max(jnp.max(row, axis=1), axis=1, keepdims=True)
    lane = lax.broadcasted_iota(i32, (C//8, 128), 1)
    bnd_ref[...] = jnp.where(lane == 0, lo, hi)
    order = cell.T
    order_ref[...] = order
    lane = lax.broadcasted_iota(i32, (P, 128), 1)
    first = jnp.zeros((P, 128), i32)
    for step in (128, 64, 32, 16, 8, 4, 2, 1, 1):
        probe = first + step
        first = jnp.where(take2(order, probe - 1) < lane*1024, probe, first)
    first_ref[...] = first
    most = jnp.max((pltpu.roll(first, 127, 1) - first).astype(f32), axis=0, keepdims=True)
    most = jnp.where(lane[:1] < 64, most, 0.0)
    top = jnp.broadcast_to(jnp.max(most, axis=1, keepdims=True), (1, 128))
    ctl_ref[...] = jnp.broadcast_to(jnp.where(lane[:1] < 64, most, top), (8, 128)).astype(i32)
    for j in range(8):
        slot_tile(order, first_ref, 0, j, slot_ref)
    b = order >> 10
    w = c - jnp.concatenate([take(first, b[:, :128]), take(first, b[:, 128:])], axis=1)
    place = (pos << 14) + ((w >> 4) << 10) + (b << 4) + (w & 15)
    place_ref[...] = (bitonic(place.astype(f32).T).astype(i32) & 16383).T


def cell_key(row, lane):
    return ((row & 255) << 8) + ((row >> 8) << 7) + lane


def put_edges(t, wire):
    CX, CY = 16, t.shape[1] // 16
    for k in range(2):
        wire[row_of(4, k*CY, CY), :] = t[k, (CX-1)*CY:CX*CY, :]
        wire[row_of(4, (2+k)*CY, CY), :] = t[k, :CY, :]
        for i in range(CX):
            for q, at in ((k*CX+i, (i+1)*CY-1), ((2+k)*CX+i, i*CY)):
                wire[6*q+5:6*q+6, :] = t[k, at:at+1, :]
    wire[row_of(5, 4*CX, 128 - 4*CX), :] = jnp.zeros((128 - 4*CX, 128), f32)


def place_of():
    x, y = lax.axis_index("gx"), lax.axis_index("gy")
    return x, y, x * lax.axis_size("gy") + y


def pass_edges(wire, out):
    q = place_of()[2]
    step = lax.axis_size("gy")
    for r, (cut, d) in enumerate(((64, step), (32, 1))):
        x = wire[row_of(4+r), :]
        out[r] = jnp.where(q < cut, pltpu.roll(x, d, 0), pltpu.roll(x, 128-d, 0))


def beside_tile(wire):
    x, y = place_of()[:2]
    a, b = wire[row_of(4), :], wire[row_of(5, 0, 64), :]
    return (
        jnp.where(x > 0, a[:64], 0.0),
        jnp.where(x < lax.axis_size("gx") - 1, a[64:], 0.0),
        jnp.where(y > 0, b[:32], 0.0),
        jnp.where(y < lax.axis_size("gy") - 1, b[32:], 0.0),
    )


def tube_sort_kernel(tub, pnt, weight, count, drift, *outs):
    side, gain, drift_out = outs[:8], outs[8], outs[9]
    p = pnt[0]
    sort_side(cell_key((p >> 7)*128 + tub[0], p & 127), *side)
    own = place_of()[2]
    lane = lax.broadcasted_iota(i32, (128, 128), 1)
    live = jnp.sum(jnp.where(lane == own, count[...], 0).astype(f32), axis=1, keepdims=True)
    c = lax.broadcasted_iota(i32, (128, 256), 1).astype(f32)
    gain[...] = jnp.where(c < live, weight[0], 0.0)
    drift_out[...] = jnp.broadcast_to(drift[...], (128, 128)).T


def permute_lanes(x, idx):
    return [take2(x, idx[:, :128]), take2(x, idx[:, 128:])]


def lookup(ctl, slot, order, first, place, t_ref, wire, s_ref, key_ref, gain=None, limit_copy=None):
    half = t_ref.shape[1] // 2

    def group(at_bucket, count, keys):
        for b in range(count):
            rows = []
            for j in range(8):
                at = at_bucket*4 + 4*b + j//2 + (j % 2)*half
                rows.append([jnp.broadcast_to(t_ref[k, pl.ds(at, 1), :], (8, 128)) for k in range(2)])
            for i in range(2):
                sl = pl.ds(pl.multiple_of(at_bucket*16 + b*16 + i*8, 8), 8)
                key = keys[sl, :]
                sub, lev = key >> 7, key & 127
                acc = [take(rows[0][k], lev) for k in range(2)]
                for j in range(1, 8):
                    m = sub == j
                    for k in range(2):
                        acc[k] = jnp.where(m, take(rows[j][k], lev), acc[k])
                for k in range(2):
                    s_ref[k, sl, :] = acc[k]

    def each(g, _):
        group(g*GB, GB, slot)
        return 0

    def scaled(x, h):
        return x if gain is None else x * gain[:, h*128:(h+1)*128]

    lax.fori_loop(0, 64//GB, each, 0)
    if limit_copy is not None:
        limit_copy.start()
    parts = [[s_ref[k, j*128:(j+1)*128, :].T for j in range(8)] for k in range(2)]
    for h in range(2):
        at = place[:, h*128:(h+1)*128]
        low, tile = at & 127, (at >> 7) & 7
        for k in range(2):
            x = take(parts[k][0], low)
            for j in range(1, 8):
                x = jnp.where(tile == j, take(parts[k][j], low), x)
            wire[row_of(2*k+h), :] = scaled(x, h)

    def turn(t, _):
        def late(g, _):
            most = ctl[0, 8*g]
            for b in range(1, 8):
                most = jnp.maximum(most, ctl[0, 8*g + b])

            @pl.when(most > 16*t)
            def _():
                slot_tile(order[...], first, t, g, key_ref)
                group(g*8, 8, key_ref)
                tile = pl.ds(pl.multiple_of(g*128, 128), 128)
                for h in range(2):
                    at = place[:, h*128:(h+1)*128]
                    mine = (at >> 7) == 8*t + g
                    for k in range(2):
                        x = take(s_ref[k, tile, :].T, at & 127)
                        wire[row_of(2*k+h), :] = jnp.where(mine, scaled(x, h), wire[row_of(2*k+h), :])
            return 0

        lax.fori_loop(0, 8, late, 0)
        return 0

    if limit_copy is not None:
        limit_copy.wait()
    lax.fori_loop(1, (ctl[0, 64] + 15) // 16, turn, 0)


def scatter_add(bnd, cell_ref, val_ref, acc_ref):
    acc_ref[...] = jnp.zeros_like(acc_ref)
    iota = lax.broadcasted_iota(i32, (256, 128), 0).astype(f32).astype(bf16)
    one, zero = jnp.ones((256, 128), bf16), jnp.zeros((256, 128), bf16)

    def spread(x, n):
        return jnp.broadcast_to(x, (n, 128)).astype(bf16)

    def begin(v):
        return ((bnd[v*(NB//8), 0] >> 1) // 8) * 8

    def window(v, rb):
        rb = pl.multiple_of(rb, 8)
        sl = pl.ds(pl.multiple_of(v*NB, 8), NB)
        key = cell_ref[sl, :]
        rel, lane = ((key >> 8) - rb).astype(f32), (key & 255).astype(f32)
        vals = []
        for k in range(2):
            x = val_ref[k, sl, :]
            h = x.astype(bf16).astype(f32)
            vals += [h, x - h]
        rows, lanes = [], []
        for r in range(NB):
            lanes.append(jnp.where(iota == spread(lane[r:r+1], 256), one, zero))
            m = iota[:W] == spread(rel[r:r+1], W)
            rows.append(jnp.concatenate([jnp.where(m, spread(x[r:r+1], W), zero[:W]) for x in vals], axis=0))
        z = lax.dot_general(
            jnp.concatenate(rows, axis=1), jnp.concatenate(lanes, axis=1),
            (((1,), (1,)), ((), ())), preferred_element_type=f32)
        for k in range(2):
            acc_ref[k, pl.ds(rb, W), :] += z[2*k*W:(2*k+1)*W] + z[(2*k+1)*W:(2*k+2)*W]

    def block(v, _):
        window(v, begin(v))
        return 0

    def rest(v, _):
        base = begin(v)

        def more(it, _):
            window(v, base + it*W)
            return 0

        return lax.fori_loop(1, ((bnd[(v+1)*(NB//8) - 1, 1] >> 1) - base)//W + 1, more, 0)

    lax.fori_loop(0, 256//NB, block, 0, unroll=UN)
    lax.fori_loop(0, 256//NB, rest, 0)


def from_wire(pos, wire, val, gain=None):
    for k in range(2):
        x = [wire[row_of(2*k+h), :] for h in range(2)]
        if gain is not None:
            x = [x[h] * gain[:, h*128:(h+1)*128] for h in range(2)]
        o = permute_lanes(jnp.concatenate(x, axis=1), pos[...])
        val[k, :128, :] = o[0].T
        val[k, 128:, :] = o[1].T


def first_kernel(col, lev, t, *refs):
    side, wire, s, keys, limits, sem = refs[:8], refs[8], *refs[9:]
    sort_side(cell_key(col[0], lev[0]), *side)
    copy = pltpu.make_async_copy(side[7], limits, sem)
    put_edges(t, wire)
    lookup(limits, *side[3:7], t, wire, s, keys, limit_copy=copy)


def tube_kernel(bnd, coupling, cell, pos, gain, drift, wire, ions, inverse, w_out, smooth_out, last_out, edge_out, val, acc):
    pass_edges(wire, edge_out)
    from_wire(pos, wire, val, gain)
    scatter_add(bnd, cell, val, acc)
    w = []
    for k in range(2):
        for j in range(4):
            w_out[k, :, j*128:(j+1)*128] = acc[k, (j%2)*128:(j%2+1)*128, (j//2)*128:(j//2+1)*128]
    for k in range(2):
        n = ions[k]
        growth = coupling[k, 0] * w_out[0] + coupling[k, 1] * w_out[1]
        rhs = n + ion_factor * n * growth
        mix = lax.dot_general(rhs.astype(bf16), inverse[0, k], (((1,), (0,)), ((), ())), preferred_element_type=f32)
        sm = rhs + mix
        smooth_out[k] = sm
        last_out[k] = drift[127:128, :1] * sm[127:128, :]


def drag_kernel(last, ctl, drag, slot, order, first_at, place, gain, drift, w, smooth, up, ions, edge, n_out, wire, t, s, keys):
    for r in range(2):
        wire[row_of(4+r), :] = edge[r]
    first = lax.broadcasted_iota(i32, (128, 128), 0) == 0
    d = drift[...]
    n = [[], []]
    for k in range(2):
        for j in range(4):
            sl = slice(j*128, (j+1)*128)
            sm = smooth[k, :, sl]
            out = d * sm
            inflow = jnp.where(first, jnp.broadcast_to(up[k, :, sl], (128, 128)), pltpu.roll(out, 1, 0))
            x = sm - out + inflow
            n[k].append(x)
            n_out[k, :, sl] = 0.5 * (ions[k, :, sl] + x) if last else x
    for j in range(4):
        f = -(drag[0] * n[0][j] + drag[1] * n[1][j])
        for k in range(2):
            t[k, j*128:(j+1)*128, :] = f * w[k, :, j*128:(j+1)*128]
    lookup(ctl, slot, order, first_at, place, t, wire, s, keys, gain)


def tend_all(wind, forcing, visc, wire, acc, emit):
    CX, CY = wind.shape[1], wind.shape[2]
    xlo, xhi, ylo, yhi = beside_tile(wire)
    sub = lax.broadcasted_iota(i32, (CY, 128), 0)
    lane = lax.broadcasted_iota(i32, (CY, 128), 1)
    v = jnp.broadcast_to(visc[...], (CY, 128))
    for k in range(2):
        for i in range(CX):
            u = wind[k, i]
            b = (wind[k, i+1] if i < CX-1 else xhi[k*CY:(k+1)*CY]) + (wind[k, i-1] if i > 0 else xlo[k*CY:(k+1)*CY])
            nxt = jnp.where(sub == CY-1, jnp.broadcast_to(yhi[k*CX+i:k*CX+i+1], (CY, 128)), pltpu.roll(u, CY-1, 0))
            prv = jnp.where(sub == 0, jnp.broadcast_to(ylo[k*CX+i:k*CX+i+1], (CY, 128)), pltpu.roll(u, 1, 0))
            b = b + nxt + prv
            b = b + jnp.where(lane == 127, 0.0, pltpu.roll(u, 127, 1)) + jnp.where(lane == 0, 0.0, pltpu.roll(u, 1, 1))
            emit(k, i, u, v * (b - 6.0 * u) + acc[k, (i*CY) % 256:(i*CY) % 256 + CY, (i*CY)//256*128:(i*CY)//256*128 + 128] + forcing[k, i])


def mid_kernel(bnd, ctl, cell, pos, slot, order, first, place, wire, wind, forcing, visc, mid, wire_out, val, acc, s, keys):
    from_wire(pos, wire, val)
    scatter_add(bnd, cell, val, acc)
    CY = wind.shape[2]

    def emit(k, i, u, f):
        mid[k, i*CY:(i+1)*CY, :] = u + neutral_step * f

    tend_all(wind, forcing, visc, wire, acc, emit)
    put_edges(mid, wire_out)
    lookup(ctl, slot, order, first, place, mid, wire_out, s, keys)


def end_kernel(bnd, cell, pos, wire, start, wind, forcing, visc, out, val, acc):
    from_wire(pos, wire, val)
    scatter_add(bnd, cell, val, acc)

    def emit(k, i, u, f):
        out[k, i] = 0.5 * (start[k, i] + u) + (0.5 * neutral_step) * f

    tend_all(wind, forcing, visc, wire, acc, emit)


def call(kernel, outs, scratch, *args, smem=1, name=None):
    return pl.pallas_call(
        kernel,
        out_shape=outs,
        in_specs=[SM] * smem + [VM] * (len(args) - smem),
        out_specs=jax.tree.map(lambda _: VM, outs),
        scratch_shapes=scratch,
        compiler_params=pltpu.CompilerParams(vmem_limit_bytes=LIMIT << 20),
        name=name,
    )(*args)


def tied(*arrays):
    return lax.optimization_barrier(arrays)


def exchange(x):
    x = x.reshape(128, 3, 2, 128)
    return lax.all_to_all(x, ("gx", "gy"), split_axis=0, concat_axis=0, tiled=True).reshape(768, 128)


def per_device(
    neutral_wind,
    forcing,
    ion_density,
    inverse,
    drift_fraction,
    viscosity,
    coupling,
    drag_rate,
    outgoing_column,
    send_level,
    recv_tube,
    recv_point,
    recv_weight,
    pair_count,
):
    visc = viscosity[None, :]
    sd = jax.ShapeDtypeStruct
    wire_t = sd((768, 128), f32)
    tube_t = sd(ion_density.shape, f32)
    vals = pltpu.VMEM((2, 256, 128), f32)
    accs = pltpu.VMEM((2, 256 + W, 256), f32)
    tabs = pltpu.VMEM((2, 512, 128), f32)
    flat = (2, 512, 128)
    up_route = [(i, i + 1) for i in range(lax.axis_size("gy") - 1)]
    side_t = (sd((256, 128), i32), sd((128, 256), i32), sd((32, 128), i32), sd((1024, 128), i32))
    side_t += (sd((128, 256), i32), sd((128, 128), i32), sd((128, 256), i32), sd((8, 128), i32))
    seek = [pltpu.VMEM((2, 1024, 128), f32), pltpu.VMEM((1024, 128), i32)]

    cA, pA, bA, *gA, ctA, wire = call(
        first_kernel, side_t + (wire_t,), seek + [pltpu.SMEM((8, 128), i32), pltpu.SemaphoreType.DMA],
        outgoing_column, send_level, neutral_wind.reshape(flat), smem=0, name="first")
    came = exchange(wire)
    wire, tub = tied(wire, recv_tube)
    cB, pB, bB, *gB, ctB, gain, drift = call(
        tube_sort_kernel, side_t + (sd((128, 256), f32), sd((128, 128), f32)), [],
        tub, recv_point, recv_weight, pair_count, drift_fraction[None, :], smem=0, name="tubesort")

    def tubes(came, ions, last):
        w, smooth, out_last, edge = call(
            tube_kernel, (tube_t, tube_t, sd((2, 1, 512), f32), sd((2, 128, 128), f32)), [vals, accs],
            bB, coupling, cB, pB, gain, drift, came, ions, inverse, smem=2, name="tube")
        up = lax.ppermute(out_last, "gy", up_route)
        return call(
            lambda *a: drag_kernel(last, *a), (tube_t, wire_t), [tabs] + seek,
            ctB, drag_rate, *gB, gain, drift, w, smooth, up, ion_density, edge, smem=2, name="drag")

    n1, wire = tubes(came, ion_density, False)
    mid, wire = call(
        mid_kernel, (sd(flat, f32), wire_t), [vals, accs] + seek,
        bA, ctA, cA, pA, *gA, exchange(wire), neutral_wind, forcing, visc, smem=2, name="mid")
    ion_out, wire = tubes(exchange(wire), n1, True)
    wind_out = call(
        end_kernel, sd(neutral_wind.shape, f32), [vals, accs],
        bA, cA, pA, exchange(wire), neutral_wind, mid.reshape(neutral_wind.shape), forcing, visc, name="end")
    return (wind_out, ion_out)


def solution(mesh):
    placed = (
        P(None, "gx", "gy", None),
        P(None, "gx", "gy", None),
        P(None, ("gx", "gy"), None),
        P("gx", None, None, None),
        P(("gx", "gy")),
        P(),
        P(),
        P(),
        P(("gx", "gy"), None, None),
        P(("gx", "gy"), None, None),
        P(("gx", "gy"), None, None),
        P(("gx", "gy"), None, None),
        P(("gx", "gy"), None, None),
        P(),
    )
    return jax.shard_map(
        per_device,
        mesh=mesh,
        in_specs=placed,
        out_specs=(P(None, "gx", "gy", None), P(None, ("gx", "gy"), None)),
        check_vma=False,
    )
```

```python
import jax
import jax.numpy as jnp
from jax import lax
from jax.experimental import pallas as pl
from jax.experimental.pallas import tpu as pltpu
from jax.sharding import PartitionSpec as P

i32, f32, bf16 = jnp.int32, jnp.float32, jnp.bfloat16
VM = pl.BlockSpec(memory_space=pltpu.VMEM)
SM = pl.BlockSpec(memory_space=pltpu.SMEM)
W, NB, UN, GB = 80, 16, 2, 16
LIMITS = {"first": None, "tubesort": 24, "tube0": 24, "drag0": 24, "mid": 24, "tube1": 24, "drag1": 24, "end": 24}
neutral_step = 0.4
ion_factor = 0.5


def bitonic(x):
    n, L = x.shape
    x = x.reshape(n//8, 8, L)
    sub = lax.broadcasted_iota(i32, (1, 8, L), 1)
    k = 2
    while k <= n:
        d = k//2
        while d >= 1:
            if d >= 8:
                dv = d//8
                y = x.reshape(n//(16*dv), 2, dv, 8, L)
                a, b = y[:, 0], y[:, 1]
                lo, hi = jnp.minimum(a, b), jnp.maximum(a, b)
                parts = []
                for g in range(n//(16*dv)):
                    up = ((g*2*d) & k) == 0
                    parts += [lo[g], hi[g]] if up else [hi[g], lo[g]]
                x = jnp.concatenate(parts, axis=0)
            else:
                up_r = pltpu.roll(x, 8-d, 1)
                dn_r = pltpu.roll(x, d, 1)
                first = (sub & d) == 0
                p = jnp.where(first, up_r, dn_r)
                mn, mx = jnp.minimum(x, p), jnp.maximum(x, p)
                if k >= 8:
                    if k == 8:
                        vi = lax.broadcasted_iota(i32, (n//8, 1, 1), 0)
                    parts = []
                    xs = []
                    take_min_up = first
                    kv = k//8
                    for g in range(0, n//8, kv):
                        up = (g*8 & k) == 0
                        sel = first if up else jnp.logical_not(first)
                        xs.append(jnp.where(sel, mn[g:g+kv], mx[g:g+kv]))
                    x = jnp.concatenate(xs, axis=0) if len(xs) > 1 else xs[0]
                else:
                    up = (sub & k) == 0
                    sel = first == up
                    x = jnp.where(sel, mn, mx)
            d //= 2
        k *= 2
    return x.reshape(n, L)

def row_of(r, start=0, count=128):
    return pl.ds(6*start + r, count, stride=6)


def take(x, idx):
    return jnp.take_along_axis(x, idx, axis=1, mode="promise_in_bounds")


def take2(x, idx):
    low = idx & 127
    return jnp.where(idx < 128, take(x[:, :128], low), take(x[:, 128:], low))


def slot_tile(order, first, turn, j, slots):
    lane = lax.broadcasted_iota(i32, (128, 128), 1)
    idx = take(first[...], 8*j + (lane >> 4)) + 16*turn + (lane & 15)
    slots[pl.ds(pl.multiple_of(j*128, 128), 128), :] = (take2(order, jnp.minimum(idx, 255)) & 1023).T


def sort_side(key16, cell_ref, pos_ref, bnd_ref, slot_ref, order_ref, first_ref, place_ref, ctl_ref):
    P, C = key16.shape
    c = lax.broadcasted_iota(i32, (P, C), 1)
    s = bitonic((key16 * 256 + c).astype(f32).T).astype(i32)
    cell = s >> 8
    cell_ref[...] = cell
    pos = (s & 255).T
    pos_ref[...] = pos
    row = (cell >> 7).reshape(C//8, 8, P)
    lo = jnp.min(jnp.min(row, axis=1), axis=1, keepdims=True)
    hi = jnp.max(jnp.max(row, axis=1), axis=1, keepdims=True)
    lane = lax.broadcasted_iota(i32, (C//8, 128), 1)
    bnd_ref[...] = jnp.where(lane == 0, lo, hi)
    order = cell.T
    order_ref[...] = order
    lane = lax.broadcasted_iota(i32, (P, 128), 1)
    first = jnp.zeros((P, 128), i32)
    for step in (128, 64, 32, 16, 8, 4, 2, 1, 1):
        probe = first + step
        first = jnp.where(take2(order, probe - 1) < lane*1024, probe, first)
    first_ref[...] = first
    most = jnp.max((pltpu.roll(first, 127, 1) - first).astype(f32), axis=0, keepdims=True)
    most = jnp.where(lane[:1] < 64, most, 0.0)
    top = jnp.broadcast_to(jnp.max(most, axis=1, keepdims=True), (1, 128))
    ctl_ref[...] = jnp.broadcast_to(jnp.where(lane[:1] < 64, most, top), (8, 128)).astype(i32)
    for j in range(8):
        slot_tile(order, first_ref, 0, j, slot_ref)
    b = order >> 10
    w = c - jnp.concatenate([take(first, b[:, :128]), take(first, b[:, 128:])], axis=1)
    place = (pos << 14) + ((w >> 4) << 10) + (b << 4) + (w & 15)
    place_ref[...] = (bitonic(place.astype(f32).T).astype(i32) & 16383).T


def cell_key(row, lane):
    return ((row & 255) << 8) + ((row >> 8) << 7) + lane


def put_edges(t, wire):
    CX, CY = 16, t.shape[1] // 16
    for k in range(2):
        wire[row_of(4, k*CY, CY), :] = t[k, (CX-1)*CY:CX*CY, :]
        wire[row_of(4, (2+k)*CY, CY), :] = t[k, :CY, :]
        for i in range(CX):
            for q, at in ((k*CX+i, (i+1)*CY-1), ((2+k)*CX+i, i*CY)):
                wire[6*q+5:6*q+6, :] = t[k, at:at+1, :]
    wire[row_of(5, 4*CX, 128 - 4*CX), :] = jnp.zeros((128 - 4*CX, 128), f32)


def place_of():
    x, y = lax.axis_index("gx"), lax.axis_index("gy")
    return x, y, x * lax.axis_size("gy") + y


def pass_edges(wire, out):
    q = place_of()[2]
    step = lax.axis_size("gy")
    for r, (cut, d) in enumerate(((64, step), (32, 1))):
        x = wire[row_of(4+r), :]
        out[r] = jnp.where(q < cut, pltpu.roll(x, d, 0), pltpu.roll(x, 128-d, 0))


def beside_tile(wire):
    x, y = place_of()[:2]
    a, b = wire[row_of(4), :], wire[row_of(5, 0, 64), :]
    return (
        jnp.where(x > 0, a[:64], 0.0),
        jnp.where(x < lax.axis_size("gx") - 1, a[64:], 0.0),
        jnp.where(y > 0, b[:32], 0.0),
        jnp.where(y < lax.axis_size("gy") - 1, b[32:], 0.0),
    )


def tube_sort_kernel(tub, pnt, weight, count, drift, *outs):
    side, gain, drift_out = outs[:8], outs[8], outs[9]
    p = pnt[0]
    sort_side(cell_key((p >> 7)*128 + tub[0], p & 127), *side)
    own = place_of()[2]
    lane = lax.broadcasted_iota(i32, (128, 128), 1)
    live = jnp.sum(jnp.where(lane == own, count[...], 0).astype(f32), axis=1, keepdims=True)
    c = lax.broadcasted_iota(i32, (128, 256), 1).astype(f32)
    gain[...] = jnp.where(c < live, weight[0], 0.0)
    drift_out[...] = jnp.broadcast_to(drift[...], (128, 128)).T


def permute_lanes(x, idx):
    return [take2(x, idx[:, :128]), take2(x, idx[:, 128:])]


def lookup(ctl, slot, order, first, place, t_ref, wire, s_ref, key_ref, gain=None, limit_copy=None):
    half = t_ref.shape[1] // 2

    def group(at_bucket, count, keys):
        for b in range(count):
            rows = []
            for j in range(8):
                at = at_bucket*4 + 4*b + j//2 + (j % 2)*half
                rows.append([jnp.broadcast_to(t_ref[k, pl.ds(at, 1), :], (8, 128)) for k in range(2)])
            for i in range(2):
                sl = pl.ds(pl.multiple_of(at_bucket*16 + b*16 + i*8, 8), 8)
                key = keys[sl, :]
                sub, lev = key >> 7, key & 127
                acc = [take(rows[0][k], lev) for k in range(2)]
                for j in range(1, 8):
                    m = sub == j
                    for k in range(2):
                        acc[k] = jnp.where(m, take(rows[j][k], lev), acc[k])
                for k in range(2):
                    s_ref[k, sl, :] = acc[k]

    def each(g, _):
        group(g*GB, GB, slot)
        return 0

    def scaled(x, h):
        return x if gain is None else x * gain[:, h*128:(h+1)*128]

    lax.fori_loop(0, 64//GB, each, 0)
    if limit_copy is not None:
        limit_copy.start()
    parts = [[s_ref[k, j*128:(j+1)*128, :].T for j in range(8)] for k in range(2)]
    for h in range(2):
        at = place[:, h*128:(h+1)*128]
        low, tile = at & 127, (at >> 7) & 7
        for k in range(2):
            x = take(parts[k][0], low)
            for j in range(1, 8):
                x = jnp.where(tile == j, take(parts[k][j], low), x)
            wire[row_of(2*k+h), :] = scaled(x, h)

    def turn(t, _):
        def late(g, _):
            most = ctl[0, 8*g]
            for b in range(1, 8):
                most = jnp.maximum(most, ctl[0, 8*g + b])

            @pl.when(most > 16*t)
            def _():
                slot_tile(order[...], first, t, g, key_ref)
                group(g*8, 8, key_ref)
                tile = pl.ds(pl.multiple_of(g*128, 128), 128)
                for h in range(2):
                    at = place[:, h*128:(h+1)*128]
                    mine = (at >> 7) == 8*t + g
                    for k in range(2):
                        x = take(s_ref[k, tile, :].T, at & 127)
                        wire[row_of(2*k+h), :] = jnp.where(mine, scaled(x, h), wire[row_of(2*k+h), :])
            return 0

        lax.fori_loop(0, 8, late, 0)
        return 0

    if limit_copy is not None:
        limit_copy.wait()
    else:
        ctl = ctl()
    lax.fori_loop(1, (ctl[0, 64] + 15) // 16, turn, 0)


def scatter_add(bnd, cell_ref, val_ref, acc_ref):
    bnd = bnd()
    acc_ref[...] = jnp.zeros_like(acc_ref)
    iota = lax.broadcasted_iota(i32, (256, 128), 0).astype(f32).astype(bf16)
    one, zero = jnp.ones((256, 128), bf16), jnp.zeros((256, 128), bf16)

    def spread(x, n):
        return jnp.broadcast_to(x, (n, 128)).astype(bf16)

    def begin(v):
        return ((bnd[v*(NB//8), 0] >> 1) // 8) * 8

    def window(v, rb):
        rb = pl.multiple_of(rb, 8)
        sl = pl.ds(pl.multiple_of(v*NB, 8), NB)
        key = cell_ref[sl, :]
        rel, lane = ((key >> 8) - rb).astype(f32), (key & 255).astype(f32)
        vals = []
        for k in range(2):
            x = val_ref[k, sl, :]
            h = x.astype(bf16).astype(f32)
            vals += [h, x - h]
        rows, lanes = [], []
        for r in range(NB):
            lanes.append(jnp.where(iota == spread(lane[r:r+1], 256), one, zero))
            m = iota[:W] == spread(rel[r:r+1], W)
            rows.append(jnp.concatenate([jnp.where(m, spread(x[r:r+1], W), zero[:W]) for x in vals], axis=0))
        z = lax.dot_general(
            jnp.concatenate(rows, axis=1), jnp.concatenate(lanes, axis=1),
            (((1,), (1,)), ((), ())), preferred_element_type=f32)
        for k in range(2):
            acc_ref[k, pl.ds(rb, W), :] += z[2*k*W:(2*k+1)*W] + z[(2*k+1)*W:(2*k+2)*W]

    def block(v, _):
        window(v, begin(v))
        return 0

    def rest(v, _):
        base = begin(v)

        def more(it, _):
            window(v, base + it*W)
            return 0

        return lax.fori_loop(1, ((bnd[(v+1)*(NB//8) - 1, 1] >> 1) - base)//W + 1, more, 0)

    lax.fori_loop(0, 256//NB, block, 0, unroll=UN)
    lax.fori_loop(0, 256//NB, rest, 0)


def from_wire(pos, wire, val, gain=None):
    for k in range(2):
        x = [wire[row_of(2*k+h), :] for h in range(2)]
        if gain is not None:
            x = [x[h] * gain[:, h*128:(h+1)*128] for h in range(2)]
        o = permute_lanes(jnp.concatenate(x, axis=1), pos[...])
        val[k, :128, :] = o[0].T
        val[k, 128:, :] = o[1].T


def first_kernel(col, lev, t, *refs):
    side, wire, s, keys, limits, sem = refs[:8], refs[8], *refs[9:]
    sort_side(cell_key(col[0], lev[0]), *side)
    copy = pltpu.make_async_copy(side[7], limits, sem)
    put_edges(t, wire)
    lookup(limits, *side[3:7], t, wire, s, keys, limit_copy=copy)


def tube_kernel(bnd, coupling, cell, pos, gain, drift, wire, ions, inverse, w_out, smooth_out, last_out, edge_out, val, acc):
    pass_edges(wire, edge_out)
    from_wire(pos, wire, val, gain)
    scatter_add(bnd, cell, val, acc)
    w = []
    for k in range(2):
        for j in range(4):
            w_out[k, :, j*128:(j+1)*128] = acc[k, (j%2)*128:(j%2+1)*128, (j//2)*128:(j//2+1)*128]
    coupling = coupling()
    for k in range(2):
        n = ions[k]
        growth = coupling[k, 0] * w_out[0] + coupling[k, 1] * w_out[1]
        rhs = n + ion_factor * n * growth
        mix = lax.dot_general(rhs.astype(bf16), inverse[0, k], (((1,), (0,)), ((), ())), preferred_element_type=f32)
        sm = rhs + mix
        smooth_out[k] = sm
        last_out[k] = drift[127:128, :1] * sm[127:128, :]


def drag_kernel(last, ctl, drag, slot, order, first_at, place, gain, drift, w, smooth, up, ions, edge, n_out, wire, t, s, keys):
    for r in range(2):
        wire[row_of(4+r), :] = edge[r]
    first = lax.broadcasted_iota(i32, (128, 128), 0) == 0
    d = drift[...]
    n = [[], []]
    for k in range(2):
        for j in range(4):
            sl = slice(j*128, (j+1)*128)
            sm = smooth[k, :, sl]
            out = d * sm
            inflow = jnp.where(first, jnp.broadcast_to(up[k, :, sl], (128, 128)), pltpu.roll(out, 1, 0))
            x = sm - out + inflow
            n[k].append(x)
            n_out[k, :, sl] = 0.5 * (ions[k, :, sl] + x) if last else x
    drag = drag()
    for j in range(4):
        f = -(drag[0] * n[0][j] + drag[1] * n[1][j])
        for k in range(2):
            t[k, j*128:(j+1)*128, :] = f * w[k, :, j*128:(j+1)*128]
    lookup(ctl, slot, order, first_at, place, t, wire, s, keys, gain)


def tend_all(wind, forcing, visc, wire, acc, emit):
    CX, CY = wind.shape[1], wind.shape[2]
    xlo, xhi, ylo, yhi = beside_tile(wire)
    sub = lax.broadcasted_iota(i32, (CY, 128), 0)
    lane = lax.broadcasted_iota(i32, (CY, 128), 1)
    v = jnp.broadcast_to(visc()[...], (CY, 128))
    for k in range(2):
        for i in range(CX):
            u = wind[k, i]
            b = (wind[k, i+1] if i < CX-1 else xhi[k*CY:(k+1)*CY]) + (wind[k, i-1] if i > 0 else xlo[k*CY:(k+1)*CY])
            nxt = jnp.where(sub == CY-1, jnp.broadcast_to(yhi[k*CX+i:k*CX+i+1], (CY, 128)), pltpu.roll(u, CY-1, 0))
            prv = jnp.where(sub == 0, jnp.broadcast_to(ylo[k*CX+i:k*CX+i+1], (CY, 128)), pltpu.roll(u, 1, 0))
            b = b + nxt + prv
            b = b + jnp.where(lane == 127, 0.0, pltpu.roll(u, 127, 1)) + jnp.where(lane == 0, 0.0, pltpu.roll(u, 1, 1))
            emit(k, i, u, v * (b - 6.0 * u) + acc[k, (i*CY) % 256:(i*CY) % 256 + CY, (i*CY)//256*128:(i*CY)//256*128 + 128] + forcing[k, i])


def mid_kernel(bnd, ctl, cell, pos, slot, order, first, place, wire, wind, forcing, visc, mid, wire_out, val, acc, s, keys):
    from_wire(pos, wire, val)
    scatter_add(bnd, cell, val, acc)
    CY = wind.shape[2]

    def emit(k, i, u, f):
        mid[k, i*CY:(i+1)*CY, :] = u + neutral_step * f

    tend_all(wind, forcing, visc, wire, acc, emit)
    put_edges(mid, wire_out)
    lookup(ctl, slot, order, first, place, mid, wire_out, s, keys)


def end_kernel(bnd, cell, pos, wire, start, wind, forcing, visc, out, val, acc):
    from_wire(pos, wire, val)
    scatter_add(bnd, cell, val, acc)

    def emit(k, i, u, f):
        out[k, i] = 0.5 * (start[k, i] + u) + (0.5 * neutral_step) * f

    tend_all(wind, forcing, visc, wire, acc, emit)


class Incoming:
    def __init__(self, src, dst, sem):
        self.ref, self.copy, self.due = dst, pltpu.make_async_copy(src, dst, sem), True
        self.copy.start()

    def __call__(self):
        if self.due:
            self.due = False
            self.copy.wait()
        return self.ref


def call(kernel, outs, scratch, *args, smem=(), vmem=(), limit=None, name=None):
    small = list(smem) + list(vmem)
    boxes = [pltpu.SMEM(args[i].shape, args[i].dtype) for i in smem]
    boxes += [pltpu.VMEM(args[i].shape, args[i].dtype) for i in vmem]
    boxes += [pltpu.SemaphoreType.DMA((len(small),))] if small else []

    def body(*refs):
        refs = list(refs)
        own = refs[len(refs) - len(boxes):]
        refs = refs[:len(refs) - len(boxes)]
        for n, i in enumerate(small):
            refs[i] = Incoming(refs[i], own[n], own[-1].at[n])
        kernel(*refs)
        for i in small:
            refs[i]()

    return pl.pallas_call(
        body,
        out_shape=outs,
        in_specs=[pl.BlockSpec(memory_space=pltpu.HBM) if i in small else VM for i in range(len(args))],
        out_specs=jax.tree.map(lambda _: VM, outs),
        scratch_shapes=list(scratch) + boxes,
        compiler_params=pltpu.CompilerParams(vmem_limit_bytes=limit and limit << 20),
        name=name,
    )(*args)


def tied(*arrays):
    return lax.optimization_barrier(arrays)


def exchange(x):
    x = x.reshape(128, 3, 2, 128)
    return lax.all_to_all(x, ("gx", "gy"), split_axis=0, concat_axis=0, tiled=True).reshape(768, 128)


def per_device(
    neutral_wind,
    forcing,
    ion_density,
    inverse,
    drift_fraction,
    viscosity,
    coupling,
    drag_rate,
    outgoing_column,
    send_level,
    recv_tube,
    recv_point,
    recv_weight,
    pair_count,
):
    visc = viscosity[None, :]
    sd = jax.ShapeDtypeStruct
    wire_t = sd((768, 128), f32)
    tube_t = sd(ion_density.shape, f32)
    vals = pltpu.VMEM((2, 256, 128), f32)
    accs = pltpu.VMEM((2, 256 + W, 256), f32)
    tabs = pltpu.VMEM((2, 512, 128), f32)
    flat = (2, 512, 128)
    up_route = [(i, i + 1) for i in range(lax.axis_size("gy") - 1)]
    side_t = (sd((256, 128), i32), sd((128, 256), i32), sd((32, 128), i32), sd((1024, 128), i32))
    side_t += (sd((128, 256), i32), sd((128, 128), i32), sd((128, 256), i32), sd((8, 128), i32))
    seek = [pltpu.VMEM((2, 1024, 128), f32), pltpu.VMEM((1024, 128), i32)]

    cA, pA, bA, *gA, ctA, wire = call(
        first_kernel, side_t + (wire_t,), seek + [pltpu.SMEM((8, 128), i32), pltpu.SemaphoreType.DMA],
        outgoing_column, send_level, neutral_wind.reshape(flat), limit=LIMITS["first"], name="first")
    came = exchange(wire)
    wire, tub = tied(wire, recv_tube)
    cB, pB, bB, *gB, ctB, gain, drift = call(
        tube_sort_kernel, side_t + (sd((128, 256), f32), sd((128, 128), f32)), [],
        tub, recv_point, recv_weight, pair_count, drift_fraction[None, :], limit=LIMITS["tubesort"], name="tubesort")

    def tubes(came, ions, last):
        w, smooth, out_last, edge = call(
            tube_kernel, (tube_t, tube_t, sd((2, 1, 512), f32), sd((2, 128, 128), f32)), [vals, accs],
            bB, coupling, cB, pB, gain, drift, came, ions, inverse, smem=(0, 1), limit=LIMITS["tube1" if last else "tube0"], name="tube")
        up = lax.ppermute(out_last, "gy", up_route)
        return call(
            lambda *a: drag_kernel(last, *a), (tube_t, wire_t), [tabs] + seek,
            ctB, drag_rate, *gB, gain, drift, w, smooth, up, ion_density if last else up, edge, smem=(0, 1), limit=LIMITS["drag1" if last else "drag0"], name="drag")

    n1, wire = tubes(came, ion_density, False)
    mid, wire = call(
        mid_kernel, (sd(flat, f32), wire_t), [vals, accs] + seek,
        bA, ctA, cA, pA, *gA, exchange(wire), neutral_wind, forcing, visc, smem=(0, 1), vmem=(11,), limit=LIMITS["mid"], name="mid")
    ion_out, wire = tubes(exchange(wire), n1, True)
    wind_out = call(
        end_kernel, sd(neutral_wind.shape, f32), [vals, accs],
        bA, cA, pA, exchange(wire), neutral_wind, mid.reshape(neutral_wind.shape), forcing, visc, smem=(0,), vmem=(7,), limit=LIMITS["end"], name="end")
    return (wind_out, ion_out)


def solution(mesh):
    placed = (
        P(None, "gx", "gy", None),
        P(None, "gx", "gy", None),
        P(None, ("gx", "gy"), None),
        P("gx", None, None, None),
        P(("gx", "gy")),
        P(),
        P(),
        P(),
        P(("gx", "gy"), None, None),
        P(("gx", "gy"), None, None),
        P(("gx", "gy"), None, None),
        P(("gx", "gy"), None, None),
        P(("gx", "gy"), None, None),
        P(),
    )
    return jax.shard_map(
        per_device,
        mesh=mesh,
        in_specs=placed,
        out_specs=(P(None, "gx", "gy", None), P(None, ("gx", "gy"), None)),
        check_vma=False,
    )
```

```python
import jax
import jax.numpy as jnp
from jax import lax
from jax.experimental import pallas as pl
from jax.experimental.pallas import tpu as pltpu
from jax.sharding import PartitionSpec as P

i32, f32, bf16 = jnp.int32, jnp.float32, jnp.bfloat16
VM = pl.BlockSpec(memory_space=pltpu.VMEM)
SM = pl.BlockSpec(memory_space=pltpu.SMEM)
W, NB, UN, GB = 72, 16, 4, 16
LIMITS = {"first": None, "tubesort": 24, "tube0": 24, "drag0": 24, "mid": 24, "tube1": 24, "drag1": 24, "end": 24}
neutral_step = 0.4
ion_factor = 0.5


def bitonic(x):
    n, L = x.shape
    x = x.reshape(n//8, 8, L)
    sub = lax.broadcasted_iota(i32, (1, 8, L), 1)
    k = 2
    while k <= n:
        d = k//2
        while d >= 1:
            if d >= 8:
                dv = d//8
                y = x.reshape(n//(16*dv), 2, dv, 8, L)
                a, b = y[:, 0], y[:, 1]
                lo, hi = jnp.minimum(a, b), jnp.maximum(a, b)
                parts = []
                for g in range(n//(16*dv)):
                    up = ((g*2*d) & k) == 0
                    parts += [lo[g], hi[g]] if up else [hi[g], lo[g]]
                x = jnp.concatenate(parts, axis=0)
            else:
                up_r = pltpu.roll(x, 8-d, 1)
                dn_r = pltpu.roll(x, d, 1)
                first = (sub & d) == 0
                p = jnp.where(first, up_r, dn_r)
                mn, mx = jnp.minimum(x, p), jnp.maximum(x, p)
                if k >= 8:
                    if k == 8:
                        vi = lax.broadcasted_iota(i32, (n//8, 1, 1), 0)
                    parts = []
                    xs = []
                    take_min_up = first
                    kv = k//8
                    for g in range(0, n//8, kv):
                        up = (g*8 & k) == 0
                        sel = first if up else jnp.logical_not(first)
                        xs.append(jnp.where(sel, mn[g:g+kv], mx[g:g+kv]))
                    x = jnp.concatenate(xs, axis=0) if len(xs) > 1 else xs[0]
                else:
                    up = (sub & k) == 0
                    sel = first == up
                    x = jnp.where(sel, mn, mx)
            d //= 2
        k *= 2
    return x.reshape(n, L)

def row_of(r, start=0, count=128):
    return pl.ds(6*start + r, count, stride=6)


def take(x, idx):
    return jnp.take_along_axis(x, idx, axis=1, mode="promise_in_bounds")


def take2(x, idx):
    low = idx & 127
    return jnp.where(idx < 128, take(x[:, :128], low), take(x[:, 128:], low))


def slot_tile(order, first, turn, j, slots):
    lane = lax.broadcasted_iota(i32, (128, 128), 1)
    idx = take(first[...], 8*j + (lane >> 4)) + 16*turn + (lane & 15)
    slots[pl.ds(pl.multiple_of(j*128, 128), 128), :] = (take2(order, jnp.minimum(idx, 255)) & 1023).T


def sort_side(key16, cell_ref, pos_ref, bnd_ref, slot_ref, order_ref, first_ref, place_ref, ctl_ref):
    P, C = key16.shape
    c = lax.broadcasted_iota(i32, (P, C), 1)
    s = bitonic((key16 * 256 + c).astype(f32).T).astype(i32)
    cell = s >> 8
    cell_ref[...] = cell
    pos = (s & 255).T
    pos_ref[...] = pos
    row = (cell >> 7).reshape(C//8, 8, P)
    lo = jnp.min(jnp.min(row, axis=1), axis=1, keepdims=True)
    hi = jnp.max(jnp.max(row, axis=1), axis=1, keepdims=True)
    lane = lax.broadcasted_iota(i32, (C//8, 128), 1)
    bnd_ref[...] = jnp.where(lane == 0, lo, hi)
    order = cell.T
    order_ref[...] = order
    lane = lax.broadcasted_iota(i32, (P, 128), 1)
    first = jnp.zeros((P, 128), i32)
    for step in (128, 64, 32, 16, 8, 4, 2, 1, 1):
        probe = first + step
        first = jnp.where(take2(order, probe - 1) < lane*1024, probe, first)
    first_ref[...] = first
    most = jnp.max((pltpu.roll(first, 127, 1) - first).astype(f32), axis=0, keepdims=True)
    most = jnp.where(lane[:1] < 64, most, 0.0)
    top = jnp.broadcast_to(jnp.max(most, axis=1, keepdims=True), (1, 128))
    ctl_ref[...] = jnp.broadcast_to(jnp.where(lane[:1] < 64, most, top), (8, 128)).astype(i32)
    for j in range(8):
        slot_tile(order, first_ref, 0, j, slot_ref)
    b = order >> 10
    w = c - jnp.concatenate([take(first, b[:, :128]), take(first, b[:, 128:])], axis=1)
    place = (pos << 14) + ((w >> 4) << 10) + (b << 4) + (w & 15)
    place_ref[...] = (bitonic(place.astype(f32).T).astype(i32) & 16383).T


def cell_key(row, lane):
    return ((row & 255) << 8) + ((row >> 8) << 7) + lane


def put_edges(t, wire):
    CX, CY = 16, t.shape[1] // 16
    for k in range(2):
        wire[row_of(4, k*CY, CY), :] = t[k, (CX-1)*CY:CX*CY, :]
        wire[row_of(4, (2+k)*CY, CY), :] = t[k, :CY, :]
        for i in range(CX):
            for q, at in ((k*CX+i, (i+1)*CY-1), ((2+k)*CX+i, i*CY)):
                wire[6*q+5:6*q+6, :] = t[k, at:at+1, :]
    wire[row_of(5, 4*CX, 128 - 4*CX), :] = jnp.zeros((128 - 4*CX, 128), f32)


def place_of():
    x, y = lax.axis_index("gx"), lax.axis_index("gy")
    return x, y, x * lax.axis_size("gy") + y


def pass_edges(wire, out):
    q = place_of()[2]
    step = lax.axis_size("gy")
    for r, (cut, d) in enumerate(((64, step), (32, 1))):
        x = wire[row_of(4+r), :]
        out[r] = jnp.where(q < cut, pltpu.roll(x, d, 0), pltpu.roll(x, 128-d, 0))


def beside_tile(wire):
    x, y = place_of()[:2]
    a, b = wire[row_of(4), :], wire[row_of(5, 0, 64), :]
    return (
        jnp.where(x > 0, a[:64], 0.0),
        jnp.where(x < lax.axis_size("gx") - 1, a[64:], 0.0),
        jnp.where(y > 0, b[:32], 0.0),
        jnp.where(y < lax.axis_size("gy") - 1, b[32:], 0.0),
    )


def tube_sort_kernel(tub, pnt, weight, count, drift, *outs):
    side, gain, drift_out = outs[:8], outs[8], outs[9]
    p = pnt[0]
    sort_side(cell_key((p >> 7)*128 + tub[0], p & 127), *side)
    own = place_of()[2]
    lane = lax.broadcasted_iota(i32, (128, 128), 1)
    live = jnp.sum(jnp.where(lane == own, count[...], 0).astype(f32), axis=1, keepdims=True)
    c = lax.broadcasted_iota(i32, (128, 256), 1).astype(f32)
    gain[...] = jnp.where(c < live, weight[0], 0.0)
    drift_out[...] = jnp.broadcast_to(drift[...], (128, 128)).T


def permute_lanes(x, idx):
    return [take2(x, idx[:, :128]), take2(x, idx[:, 128:])]


def lookup(ctl, slot, order, first, place, t_ref, wire, s_ref, key_ref, gain=None, limit_copy=None):
    half = t_ref.shape[1] // 2

    def group(at_bucket, count, keys):
        for b in range(count):
            rows = []
            for j in range(8):
                at = at_bucket*4 + 4*b + j//2 + (j % 2)*half
                rows.append([jnp.broadcast_to(t_ref[k, pl.ds(at, 1), :], (8, 128)) for k in range(2)])
            for i in range(2):
                sl = pl.ds(pl.multiple_of(at_bucket*16 + b*16 + i*8, 8), 8)
                key = keys[sl, :]
                sub, lev = key >> 7, key & 127
                acc = [take(rows[0][k], lev) for k in range(2)]
                for j in range(1, 8):
                    m = sub == j
                    for k in range(2):
                        acc[k] = jnp.where(m, take(rows[j][k], lev), acc[k])
                for k in range(2):
                    s_ref[k, sl, :] = acc[k]

    def each(g, _):
        group(g*GB, GB, slot)
        return 0

    def scaled(x, h):
        return x if gain is None else x * gain[:, h*128:(h+1)*128]

    lax.fori_loop(0, 64//GB, each, 0)
    if limit_copy is not None:
        limit_copy.start()
    parts = [[s_ref[k, j*128:(j+1)*128, :].T for j in range(8)] for k in range(2)]
    for h in range(2):
        at = place[:, h*128:(h+1)*128]
        low, tile = at & 127, (at >> 7) & 7
        for k in range(2):
            x = take(parts[k][0], low)
            for j in range(1, 8):
                x = jnp.where(tile == j, take(parts[k][j], low), x)
            wire[row_of(2*k+h), :] = scaled(x, h)

    def turn(t, _):
        def late(g, _):
            most = ctl[0, 8*g]
            for b in range(1, 8):
                most = jnp.maximum(most, ctl[0, 8*g + b])

            @pl.when(most > 16*t)
            def _():
                slot_tile(order[...], first, t, g, key_ref)
                group(g*8, 8, key_ref)
                tile = pl.ds(pl.multiple_of(g*128, 128), 128)
                for h in range(2):
                    at = place[:, h*128:(h+1)*128]
                    mine = (at >> 7) == 8*t + g
                    for k in range(2):
                        x = take(s_ref[k, tile, :].T, at & 127)
                        wire[row_of(2*k+h), :] = jnp.where(mine, scaled(x, h), wire[row_of(2*k+h), :])
            return 0

        lax.fori_loop(0, 8, late, 0)
        return 0

    if limit_copy is not None:
        limit_copy.wait()
    else:
        ctl = ctl()
    lax.fori_loop(1, (ctl[0, 64] + 15) // 16, turn, 0)


def scatter_add(bnd, cell_ref, val_ref, acc_ref):
    bnd = bnd()
    acc_ref[...] = jnp.zeros_like(acc_ref)
    iota = lax.broadcasted_iota(i32, (256, 128), 0).astype(f32).astype(bf16)
    one, zero = jnp.ones((256, 128), bf16), jnp.zeros((256, 128), bf16)

    def spread(x, n):
        return jnp.broadcast_to(x, (n, 128)).astype(bf16)

    def begin(v):
        return ((bnd[v*(NB//8), 0] >> 1) // 8) * 8

    def window(v, rb):
        rb = pl.multiple_of(rb, 8)
        sl = pl.ds(pl.multiple_of(v*NB, 8), NB)
        key = cell_ref[sl, :]
        rel, lane = ((key >> 8) - rb).astype(f32), (key & 255).astype(f32)
        vals = []
        for k in range(2):
            x = val_ref[k, sl, :]
            h = x.astype(bf16).astype(f32)
            vals += [h, x - h]
        rows, lanes = [], []
        for r in range(NB):
            lanes.append(jnp.where(iota == spread(lane[r:r+1], 256), one, zero))
            m = iota[:W] == spread(rel[r:r+1], W)
            rows.append(jnp.concatenate([jnp.where(m, spread(x[r:r+1], W), zero[:W]) for x in vals], axis=0))
        z = lax.dot_general(
            jnp.concatenate(rows, axis=1), jnp.concatenate(lanes, axis=1),
            (((1,), (1,)), ((), ())), preferred_element_type=f32)
        for k in range(2):
            acc_ref[k, pl.ds(rb, W), :] += z[2*k*W:(2*k+1)*W] + z[(2*k+1)*W:(2*k+2)*W]

    def block(v, _):
        window(v, begin(v))
        return 0

    def rest(v, _):
        base = begin(v)

        def more(it, _):
            window(v, base + it*W)
            return 0

        return lax.fori_loop(1, ((bnd[(v+1)*(NB//8) - 1, 1] >> 1) - base)//W + 1, more, 0)

    lax.fori_loop(0, 256//NB, block, 0, unroll=UN)
    lax.fori_loop(0, 256//NB, rest, 0)


def from_wire(pos, wire, val, gain=None):
    for k in range(2):
        x = [wire[row_of(2*k+h), :] for h in range(2)]
        if gain is not None:
            x = [x[h] * gain[:, h*128:(h+1)*128] for h in range(2)]
        o = permute_lanes(jnp.concatenate(x, axis=1), pos[...])
        val[k, :128, :] = o[0].T
        val[k, 128:, :] = o[1].T


def first_kernel(col, lev, t, *refs):
    side, wire, s, keys, limits, sem = refs[:8], refs[8], *refs[9:]
    sort_side(cell_key(col[0], lev[0]), *side)
    copy = pltpu.make_async_copy(side[7], limits, sem)
    put_edges(t, wire)
    lookup(limits, *side[3:7], t, wire, s, keys, limit_copy=copy)


def tube_kernel(bnd, coupling, cell, pos, gain, drift, wire, ions, inverse, w_out, smooth_out, last_out, edge_out, val, acc):
    pass_edges(wire, edge_out)
    from_wire(pos, wire, val, gain)
    scatter_add(bnd, cell, val, acc)
    w = []
    for k in range(2):
        for j in range(4):
            w_out[k, :, j*128:(j+1)*128] = acc[k, (j%2)*128:(j%2+1)*128, (j//2)*128:(j//2+1)*128]
    coupling = coupling()
    for k in range(2):
        n = ions[k]
        growth = coupling[k, 0] * w_out[0] + coupling[k, 1] * w_out[1]
        rhs = n + ion_factor * n * growth
        mix = lax.dot_general(rhs.astype(bf16), inverse[0, k], (((1,), (0,)), ((), ())), preferred_element_type=f32)
        sm = rhs + mix
        smooth_out[k] = sm
        last_out[k] = drift[127:128, :1] * sm[127:128, :]


def drag_kernel(last, ctl, drag, slot, order, first_at, place, gain, drift, w, smooth, up, ions, edge, n_out, wire, t, s, keys):
    for r in range(2):
        wire[row_of(4+r), :] = edge[r]
    first = lax.broadcasted_iota(i32, (128, 128), 0) == 0
    d = drift[...]
    n = [[], []]
    for k in range(2):
        for j in range(4):
            sl = slice(j*128, (j+1)*128)
            sm = smooth[k, :, sl]
            out = d * sm
            inflow = jnp.where(first, jnp.broadcast_to(up[k, :, sl], (128, 128)), pltpu.roll(out, 1, 0))
            x = sm - out + inflow
            n[k].append(x)
            n_out[k, :, sl] = 0.5 * (ions[k, :, sl] + x) if last else x
    drag = drag()
    for j in range(4):
        f = -(drag[0] * n[0][j] + drag[1] * n[1][j])
        for k in range(2):
            t[k, j*128:(j+1)*128, :] = f * w[k, :, j*128:(j+1)*128]
    lookup(ctl, slot, order, first_at, place, t, wire, s, keys, gain)


def tend_all(wind, forcing, visc, wire, acc, emit):
    CX, CY = wind.shape[1], wind.shape[2]
    xlo, xhi, ylo, yhi = beside_tile(wire)
    sub = lax.broadcasted_iota(i32, (CY, 128), 0)
    lane = lax.broadcasted_iota(i32, (CY, 128), 1)
    v = jnp.broadcast_to(visc()[...], (CY, 128))
    for k in range(2):
        for i in range(CX):
            u = wind[k, i]
            b = (wind[k, i+1] if i < CX-1 else xhi[k*CY:(k+1)*CY]) + (wind[k, i-1] if i > 0 else xlo[k*CY:(k+1)*CY])
            nxt = jnp.where(sub == CY-1, jnp.broadcast_to(yhi[k*CX+i:k*CX+i+1], (CY, 128)), pltpu.roll(u, CY-1, 0))
            prv = jnp.where(sub == 0, jnp.broadcast_to(ylo[k*CX+i:k*CX+i+1], (CY, 128)), pltpu.roll(u, 1, 0))
            b = b + nxt + prv
            b = b + jnp.where(lane == 127, 0.0, pltpu.roll(u, 127, 1)) + jnp.where(lane == 0, 0.0, pltpu.roll(u, 1, 1))
            emit(k, i, u, v * (b - 6.0 * u) + acc[k, (i*CY) % 256:(i*CY) % 256 + CY, (i*CY)//256*128:(i*CY)//256*128 + 128] + forcing[k, i])


def mid_kernel(bnd, ctl, cell, pos, slot, order, first, place, wire, wind, forcing, visc, mid, wire_out, val, acc, s, keys):
    from_wire(pos, wire, val)
    scatter_add(bnd, cell, val, acc)
    CY = wind.shape[2]

    def emit(k, i, u, f):
        mid[k, i*CY:(i+1)*CY, :] = u + neutral_step * f

    tend_all(wind, forcing, visc, wire, acc, emit)
    put_edges(mid, wire_out)
    lookup(ctl, slot, order, first, place, mid, wire_out, s, keys)


def end_kernel(bnd, cell, pos, wire, start, wind, forcing, visc, out, val, acc):
    from_wire(pos, wire, val)
    scatter_add(bnd, cell, val, acc)

    def emit(k, i, u, f):
        out[k, i] = 0.5 * (start[k, i] + u) + (0.5 * neutral_step) * f

    tend_all(wind, forcing, visc, wire, acc, emit)


class Incoming:
    def __init__(self, src, dst, sem):
        self.ref, self.copy, self.due = dst, pltpu.make_async_copy(src, dst, sem), True
        self.copy.start()

    def __call__(self):
        if self.due:
            self.due = False
            self.copy.wait()
        return self.ref


def call(kernel, outs, scratch, *args, smem=(), vmem=(), limit=None, name=None):
    small = list(smem) + list(vmem)
    boxes = [pltpu.SMEM(args[i].shape, args[i].dtype) for i in smem]
    boxes += [pltpu.VMEM(args[i].shape, args[i].dtype) for i in vmem]
    boxes += [pltpu.SemaphoreType.DMA((len(small),))] if small else []

    def body(*refs):
        refs = list(refs)
        own = refs[len(refs) - len(boxes):]
        refs = refs[:len(refs) - len(boxes)]
        for n, i in enumerate(small):
            refs[i] = Incoming(refs[i], own[n], own[-1].at[n])
        kernel(*refs)
        for i in small:
            refs[i]()

    return pl.pallas_call(
        body,
        out_shape=outs,
        in_specs=[pl.BlockSpec(memory_space=pltpu.HBM) if i in small else VM for i in range(len(args))],
        out_specs=jax.tree.map(lambda _: VM, outs),
        scratch_shapes=list(scratch) + boxes,
        compiler_params=pltpu.CompilerParams(vmem_limit_bytes=limit and limit << 20),
        name=name,
    )(*args)


def tied(*arrays):
    return lax.optimization_barrier(arrays)


def exchange(x):
    x = x.reshape(128, 3, 2, 128)
    return lax.all_to_all(x, ("gx", "gy"), split_axis=0, concat_axis=0, tiled=True).reshape(768, 128)


def per_device(
    neutral_wind,
    forcing,
    ion_density,
    inverse,
    drift_fraction,
    viscosity,
    coupling,
    drag_rate,
    outgoing_column,
    send_level,
    recv_tube,
    recv_point,
    recv_weight,
    pair_count,
):
    visc = viscosity[None, :]
    sd = jax.ShapeDtypeStruct
    wire_t = sd((768, 128), f32)
    tube_t = sd(ion_density.shape, f32)
    vals = pltpu.VMEM((2, 256, 128), f32)
    accs = pltpu.VMEM((2, 256 + W, 256), f32)
    tabs = pltpu.VMEM((2, 512, 128), f32)
    flat = (2, 512, 128)
    up_route = [(i, i + 1) for i in range(lax.axis_size("gy") - 1)]
    side_t = (sd((256, 128), i32), sd((128, 256), i32), sd((32, 128), i32), sd((1024, 128), i32))
    side_t += (sd((128, 256), i32), sd((128, 128), i32), sd((128, 256), i32), sd((8, 128), i32))
    seek = [pltpu.VMEM((2, 1024, 128), f32), pltpu.VMEM((1024, 128), i32)]

    cA, pA, bA, *gA, ctA, wire = call(
        first_kernel, side_t + (wire_t,), seek + [pltpu.SMEM((8, 128), i32), pltpu.SemaphoreType.DMA],
        outgoing_column, send_level, neutral_wind.reshape(flat), limit=LIMITS["first"], name="first")
    came = exchange(wire)
    wire, tub = tied(wire, recv_tube)
    cB, pB, bB, *gB, ctB, gain, drift = call(
        tube_sort_kernel, side_t + (sd((128, 256), f32), sd((128, 128), f32)), [],
        tub, recv_point, recv_weight, pair_count, drift_fraction[None, :], limit=LIMITS["tubesort"], name="tubesort")

    def tubes(came, ions, last):
        w, smooth, out_last, edge = call(
            tube_kernel, (tube_t, tube_t, sd((2, 1, 512), f32), sd((2, 128, 128), f32)), [vals, accs],
            bB, coupling, cB, pB, gain, drift, came, ions, inverse, smem=(0, 1), limit=LIMITS["tube1" if last else "tube0"], name="tube")
        up = lax.ppermute(out_last, "gy", up_route)
        return call(
            lambda *a: drag_kernel(last, *a), (tube_t, wire_t), [tabs] + seek,
            ctB, drag_rate, *gB, gain, drift, w, smooth, up, ion_density if last else up, edge, smem=(0, 1), limit=LIMITS["drag1" if last else "drag0"], name="drag")

    n1, wire = tubes(came, ion_density, False)
    mid, wire = call(
        mid_kernel, (sd(flat, f32), wire_t), [vals, accs] + seek,
        bA, ctA, cA, pA, *gA, exchange(wire), neutral_wind, forcing, visc, smem=(0, 1), vmem=(11,), limit=LIMITS["mid"], name="mid")
    ion_out, wire = tubes(exchange(wire), n1, True)
    wind_out = call(
        end_kernel, sd(neutral_wind.shape, f32), [vals, accs],
        bA, cA, pA, exchange(wire), neutral_wind, mid.reshape(neutral_wind.shape), forcing, visc, smem=(0,), vmem=(7,), limit=LIMITS["end"], name="end")
    return (wind_out, ion_out)


def solution(mesh):
    placed = (
        P(None, "gx", "gy", None),
        P(None, "gx", "gy", None),
        P(None, ("gx", "gy"), None),
        P("gx", None, None, None),
        P(("gx", "gy")),
        P(),
        P(),
        P(),
        P(("gx", "gy"), None, None),
        P(("gx", "gy"), None, None),
        P(("gx", "gy"), None, None),
        P(("gx", "gy"), None, None),
        P(("gx", "gy"), None, None),
        P(),
    )
    return jax.shard_map(
        per_device,
        mesh=mesh,
        in_specs=placed,
        out_specs=(P(None, "gx", "gy", None), P(None, ("gx", "gy"), None)),
        check_vma=False,
    )
```

```python
import jax
import jax.numpy as jnp
from jax import lax
from jax.experimental import pallas as pl
from jax.experimental.pallas import tpu as pltpu
from jax.sharding import PartitionSpec as P

i32, f32, bf16 = jnp.int32, jnp.float32, jnp.bfloat16
VM = pl.BlockSpec(memory_space=pltpu.VMEM)
SM = pl.BlockSpec(memory_space=pltpu.SMEM)
W, NB, UN, GB = 72, 16, 8, 16
LIMITS = {"first": None, "tubesort": 24, "tube0": 24, "drag0": 24, "mid": 24, "tube1": 24, "drag1": 24, "end": 24}
neutral_step = 0.4
ion_factor = 0.5


def bitonic(x):
    n, L = x.shape
    x = x.reshape(n//8, 8, L)
    sub = lax.broadcasted_iota(i32, (1, 8, L), 1)
    k = 2
    while k <= n:
        d = k//2
        while d >= 1:
            if d >= 8:
                dv = d//8
                y = x.reshape(n//(16*dv), 2, dv, 8, L)
                a, b = y[:, 0], y[:, 1]
                lo, hi = jnp.minimum(a, b), jnp.maximum(a, b)
                parts = []
                for g in range(n//(16*dv)):
                    up = ((g*2*d) & k) == 0
                    parts += [lo[g], hi[g]] if up else [hi[g], lo[g]]
                x = jnp.concatenate(parts, axis=0)
            else:
                up_r = pltpu.roll(x, 8-d, 1)
                dn_r = pltpu.roll(x, d, 1)
                first = (sub & d) == 0
                p = jnp.where(first, up_r, dn_r)
                mn, mx = jnp.minimum(x, p), jnp.maximum(x, p)
                if k >= 8:
                    if k == 8:
                        vi = lax.broadcasted_iota(i32, (n//8, 1, 1), 0)
                    parts = []
                    xs = []
                    take_min_up = first
                    kv = k//8
                    for g in range(0, n//8, kv):
                        up = (g*8 & k) == 0
                        sel = first if up else jnp.logical_not(first)
                        xs.append(jnp.where(sel, mn[g:g+kv], mx[g:g+kv]))
                    x = jnp.concatenate(xs, axis=0) if len(xs) > 1 else xs[0]
                else:
                    up = (sub & k) == 0
                    sel = first == up
                    x = jnp.where(sel, mn, mx)
            d //= 2
        k *= 2
    return x.reshape(n, L)

def row_of(r, start=0, count=128):
    return pl.ds(6*start + r, count, stride=6)


def take(x, idx):
    return jnp.take_along_axis(x, idx, axis=1, mode="promise_in_bounds")


def take2(x, idx):
    low = idx & 127
    return jnp.where(idx < 128, take(x[:, :128], low), take(x[:, 128:], low))


def slot_tile(order, first, turn, j, slots):
    lane = lax.broadcasted_iota(i32, (128, 128), 1)
    idx = take(first[...], 8*j + (lane >> 4)) + 16*turn + (lane & 15)
    slots[pl.ds(pl.multiple_of(j*128, 128), 128), :] = (take2(order, jnp.minimum(idx, 255)) & 1023).T


def sort_side(key16, cell_ref, pos_ref, bnd_ref, slot_ref, order_ref, first_ref, place_ref, ctl_ref):
    P, C = key16.shape
    c = lax.broadcasted_iota(i32, (P, C), 1)
    s = bitonic((key16 * 256 + c).astype(f32).T).astype(i32)
    cell = s >> 8
    cell_ref[...] = cell
    pos = (s & 255).T
    pos_ref[...] = pos
    row = (cell >> 7).reshape(C//8, 8, P)
    lo = jnp.min(jnp.min(row, axis=1), axis=1, keepdims=True)
    hi = jnp.max(jnp.max(row, axis=1), axis=1, keepdims=True)
    lane = lax.broadcasted_iota(i32, (C//8, 128), 1)
    bnd_ref[...] = jnp.where(lane == 0, lo, hi)
    order = cell.T
    order_ref[...] = order
    lane = lax.broadcasted_iota(i32, (P, 128), 1)
    first = jnp.zeros((P, 128), i32)
    for step in (128, 64, 32, 16, 8, 4, 2, 1, 1):
        probe = first + step
        first = jnp.where(take2(order, probe - 1) < lane*1024, probe, first)
    first_ref[...] = first
    most = jnp.max((pltpu.roll(first, 127, 1) - first).astype(f32), axis=0, keepdims=True)
    most = jnp.where(lane[:1] < 64, most, 0.0)
    top = jnp.broadcast_to(jnp.max(most, axis=1, keepdims=True), (1, 128))
    ctl_ref[...] = jnp.broadcast_to(jnp.where(lane[:1] < 64, most, top), (8, 128)).astype(i32)
    for j in range(8):
        slot_tile(order, first_ref, 0, j, slot_ref)
    b = order >> 10
    w = c - jnp.concatenate([take(first, b[:, :128]), take(first, b[:, 128:])], axis=1)
    place = (pos << 14) + ((w >> 4) << 10) + (b << 4) + (w & 15)
    place_ref[...] = (bitonic(place.astype(f32).T).astype(i32) & 16383).T


def cell_key(row, lane):
    return ((row & 255) << 8) + ((row >> 8) << 7) + lane


def put_edges(t, wire):
    CX, CY = 16, t.shape[1] // 16
    for k in range(2):
        wire[row_of(4, k*CY, CY), :] = t[k, (CX-1)*CY:CX*CY, :]
        wire[row_of(4, (2+k)*CY, CY), :] = t[k, :CY, :]
        for i in range(CX):
            for q, at in ((k*CX+i, (i+1)*CY-1), ((2+k)*CX+i, i*CY)):
                wire[6*q+5:6*q+6, :] = t[k, at:at+1, :]
    wire[row_of(5, 4*CX, 128 - 4*CX), :] = jnp.zeros((128 - 4*CX, 128), f32)


def place_of():
    x, y = lax.axis_index("gx"), lax.axis_index("gy")
    return x, y, x * lax.axis_size("gy") + y


def pass_edges(wire, out):
    q = place_of()[2]
    step = lax.axis_size("gy")
    for r, (cut, d) in enumerate(((64, step), (32, 1))):
        x = wire[row_of(4+r), :]
        out[r] = jnp.where(q < cut, pltpu.roll(x, d, 0), pltpu.roll(x, 128-d, 0))


def beside_tile(wire):
    x, y = place_of()[:2]
    a, b = wire[row_of(4), :], wire[row_of(5, 0, 64), :]
    return (
        jnp.where(x > 0, a[:64], 0.0),
        jnp.where(x < lax.axis_size("gx") - 1, a[64:], 0.0),
        jnp.where(y > 0, b[:32], 0.0),
        jnp.where(y < lax.axis_size("gy") - 1, b[32:], 0.0),
    )


def tube_sort_kernel(tub, pnt, weight, count, drift, *outs):
    side, gain, drift_out = outs[:8], outs[8], outs[9]
    p = pnt[0]
    sort_side(cell_key((p >> 7)*128 + tub[0], p & 127), *side)
    own = place_of()[2]
    lane = lax.broadcasted_iota(i32, (128, 128), 1)
    live = jnp.sum(jnp.where(lane == own, count[...], 0).astype(f32), axis=1, keepdims=True)
    c = lax.broadcasted_iota(i32, (128, 256), 1).astype(f32)
    gain[...] = jnp.where(c < live, weight[0], 0.0)
    drift_out[...] = jnp.broadcast_to(drift[...], (128, 128)).T


def permute_lanes(x, idx):
    return [take2(x, idx[:, :128]), take2(x, idx[:, 128:])]


def lookup(ctl, slot, order, first, place, t_ref, wire, s_ref, key_ref, gain=None, limit_copy=None):
    half = t_ref.shape[1] // 2

    def group(at_bucket, count, keys):
        for b in range(count):
            rows = []
            for j in range(8):
                at = at_bucket*4 + 4*b + j//2 + (j % 2)*half
                rows.append([jnp.broadcast_to(t_ref[k, pl.ds(at, 1), :], (8, 128)) for k in range(2)])
            for i in range(2):
                sl = pl.ds(pl.multiple_of(at_bucket*16 + b*16 + i*8, 8), 8)
                key = keys[sl, :]
                sub, lev = key >> 7, key & 127
                acc = [take(rows[0][k], lev) for k in range(2)]
                for j in range(1, 8):
                    m = sub == j
                    for k in range(2):
                        acc[k] = jnp.where(m, take(rows[j][k], lev), acc[k])
                for k in range(2):
                    s_ref[k, sl, :] = acc[k]

    def each(g, _):
        group(g*GB, GB, slot)
        return 0

    def scaled(x, h):
        return x if gain is None else x * gain[:, h*128:(h+1)*128]

    lax.fori_loop(0, 64//GB, each, 0)
    if limit_copy is not None:
        limit_copy.start()
    parts = [[s_ref[k, j*128:(j+1)*128, :].T for j in range(8)] for k in range(2)]
    for h in range(2):
        at = place[:, h*128:(h+1)*128]
        low, tile = at & 127, (at >> 7) & 7
        for k in range(2):
            x = take(parts[k][0], low)
            for j in range(1, 8):
                x = jnp.where(tile == j, take(parts[k][j], low), x)
            wire[row_of(2*k+h), :] = scaled(x, h)

    def turn(t, _):
        def late(g, _):
            most = ctl[0, 8*g]
            for b in range(1, 8):
                most = jnp.maximum(most, ctl[0, 8*g + b])

            @pl.when(most > 16*t)
            def _():
                slot_tile(order[...], first, t, g, key_ref)
                group(g*8, 8, key_ref)
                tile = pl.ds(pl.multiple_of(g*128, 128), 128)
                for h in range(2):
                    at = place[:, h*128:(h+1)*128]
                    mine = (at >> 7) == 8*t + g
                    for k in range(2):
                        x = take(s_ref[k, tile, :].T, at & 127)
                        wire[row_of(2*k+h), :] = jnp.where(mine, scaled(x, h), wire[row_of(2*k+h), :])
            return 0

        lax.fori_loop(0, 8, late, 0)
        return 0

    if limit_copy is not None:
        limit_copy.wait()
    else:
        ctl = ctl()
    lax.fori_loop(1, (ctl[0, 64] + 15) // 16, turn, 0)


def scatter_add(bnd, cell_ref, val_ref, acc_ref):
    bnd = bnd()
    acc_ref[...] = jnp.zeros_like(acc_ref)
    iota = lax.broadcasted_iota(i32, (256, 128), 0).astype(f32).astype(bf16)
    one, zero = jnp.ones((256, 128), bf16), jnp.zeros((256, 128), bf16)

    def spread(x, n):
        return jnp.broadcast_to(x, (n, 128)).astype(bf16)

    def begin(v):
        return ((bnd[v*(NB//8), 0] >> 1) // 8) * 8

    def window(v, rb):
        rb = pl.multiple_of(rb, 8)
        sl = pl.ds(pl.multiple_of(v*NB, 8), NB)
        key = cell_ref[sl, :]
        rel, lane = ((key >> 8) - rb).astype(f32), (key & 255).astype(f32)
        vals = []
        for k in range(2):
            x = val_ref[k, sl, :]
            h = x.astype(bf16).astype(f32)
            vals += [h, x - h]
        rows, lanes = [], []
        for r in range(NB):
            lanes.append(jnp.where(iota == spread(lane[r:r+1], 256), one, zero))
            m = iota[:W] == spread(rel[r:r+1], W)
            rows.append(jnp.concatenate([jnp.where(m, spread(x[r:r+1], W), zero[:W]) for x in vals], axis=0))
        z = lax.dot_general(
            jnp.concatenate(rows, axis=1), jnp.concatenate(lanes, axis=1),
            (((1,), (1,)), ((), ())), preferred_element_type=f32)
        for k in range(2):
            acc_ref[k, pl.ds(rb, W), :] += z[2*k*W:(2*k+1)*W] + z[(2*k+1)*W:(2*k+2)*W]

    def block(v, _):
        window(v, begin(v))
        return 0

    def rest(v, _):
        base = begin(v)

        def more(it, _):
            window(v, base + it*W)
            return 0

        return lax.fori_loop(1, ((bnd[(v+1)*(NB//8) - 1, 1] >> 1) - base)//W + 1, more, 0)

    lax.fori_loop(0, 256//NB, block, 0, unroll=UN)
    lax.fori_loop(0, 256//NB, rest, 0)


def from_wire(pos, wire, val, gain=None):
    for k in range(2):
        x = [wire[row_of(2*k+h), :] for h in range(2)]
        if gain is not None:
            x = [x[h] * gain[:, h*128:(h+1)*128] for h in range(2)]
        o = permute_lanes(jnp.concatenate(x, axis=1), pos[...])
        val[k, :128, :] = o[0].T
        val[k, 128:, :] = o[1].T


def first_kernel(col, lev, t, *refs):
    side, wire, s, keys, limits, sem = refs[:8], refs[8], *refs[9:]
    sort_side(cell_key(col[0], lev[0]), *side)
    copy = pltpu.make_async_copy(side[7], limits, sem)
    put_edges(t, wire)
    lookup(limits, *side[3:7], t, wire, s, keys, limit_copy=copy)


def tube_kernel(bnd, coupling, cell, pos, gain, drift, wire, ions, inverse, w_out, smooth_out, last_out, edge_out, val, acc):
    pass_edges(wire, edge_out)
    from_wire(pos, wire, val, gain)
    scatter_add(bnd, cell, val, acc)
    w = []
    for k in range(2):
        for j in range(4):
            w_out[k, :, j*128:(j+1)*128] = acc[k, (j%2)*128:(j%2+1)*128, (j//2)*128:(j//2+1)*128]
    coupling = coupling()
    for k in range(2):
        n = ions[k]
        growth = coupling[k, 0] * w_out[0] + coupling[k, 1] * w_out[1]
        rhs = n + ion_factor * n * growth
        mix = lax.dot_general(rhs.astype(bf16), inverse[0, k], (((1,), (0,)), ((), ())), preferred_element_type=f32)
        sm = rhs + mix
        smooth_out[k] = sm
        last_out[k] = drift[127:128, :1] * sm[127:128, :]


def drag_kernel(last, ctl, drag, slot, order, first_at, place, gain, drift, w, smooth, up, ions, edge, n_out, wire, t, s, keys):
    for r in range(2):
        wire[row_of(4+r), :] = edge[r]
    first = lax.broadcasted_iota(i32, (128, 128), 0) == 0
    d = drift[...]
    n = [[], []]
    for k in range(2):
        for j in range(4):
            sl = slice(j*128, (j+1)*128)
            sm = smooth[k, :, sl]
            out = d * sm
            inflow = jnp.where(first, jnp.broadcast_to(up[k, :, sl], (128, 128)), pltpu.roll(out, 1, 0))
            x = sm - out + inflow
            n[k].append(x)
            n_out[k, :, sl] = 0.5 * (ions[k, :, sl] + x) if last else x
    drag = drag()
    for j in range(4):
        f = -(drag[0] * n[0][j] + drag[1] * n[1][j])
        for k in range(2):
            t[k, j*128:(j+1)*128, :] = f * w[k, :, j*128:(j+1)*128]
    lookup(ctl, slot, order, first_at, place, t, wire, s, keys, gain)


def tend_all(wind, forcing, visc, wire, acc, emit):
    CX, CY = wind.shape[1], wind.shape[2]
    xlo, xhi, ylo, yhi = beside_tile(wire)
    sub = lax.broadcasted_iota(i32, (CY, 128), 0)
    lane = lax.broadcasted_iota(i32, (CY, 128), 1)
    v = jnp.broadcast_to(visc()[...], (CY, 128))
    for k in range(2):
        for i in range(CX):
            u = wind[k, i]
            b = (wind[k, i+1] if i < CX-1 else xhi[k*CY:(k+1)*CY]) + (wind[k, i-1] if i > 0 else xlo[k*CY:(k+1)*CY])
            nxt = jnp.where(sub == CY-1, jnp.broadcast_to(yhi[k*CX+i:k*CX+i+1], (CY, 128)), pltpu.roll(u, CY-1, 0))
            prv = jnp.where(sub == 0, jnp.broadcast_to(ylo[k*CX+i:k*CX+i+1], (CY, 128)), pltpu.roll(u, 1, 0))
            b = b + nxt + prv
            b = b + jnp.where(lane == 127, 0.0, pltpu.roll(u, 127, 1)) + jnp.where(lane == 0, 0.0, pltpu.roll(u, 1, 1))
            emit(k, i, u, v * (b - 6.0 * u) + acc[k, (i*CY) % 256:(i*CY) % 256 + CY, (i*CY)//256*128:(i*CY)//256*128 + 128] + forcing[k, i])


def mid_kernel(bnd, ctl, cell, pos, slot, order, first, place, wire, wind, forcing, visc, mid, wire_out, val, acc, s, keys):
    from_wire(pos, wire, val)
    scatter_add(bnd, cell, val, acc)
    CY = wind.shape[2]

    def emit(k, i, u, f):
        mid[k, i*CY:(i+1)*CY, :] = u + neutral_step * f

    tend_all(wind, forcing, visc, wire, acc, emit)
    put_edges(mid, wire_out)
    lookup(ctl, slot, order, first, place, mid, wire_out, s, keys)


def end_kernel(bnd, cell, pos, wire, start, wind, forcing, visc, out, val, acc):
    from_wire(pos, wire, val)
    scatter_add(bnd, cell, val, acc)

    def emit(k, i, u, f):
        out[k, i] = 0.5 * (start[k, i] + u) + (0.5 * neutral_step) * f

    tend_all(wind, forcing, visc, wire, acc, emit)


class Incoming:
    def __init__(self, src, dst, sem):
        self.ref, self.copy, self.due = dst, pltpu.make_async_copy(src, dst, sem), True
        self.copy.start()

    def __call__(self):
        if self.due:
            self.due = False
            self.copy.wait()
        return self.ref


def call(kernel, outs, scratch, *args, smem=(), vmem=(), limit=None, name=None):
    small = list(smem) + list(vmem)
    boxes = [pltpu.SMEM(args[i].shape, args[i].dtype) for i in smem]
    boxes += [pltpu.VMEM(args[i].shape, args[i].dtype) for i in vmem]
    boxes += [pltpu.SemaphoreType.DMA((len(small),))] if small else []

    def body(*refs):
        refs = list(refs)
        own = refs[len(refs) - len(boxes):]
        refs = refs[:len(refs) - len(boxes)]
        for n, i in enumerate(small):
            refs[i] = Incoming(refs[i], own[n], own[-1].at[n])
        kernel(*refs)
        for i in small:
            refs[i]()

    return pl.pallas_call(
        body,
        out_shape=outs,
        in_specs=[pl.BlockSpec(memory_space=pltpu.HBM) if i in small else VM for i in range(len(args))],
        out_specs=jax.tree.map(lambda _: VM, outs),
        scratch_shapes=list(scratch) + boxes,
        compiler_params=pltpu.CompilerParams(vmem_limit_bytes=limit and limit << 20),
        name=name,
    )(*args)


def tied(*arrays):
    return lax.optimization_barrier(arrays)


def exchange(x):
    x = x.reshape(128, 3, 2, 128)
    return lax.all_to_all(x, ("gx", "gy"), split_axis=0, concat_axis=0, tiled=True).reshape(768, 128)


def per_device(
    neutral_wind,
    forcing,
    ion_density,
    inverse,
    drift_fraction,
    viscosity,
    coupling,
    drag_rate,
    outgoing_column,
    send_level,
    recv_tube,
    recv_point,
    recv_weight,
    pair_count,
):
    visc = viscosity[None, :]
    sd = jax.ShapeDtypeStruct
    wire_t = sd((768, 128), f32)
    tube_t = sd(ion_density.shape, f32)
    vals = pltpu.VMEM((2, 256, 128), f32)
    accs = pltpu.VMEM((2, 256 + W, 256), f32)
    tabs = pltpu.VMEM((2, 512, 128), f32)
    flat = (2, 512, 128)
    up_route = [(i, i + 1) for i in range(lax.axis_size("gy") - 1)]
    side_t = (sd((256, 128), i32), sd((128, 256), i32), sd((32, 128), i32), sd((1024, 128), i32))
    side_t += (sd((128, 256), i32), sd((128, 128), i32), sd((128, 256), i32), sd((8, 128), i32))
    seek = [pltpu.VMEM((2, 1024, 128), f32), pltpu.VMEM((1024, 128), i32)]

    cA, pA, bA, *gA, ctA, wire = call(
        first_kernel, side_t + (wire_t,), seek + [pltpu.SMEM((8, 128), i32), pltpu.SemaphoreType.DMA],
        outgoing_column, send_level, neutral_wind.reshape(flat), limit=LIMITS["first"], name="first")
    came = exchange(wire)
    wire, tub = tied(wire, recv_tube)
    cB, pB, bB, *gB, ctB, gain, drift = call(
        tube_sort_kernel, side_t + (sd((128, 256), f32), sd((128, 128), f32)), [],
        tub, recv_point, recv_weight, pair_count, drift_fraction[None, :], limit=LIMITS["tubesort"], name="tubesort")

    def tubes(came, ions, last):
        w, smooth, out_last, edge = call(
            tube_kernel, (tube_t, tube_t, sd((2, 1, 512), f32), sd((2, 128, 128), f32)), [vals, accs],
            bB, coupling, cB, pB, gain, drift, came, ions, inverse, smem=(0, 1), limit=LIMITS["tube1" if last else "tube0"], name="tube")
        up = lax.ppermute(out_last, "gy", up_route)
        return call(
            lambda *a: drag_kernel(last, *a), (tube_t, wire_t), [tabs] + seek,
            ctB, drag_rate, *gB, gain, drift, w, smooth, up, ion_density if last else up, edge, smem=(0, 1), limit=LIMITS["drag1" if last else "drag0"], name="drag")

    n1, wire = tubes(came, ion_density, False)
    mid, wire = call(
        mid_kernel, (sd(flat, f32), wire_t), [vals, accs] + seek,
        bA, ctA, cA, pA, *gA, exchange(wire), neutral_wind, forcing, visc, smem=(0, 1), vmem=(11,), limit=LIMITS["mid"], name="mid")
    ion_out, wire = tubes(exchange(wire), n1, True)
    wind_out = call(
        end_kernel, sd(neutral_wind.shape, f32), [vals, accs],
        bA, cA, pA, exchange(wire), neutral_wind, mid.reshape(neutral_wind.shape), forcing, visc, smem=(0,), vmem=(7,), limit=LIMITS["end"], name="end")
    return (wind_out, ion_out)


def solution(mesh):
    placed = (
        P(None, "gx", "gy", None),
        P(None, "gx", "gy", None),
        P(None, ("gx", "gy"), None),
        P("gx", None, None, None),
        P(("gx", "gy")),
        P(),
        P(),
        P(),
        P(("gx", "gy"), None, None),
        P(("gx", "gy"), None, None),
        P(("gx", "gy"), None, None),
        P(("gx", "gy"), None, None),
        P(("gx", "gy"), None, None),
        P(),
    )
    return jax.shard_map(
        per_device,
        mesh=mesh,
        in_specs=placed,
        out_specs=(P(None, "gx", "gy", None), P(None, ("gx", "gy"), None)),
        check_vma=False,
    )
```
